128 devices in a mesh: row: 8 (over z, core), col: 16 (over x, y).
Axes of the slice: x: 4, y: 4, z: 4, core: 2. Of those that a mesh axis runs over, the one named last changes fastest.
Arguments:
- offsets: float32 [8, 16, 2, 256], P('row', 'col'), may hold values from 0 to 1
- point_order: int32 [8, 16, 256], P('row', 'col'), may hold values from 0 to 255, each once within a row
- nugget: float32 [8, 16, 256], P('row', 'col'), may hold values from 1 to 4
- interp: float32 [8, 16, 128, 128], P('row', 'col'), may hold values from -0.5 to 0.5
Outputs:
- root_work: float32 [16384, 16384], P('row', 'col')
The draws below stay inside these ranges and needn't reach their ends.
Inputs may be any that keep to these rules, and one draw needn't show every extreme that they name: `point_order`: each row lists every point of its box once; its first 128 entries name the box's skeleton points.
All inputs are finite; a program needn't handle non-finite values.
Results may differ from the reference program's by a relative error of at most 0.0001.
Values sent between devices are 32-bit elements; how exact they have to be, the bound alone decides.
A program may use at most 128 MiB of HBM per device.

```python
import math
import jax
import jax.numpy as jnp
from jax import lax

PTS = 256
SK = 128
PW = 512
RD = 128
BOX_ROWS = 8
BOX_COLS = 16
BOXES = 128
NR = 16384
N_ROW = 8
N_COL = 16


def level_of(rng, dims, split, smallest, largest):
    loudness = 1.0
    for position, shards_of in split:
        steps = jax.random.uniform(jax.random.fold_in(jax.random.fold_in(rng, 6), position), (shards_of,), jnp.float32, smallest / len(split), largest / len(split))
        loudness = loudness * jnp.repeat(jnp.exp(steps), dims[position] // shards_of).reshape((-1,) + (1,) * (len(dims) - 1 - position))
    return loudness


def bell_draw(rng, dims, scale, bound, cuts=(), held_as=jnp.bfloat16):
    entries = scale * jax.random.normal(rng, dims, jnp.float32)
    if cuts:
        entries = entries * level_of(rng, dims, cuts, -0.22, 0.18)
    return jnp.clip(entries, -bound, bound).astype(held_as)


def setup_inputs(seed: int = 0) -> dict:
    arg_keys = jax.random.split(jax.random.key(seed), 5)
    return {
        "offsets": jnp.clip(1.0 * jax.random.uniform(arg_keys[0], (BOX_ROWS, BOX_COLS, 2, PTS), jnp.float32) ** level_of(arg_keys[0], (BOX_ROWS, BOX_COLS, 2, PTS), ((0, 8), (1, 16)), -0.2, 0.2), 0.0, 1.0),
        "point_order": jax.vmap(lambda own: jax.random.permutation(own, PTS))(jax.random.split(arg_keys[1], BOX_ROWS * BOX_COLS)).reshape((BOX_ROWS, BOX_COLS, PTS)).astype(jnp.int32),
        "nugget": jnp.clip(jnp.exp(math.log(4.0) - 1.3862944 * jax.random.uniform(arg_keys[2], (BOX_ROWS, BOX_COLS, PTS), jnp.float32) ** level_of(arg_keys[2], (BOX_ROWS, BOX_COLS, PTS), ((0, 8), (1, 16)), -0.2, 0.2)), 1.0, 4.0),
        "interp": bell_draw(arg_keys[3], (BOX_ROWS, BOX_COLS, SK, RD), SK ** -0.5, 0.5, ((0, 8), (1, 16)), jnp.float32),
    }


kernel_amp = 0.015625
kernel_len = 0.5
highest = lax.Precision.HIGHEST

def offsets_all():
    return [(a, b) for a in (-1, 0, 1) for b in (-1, 0, 1)]

def block_of(a, b):
    return (a + 1) * 3 + (b + 1)

def kernel(left, right):
    gap_row = left[..., 0, :, None] - right[..., 0, None, :]
    gap_col = left[..., 1, :, None] - right[..., 1, None, :]
    return kernel_amp * jnp.exp(-jnp.sqrt(gap_row * gap_row + gap_col * gap_col) / kernel_len)

def shifted(padded, start_row, start_col, step):
    count_rows = N_ROW // step
    count_cols = N_COL // step
    return padded[start_row:start_row + step * (count_rows - 1) + 1:step, start_col:start_col + step * (count_cols - 1) + 1:step]

def cross_sum(neighbours, target, columns):
    left_rows = []
    right_rows = []
    for e in offsets_all():
        if abs(target[0] - e[0]) <= 1 and abs(target[1] - e[1]) <= 1:
            source = neighbours[block_of(e[0], e[1])]
            home_slot = block_of(-e[0], -e[1])
            other_slot = block_of(target[0] - e[0], target[1] - e[1])
            left_rows.append(source[..., home_slot * PTS:home_slot * PTS + columns])
            right_rows.append(source[..., other_slot * PTS:other_slot * PTS + columns])
    return jnp.einsum('uvrk,uvrl->uvkl', jnp.concatenate(left_rows, axis=-2), jnp.concatenate(right_rows, axis=-2), precision=highest)

def reference(offsets, point_order, nugget, interp):
    row_pos = jnp.broadcast_to(jnp.arange(N_ROW, dtype=jnp.float32)[:, None], (N_ROW, N_COL))
    col_pos = jnp.broadcast_to(jnp.arange(N_COL, dtype=jnp.float32)[None, :], (N_ROW, N_COL))
    corner = jnp.stack([row_pos, col_pos], axis=2)[..., None]
    points = jnp.take_along_axis(offsets + corner, jnp.broadcast_to(point_order[:, :, None, :], offsets.shape), axis=3)
    weights = jnp.take_along_axis(nugget, point_order, axis=2)
    padded_points = jnp.pad(points, ((1, 1), (1, 1), (0, 0), (0, 0)))
    present = jnp.pad(jnp.ones((N_ROW, N_COL), jnp.float32), 1)
    factors = jnp.zeros((N_ROW, N_COL, RD, 9 * PTS), jnp.float32)
    for a in (0, 1):
        for b in (0, 1):
            own_points = shifted(points, a, b, 2)
            weights_sub = shifted(weights, a, b, 2)
            interp_sub = shifted(interp, a, b, 2)
            padded_factors = jnp.pad(factors, ((1, 1), (1, 1), (0, 0), (0, 0)))
            neighbours = [shifted(padded_factors, 1 + a + c, 1 + b + d, 2) for c, d in offsets_all()]
            kernel_blocks = []
            for c, d in offsets_all():
                present_box = shifted(present, 1 + a + c, 1 + b + d, 2)[..., None, None]
                kernel_block = kernel(own_points, shifted(padded_points, 1 + a + c, 1 + b + d, 2)) * present_box
                if (c, d) == (0, 0):
                    kernel_block = kernel_block + weights_sub[..., :, None] * jnp.eye(PTS, dtype=jnp.float32)
                kernel_blocks.append(kernel_block)
            near_matrix = jnp.concatenate(kernel_blocks, axis=-1)
            fill_blocks = [cross_sum(neighbours, m, PTS) for m in offsets_all()]
            matrix = near_matrix - jnp.concatenate(fill_blocks, axis=-1)
            reduced_rows = matrix[..., SK:, :] - jnp.einsum('uvsr,uvsk->uvrk', interp_sub, matrix[..., :SK, :], precision=highest)
            centre = reduced_rows[..., 4 * PTS:5 * PTS]
            reduced = centre[..., SK:] - jnp.einsum('uvrs,uvst->uvrt', centre[..., :SK], interp_sub, precision=highest)
            diag_factor = jnp.linalg.cholesky(reduced)
            solved = jax.scipy.linalg.solve_triangular(diag_factor, reduced_rows, lower=True)
            factors = factors.at[a::2, b::2].set(solved)
    padded_factors = jnp.pad(factors, ((1, 1), (1, 1), (0, 0), (0, 0)))
    neighbours = [shifted(padded_factors, 1 + c, 1 + d, 1) for c, d in offsets_all()]
    deltas = []
    for c, d in offsets_all():
        fill_part = cross_sum(neighbours, (c, d), SK)
        present_box = shifted(present, 1 + c, 1 + d, 1)[..., None, None]
        if (c, d) == (0, 0):
            delta_block = weights[..., :SK, None] * jnp.eye(SK, dtype=jnp.float32) - fill_part
        else:
            delta_block = -fill_part
        deltas.append(delta_block * present_box)
    deltas = jnp.stack(deltas, axis=2)
    skeleton = points[..., :SK].reshape(BOXES, 2, SK)
    all_skeleton = jnp.transpose(skeleton, (1, 2, 0)).reshape(2, NR)
    row_blocks = jnp.transpose(skeleton, (2, 1, 0))
    root_matrix = lax.map(lambda row_block: kernel(row_block, all_skeleton), row_blocks).reshape(NR, NR)
    box_row = jnp.arange(N_ROW, dtype=jnp.int32)[:, None]
    box_col = jnp.arange(N_COL, dtype=jnp.int32)[None, :]
    sources = []
    targets = []
    for c, d in offsets_all():
        inside = (box_row + c >= 0) & (box_row + c < N_ROW) & (box_col + d >= 0) & (box_col + d < N_COL)
        home_box = box_row * N_COL + box_col
        sources.append(home_box)
        targets.append(jnp.where(inside, (box_row + c) * N_COL + box_col + d, home_box).astype(jnp.int32))
    sources = jnp.stack(sources, axis=2).astype(jnp.int32)
    targets = jnp.stack(targets, axis=2).astype(jnp.int32)
    blocks = root_matrix.reshape(SK, BOXES, SK, BOXES).at[:, sources, :, targets].add(deltas)
    root_matrix = blocks.reshape(NR, NR)
    rows_all = jnp.arange(NR, dtype=jnp.int32)[:, None]
    panels = []
    for p in range(2):
        first_col = p * PW
        diag_factor = jnp.linalg.cholesky(root_matrix[first_col:first_col + PW, first_col:first_col + PW])
        solved = jax.scipy.linalg.solve_triangular(diag_factor, root_matrix[:, first_col:first_col + PW].T, lower=True).T
        column = jnp.where(rows_all < first_col, 0.0, solved.at[first_col:first_col + PW].set(diag_factor))
        root_matrix = root_matrix - jnp.dot(column, column.T, precision=highest)
        panels.append(column)
    root_matrix = root_matrix.at[:, :PW].set(panels[0]).at[:, PW:2 * PW].set(panels[1]).at[:2 * PW, 2 * PW:].set(0.0)
    return root_matrix
```

```python
import jax
import jax.numpy as jnp
from jax import lax
from jax.experimental import pallas as pl
from jax.experimental.pallas import tpu as pltpu
from jax.sharding import PartitionSpec as P

PW = 512
SB = 1024


kernel_amp = 0.015625
kernel_len = 0.5
highest = lax.Precision.HIGHEST


def extended(block, sides, width):
    for axis, dim in sides:
        count = lax.axis_size(axis)
        forward = [(i, i + 1) for i in range(count - 1)]
        backward = [(target, source) for source, target in forward]
        low = lax.ppermute(
            lax.slice_in_dim(block, block.shape[dim] - width, None, axis=dim), axis, forward
        )
        high = lax.ppermute(lax.slice_in_dim(block, 0, width, axis=dim), axis, backward)
        block = jnp.concatenate([low, block, high], axis=dim)
    return block


def shifted(block, axis, distance):
    devices = range(lax.axis_size(axis))
    route = [(i - distance, i) for i in devices if i - distance in devices]
    return lax.ppermute(block, axis, route)


def offsets_all():
    return [(a, b) for a in (-1, 0, 1) for b in (-1, 0, 1)]


def pairs_all():
    return [
        (e, m)
        for e in offsets_all()
        for m in offsets_all()
        if abs(m[0] - e[0]) <= 1 and abs(m[1] - e[1]) <= 1
    ]


def block_of(a, b):
    return (a + 1) * 3 + (b + 1)


def vector(along, across):
    return (along, across)


def kernel(left, right):
    gap_row = left[0][:, None] - right[0][None, :]
    gap_col = left[1][:, None] - right[1][None, :]
    return kernel_amp * jnp.exp(-jnp.sqrt(gap_row * gap_row + gap_col * gap_col) / kernel_len)


def cross_pair(stored, target, columns):
    pair_index = {pair: n for n, pair in enumerate(pairs_all())}
    left_rows = []
    right_rows = []
    for e in offsets_all():
        if abs(target[0] - e[0]) <= 1 and abs(target[1] - e[1]) <= 1:
            left_rows.append(stored[pair_index[e, (0, 0)]][:, :columns])
            right_rows.append(stored[pair_index[e, target]][:, :columns])
    return (jnp.concatenate(left_rows, axis=0), jnp.concatenate(right_rows, axis=0))


def cross_sum(stored, target, columns):
    left_rows, right_rows = cross_pair(stored, target, columns)
    return jnp.einsum("rk,rl->kl", left_rows, right_rows, precision=highest)


def eliminate(stored, near_matrix, interp_box):
    box_points = near_matrix.shape[0]
    skel_count = interp_box.shape[0]
    fill_blocks = [cross_sum(stored, m, box_points) for m in offsets_all()]
    matrix = near_matrix - jnp.concatenate(fill_blocks, axis=1)
    reduced_rows = matrix[skel_count:] - jnp.einsum(
        "sr,sk->rk", interp_box, matrix[:skel_count], precision=highest
    )
    centre = reduced_rows[:, 4 * box_points : 5 * box_points]
    reduced = centre[:, skel_count:] - jnp.einsum(
        "rs,st->rt", centre[:, :skel_count], interp_box, precision=highest
    )
    diag_factor = jnp.linalg.cholesky(reduced)
    return jax.scipy.linalg.solve_triangular(diag_factor, reduced_rows, lower=True)


def spread(factor_new, move_first, move_second, p):
    box_points = factor_new.shape[1] // 9

    def take_block(m):
        k = block_of(m[0], m[1])
        return factor_new[:, k * box_points : (k + 1) * box_points]

    placed = {}
    section_one = {}
    for s in (1, -1):
        listing = [vector(u, v) for u in (0, s) for v in (-1, 0, 1)]
        arrived = move_first(jnp.stack([take_block(m) for m in listing]), s)
        source = vector(-s, 0)
        section_one[s] = (source, listing, arrived)
        for n, m in enumerate(listing):
            placed[source, (m[0] + source[0], m[1] + source[1])] = arrived[n]
    for t in (1, -1):
        payload = []
        labels = []
        for m in [vector(u, v) for u in (-1, 0, 1) for v in (0, t)]:
            payload.append(take_block(m))
            labels.append(((0, 0), m))
        for s in (1, -1):
            source, listing, arrived = section_one[s]
            for n, m in enumerate(listing):
                if m[1 - p] in (0, t):
                    payload.append(arrived[n])
                    labels.append((source, m))
        arrived = move_second(jnp.stack(payload), t)
        sender_at = vector(0, -t)
        for n, (anchor, m) in enumerate(labels):
            source = (anchor[0] + sender_at[0], anchor[1] + sender_at[1])
            placed[source, (m[0] + source[0], m[1] + source[1])] = arrived[n]
    for m in offsets_all():
        placed[(0, 0), m] = take_block(m)
    return jnp.stack([placed[pair] for pair in pairs_all()])


def factor128(a):
    n = a.shape[0]
    G = n // 8
    rows = [a[8*g:8*g+8] for g in range(G)]
    lane = lax.broadcasted_iota(jnp.int32, (8, n), 1)
    sub = lax.broadcasted_iota(jnp.int32, (8, n), 0)
    w = [(lane == sub + 8*g).astype(jnp.float32) for g in range(G)]
    def srow(v, t):
        return jnp.broadcast_to(v[t:t+1], (8, n))
    def lcol(v, t):
        return jnp.broadcast_to(v[:, t:t+1], (8, n))
    us, ws = [], []
    for p in range(G):
        q, qw = rows[p], w[p]
        cols = [lcol(q, 8*p+t) for t in range(8)]
        u, uw, dv = q, qw, None
        for t in range(8):
            pr, pw = srow(q, t), srow(qw, t)
            d = srow(cols[t], t)
            here = sub == t
            u = pr if t == 0 else jnp.where(here, pr, u)
            uw = pw if t == 0 else jnp.where(here, pw, uw)
            dv = d if t == 0 else jnp.where(here, d, dv)
            m = jnp.where(here, 0.0, cols[t]) * (1.0 / d)
            q = q - m * pr
            qw = qw - m * pw
            for v in range(t + 1, 8):
                cols[v] = cols[v] - m * srow(cols[v], t)
        r = lax.rsqrt(dv)
        us.append(jnp.where(lane >= sub + 8*p, u * r, 0.0))
        ws.append(uw * r)
        inv = 1.0 / dv
        z, zw = q * inv, qw * inv
        zs = [srow(z, t) for t in range(8)]
        zws = [srow(zw, t) for t in range(8)]
        for g in range(p + 1, G):
            cg = [lcol(rows[g], 8*p+t) for t in range(8)]
            x = [cg[t] * zs[t] for t in range(8)]
            y = [cg[t] * zws[t] for t in range(8)]
            rows[g] = rows[g] - (((x[0]+x[1])+(x[2]+x[3]))+((x[4]+x[5])+(x[6]+x[7])))
            w[g] = w[g] - (((y[0]+y[1])+(y[2]+y[3]))+((y[4]+y[5])+(y[6]+y[7])))
    return jnp.concatenate(us, 0), jnp.concatenate(ws, 0)


def split(x):
    hi = x.astype(jnp.bfloat16)
    return hi, (x - hi.astype(jnp.float32)).astype(jnp.bfloat16)


def dot3(a, b, dims):
    def one(x, y):
        return lax.dot_general(x, y, (dims, ((), ())), preferred_element_type=jnp.float32)

    return one(a[0], b[1]) + one(a[1], b[0]) + one(a[0], b[0])


NN = ((1,), (0,))
TN = ((0,), (0,))


def root_kernel(flag_ref, a_ref, b_ref, z_ref, work, inv_ref, hi_ref, lo_ref):
    count = SB // 128
    chunk = 512
    work[:, :SB] = a_ref[...]
    work[:, SB:] = b_ref[...]

    def rows_of(i):
        return pl.ds(pl.multiple_of(i * 128, 128), 128)

    def cols_of(c):
        return pl.ds(pl.multiple_of(c * chunk, chunk), chunk)

    def step(i, _):
        here = rows_of(i)
        u, w = factor128(work[here, here])
        inv_ref[i] = w
        w2 = split(w)

        def scale(c, _):
            new = dot3(w2, split(work[here, cols_of(c)]), NN)
            hi, lo = split(new)
            work[here, cols_of(c)] = new
            hi_ref[:, cols_of(c)] = hi
            lo_ref[:, cols_of(c)] = lo
            return 0

        lax.fori_loop(i * 128 // chunk, 2 * SB // chunk, scale, 0)

        def trail(j, _):
            there = rows_of(j)
            left = (hi_ref[:, there], lo_ref[:, there])

            def cols(c, _):
                right = (hi_ref[:, cols_of(c)], lo_ref[:, cols_of(c)])
                work[there, cols_of(c)] -= dot3(left, right, TN)
                return 0

            lax.fori_loop(j * 128 // chunk, 2 * SB // chunk, cols, 0)
            return 0

        lax.fori_loop(i + 1, count, trail, 0)
        return 0

    lax.fori_loop(0, count, step, 0)

    @pl.when(flag_ref[0] == 1)
    def _():
        row = lax.broadcasted_iota(jnp.int32, (SB, SB), 0)
        col = lax.broadcasted_iota(jnp.int32, (SB, SB), 1)
        work[:, SB:] = jnp.where(row == col, -1.0, 0.0)

    def back(n, _):
        i = count - 1 - n
        here = rows_of(i)
        w2 = split(inv_ref[i])

        def cols(c, _):
            right = split(work[here, cols_of(c)])
            new = dot3(w2, right, TN)
            z_ref[here, pl.ds(pl.multiple_of(c * chunk - SB, chunk), chunk)] = new
            hi, lo = split(new)

            def above(j, _):
                there = rows_of(j)
                work[there, cols_of(c)] -= dot3(split(work[there, here]), (hi, lo), NN)
                return 0

            lax.fori_loop(0, i, above, 0)
            return 0

        lax.fori_loop(SB // chunk, 2 * SB // chunk, cols, 0)
        return 0

    lax.fori_loop(0, count, back, 0)


def root_solve(flag, a, b):
    return pl.pallas_call(
        root_kernel,
        out_shape=jax.ShapeDtypeStruct((SB, SB), jnp.float32),
        in_specs=[
            pl.BlockSpec(memory_space=pltpu.SMEM),
            pl.BlockSpec(memory_space=pltpu.VMEM),
            pl.BlockSpec(memory_space=pltpu.VMEM),
        ],
        out_specs=pl.BlockSpec(memory_space=pltpu.VMEM),
        scratch_shapes=[
            pltpu.VMEM((SB, 2 * SB), jnp.float32),
            pltpu.VMEM((SB // 128, 128, 128), jnp.float32),
            pltpu.VMEM((128, 2 * SB), jnp.bfloat16),
            pltpu.VMEM((128, 2 * SB), jnp.bfloat16),
        ],
        compiler_params=pltpu.CompilerParams(vmem_limit_bytes=40 * 2**20),
    )(flag, a, b)


def root_phase(deltas, points, row_at, col_at, row_count, col_count):
    skel_count = deltas.shape[1]
    row_width = skel_count // row_count
    col_width = skel_count // col_count
    box_total = row_count * col_count
    lead = SB // box_total
    shape = (row_count, col_count, 9)
    tile = jnp.transpose(
        deltas.reshape(9, col_count, col_width, row_count, row_width), (3, 1, 0, 2, 4)
    ).reshape(shape + (col_width * row_width,))
    rows_piece = jnp.transpose(
        deltas[:, :lead].reshape(9, lead, row_count, row_width), (2, 0, 1, 3)
    ).reshape(row_count, 1, 9, lead * row_width)
    cols_piece = jnp.transpose(
        deltas[:, :, :lead].reshape(9, col_count, col_width, lead), (1, 0, 2, 3)
    ).reshape(1, col_count, 9, col_width * lead)
    corner_piece = deltas[:, :lead, :lead].reshape(1, 1, 9, lead * lead)
    pieces = [tile, rows_piece, cols_piece, corner_piece]
    sizes = [x.shape[3] for x in pieces]
    outgoing = jnp.concatenate(
        [jnp.broadcast_to(x, shape + x.shape[3:]) for x in pieces], axis=3
    ).reshape(box_total, 9, sum(sizes))
    arrived = lax.all_to_all(outgoing, ("row", "col"), split_axis=0, concat_axis=0, tiled=True)
    received = jnp.transpose(arrived, (1, 2, 0))
    all_skeleton = lax.all_gather(points[:, :skel_count][None], ("row", "col"), axis=0, tiled=True)
    ordered = jnp.transpose(all_skeleton, (1, 2, 0))

    box_ids = jnp.arange(box_total, dtype=jnp.int32)
    src_rows = (box_ids // col_count)[None, :]
    src_cols = (box_ids % col_count)[None, :]
    hits = []
    for a, b in offsets_all():
        living = (
            (src_rows + a >= 0)
            & (src_rows + a < row_count)
            & (src_cols + b >= 0)
            & (src_cols + b < col_count)
        )
        hits.append((box_ids[:, None] == (src_rows + a) * col_count + src_cols + b) & living)

    def coords(start, width):
        part = lax.dynamic_slice_in_dim(ordered, start, width, 1)
        return part.reshape(2, width * box_total)

    starts = [0]
    for size in sizes:
        starts.append(starts[-1] + size)

    def block(which, row_coords, col_coords):
        rows_n = row_coords.shape[1] // box_total
        cols_n = col_coords.shape[1] // box_total
        part = received[:, starts[which] : starts[which + 1]]
        part = jnp.transpose(part.reshape(9, cols_n, rows_n, box_total), (0, 2, 1, 3))
        placed = jnp.zeros((rows_n, box_total, cols_n, box_total), jnp.float32)
        for n in range(9):
            placed = jnp.where(hits[n][None, :, None, :], part[n][:, None, :, :], placed)
        return kernel(row_coords, col_coords) + placed.reshape(
            rows_n * box_total, cols_n * box_total
        )

    row_coords = coords(row_at * row_width, row_width)
    col_coords = coords(col_at * col_width, col_width)
    lead_coords = coords(0, lead)
    flag = (col_at == 0).astype(jnp.int32)
    inner = block(3, lead_coords, lead_coords)
    across = block(2, lead_coords, col_coords)
    factor = root_solve(flag[None], inner, across)
    down = block(1, row_coords, lead_coords)
    own = block(0, row_coords, col_coords)
    update = jnp.dot(down, factor, precision=lax.Precision.HIGH)
    result = jnp.where(col_at == 0, 0.0, own) - update
    rows_here, cols_here = result.shape
    global_rows = row_at * rows_here + jnp.arange(rows_here, dtype=jnp.int32)[:, None]
    global_cols = col_at * cols_here + jnp.arange(cols_here, dtype=jnp.int32)[None, :]
    return jnp.where((global_rows < SB) & (global_cols > global_rows), 0.0, result)


def on_device(offsets, point_order, nugget, interp):
    row_at = lax.axis_index("row")
    col_at = lax.axis_index("col")
    row_count = lax.axis_size("row")
    col_count = lax.axis_size("col")
    box_points = offsets.shape[3]
    skel_count = interp.shape[2]
    red_count = interp.shape[3]
    corner = jnp.stack([row_at, col_at]).astype(jnp.float32)[:, None]
    points = jnp.take(offsets[0, 0] + corner, point_order[0, 0], axis=1)
    weights = jnp.take(nugget[0, 0], point_order[0, 0])
    interp_box = interp[0, 0]
    neighbour_points = extended(points[None, None], (("row", 0), ("col", 1)), 1)
    present = []
    kernel_blocks = []
    for a, b in offsets_all():
        inside = (
            (row_at + a >= 0)
            & (row_at + a < row_count)
            & (col_at + b >= 0)
            & (col_at + b < col_count)
        )
        present.append(inside.astype(jnp.float32))
        kernel_block = kernel(points, neighbour_points[a + 1, b + 1]) * present[-1]
        if (a, b) == (0, 0):
            kernel_block = kernel_block + jnp.diag(weights)
        kernel_blocks.append(kernel_block)
    near_matrix = jnp.concatenate(kernel_blocks, axis=1)

    def move_first(x, amount):
        return shifted(x, "row", amount)

    def move_second(x, amount):
        return shifted(x, "col", amount)

    leading = 0
    colour = 2 * (row_at % 2) + col_at % 2
    stored = jnp.zeros((len(pairs_all()), red_count, box_points), jnp.float32)
    for k in range(4):
        factor_new = lax.cond(
            colour == k,
            lambda s: eliminate(s, near_matrix, interp_box),
            lambda s: jnp.zeros((red_count, 9 * box_points), jnp.float32),
            stored,
        )
        stored = stored + spread(factor_new, move_first, move_second, leading)
    weights_skel = weights[:skel_count]
    pieces = []
    for k, m in enumerate(offsets_all()):
        left_rows, right_rows = cross_pair(stored, m, skel_count)
        fill_part = jnp.einsum("rk,rl->kl", left_rows, right_rows, precision=highest)
        if m == (0, 0):
            delta_block = jnp.diag(weights_skel) - fill_part
        else:
            delta_block = -fill_part
        pieces.append(delta_block * present[k])
    return root_phase(jnp.stack(pieces), points, row_at, col_at, row_count, col_count)


def solution(mesh):
    in_specs = (
        P("row", "col", None, None),
        P("row", "col", None),
        P("row", "col", None),
        P("row", "col", None, None),
    )
    out_specs = P("row", "col")
    return jax.shard_map(
        on_device, mesh=mesh, in_specs=in_specs, out_specs=out_specs, check_vma=False
    )
```

```python
import jax
import jax.numpy as jnp
from jax import lax
from jax.experimental import pallas as pl
from jax.experimental.pallas import tpu as pltpu
from jax.sharding import PartitionSpec as P

PW = 512
SB = 1024


kernel_amp = 0.015625
kernel_len = 0.5


def offsets_all():
    return [(a, b) for a in (-1, 0, 1) for b in (-1, 0, 1)]


def kernel(left, right):
    gap_row = left[0][:, None] - right[0][None, :]
    gap_col = left[1][:, None] - right[1][None, :]
    return kernel_amp * jnp.exp(-jnp.sqrt(gap_row * gap_row + gap_col * gap_col) / kernel_len)


def factor128(a):
    n = a.shape[0]
    G = n // 8
    rows = [a[8*g:8*g+8] for g in range(G)]
    lane = lax.broadcasted_iota(jnp.int32, (8, n), 1)
    sub = lax.broadcasted_iota(jnp.int32, (8, n), 0)
    w = [(lane == sub + 8*g).astype(jnp.float32) for g in range(G)]
    def srow(v, t):
        return jnp.broadcast_to(v[t:t+1], (8, n))
    def lcol(v, t):
        return jnp.broadcast_to(v[:, t:t+1], (8, n))
    us, ws = [], []
    for p in range(G):
        q, qw = rows[p], w[p]
        cols = [lcol(q, 8*p+t) for t in range(8)]
        u, uw, dv = q, qw, None
        for t in range(8):
            pr, pw = srow(q, t), srow(qw, t)
            d = srow(cols[t], t)
            here = sub == t
            u = pr if t == 0 else jnp.where(here, pr, u)
            uw = pw if t == 0 else jnp.where(here, pw, uw)
            dv = d if t == 0 else jnp.where(here, d, dv)
            m = jnp.where(here, 0.0, cols[t]) * (1.0 / d)
            q = q - m * pr
            qw = qw - m * pw
            for v in range(t + 1, 8):
                cols[v] = cols[v] - m * srow(cols[v], t)
        r = lax.rsqrt(dv)
        us.append(jnp.where(lane >= sub + 8*p, u * r, 0.0))
        ws.append(uw * r)
        inv = 1.0 / dv
        z, zw = q * inv, qw * inv
        zs = [srow(z, t) for t in range(8)]
        zws = [srow(zw, t) for t in range(8)]
        for g in range(p + 1, G):
            cg = [lcol(rows[g], 8*p+t) for t in range(8)]
            x = [cg[t] * zs[t] for t in range(8)]
            y = [cg[t] * zws[t] for t in range(8)]
            rows[g] = rows[g] - (((x[0]+x[1])+(x[2]+x[3]))+((x[4]+x[5])+(x[6]+x[7])))
            w[g] = w[g] - (((y[0]+y[1])+(y[2]+y[3]))+((y[4]+y[5])+(y[6]+y[7])))
    return jnp.concatenate(us, 0), jnp.concatenate(ws, 0)


def split(x):
    hi = x.astype(jnp.bfloat16)
    return hi, (x - hi.astype(jnp.float32)).astype(jnp.bfloat16)


def dot3(a, b, dims):
    def one(x, y):
        return lax.dot_general(x, y, (dims, ((), ())), preferred_element_type=jnp.float32)

    return one(a[0], b[1]) + one(a[1], b[0]) + one(a[0], b[0])


NN = ((1,), (0,))
TN = ((0,), (0,))
NT = ((1,), (1,))


def box_kernel(pack_ref, d_ref, near, ea, f, fs, g, mat, acc, tx, rx, fx, ps, pr, ks, kr, xs, xr):
    row_at = lax.axis_index("row")
    col_at = lax.axis_index("col")
    row_count = lax.axis_size("row")
    col_count = lax.axis_size("col")

    def inside(a, b):
        r, c = row_at + a, col_at + b
        return (r >= 0) & (r < row_count) & (c >= 0) & (c < col_count)

    def colour(a, b):
        return 2 * ((row_at + a + 2) % 2) + (col_at + b + 2) % 2

    def unslot(n):
        return n // 3 - 1, n % 3 - 1

    def near_pair(a, b):
        return (a >= -1) & (a <= 1) & (b >= -1) & (b <= 1)

    def loop(body, low=0, high=9):
        def step(n, _):
            body(n)
            return 0

        lax.fori_loop(low, high, step, 0)

    def copy(src, dst, send, recv, a, b):
        return pltpu.make_async_remote_copy(
            src_ref=src,
            dst_ref=dst,
            send_sem=send,
            recv_sem=recv,
            device_id=(row_at + a, col_at + b),
            device_id_type=pl.DeviceIdType.MESH,
        )

    def neighbours(body):
        def each(n):
            a, b = unslot(n)

            @pl.when((n != 4) & inside(a, b))
            def _():
                body(n, a, b)

        loop(each)

    def pack_copy(n, a, b):
        return copy(pack_ref, near.at[8 - n], ps.at[n], pr.at[8 - n], a, b)

    def k_copy(n, e, a, b):
        return copy(tx.at[e], rx.at[8 - n, e], ks.at[n, e], kr.at[8 - n, e], a, b)

    def x_copy(h, o):
        a, b = unslot(h)
        return copy(fs.at[o], fx.at[h - 5, o], xs.at[h - 5, o], xr.at[h - 5, o], -a, -b)

    barrier = pltpu.get_barrier_semaphore()

    def greet(n, a, b):
        pl.semaphore_signal(
            barrier,
            inc=1,
            device_id=(row_at + a, col_at + b),
            device_id_type=pl.DeviceIdType.MESH,
        )

    neighbours(greet)
    tall = 1 + lax.min(row_at, 1) + lax.min(row_count - 1 - row_at, 1)
    wide = 1 + lax.min(col_at, 1) + lax.min(col_count - 1 - col_at, 1)
    pl.semaphore_wait(barrier, tall * wide - 1)
    neighbours(lambda n, a, b: pack_copy(n, a, b).start())

    own = pack_ref[128:136]
    own_interp = split(pack_ref[0:128])
    my_colour = colour(0, 0)
    eye = lax.broadcasted_iota(jnp.int32, (128, 128), 0) == lax.broadcasted_iota(
        jnp.int32, (128, 128), 1
    )

    def start_block(source, here, slot):
        where = source[128:136].T
        parts = []
        for s in range(2):
            line = []
            for t in range(2):
                gap_row = where[:, s : s + 1] - own[t : t + 1]
                gap_col = where[:, 2 + s : 3 + s] - own[2 + t : 3 + t]
                square = gap_row * gap_row + gap_col * gap_col
                block = kernel_amp * jnp.exp(-jnp.sqrt(square) / kernel_len)
                if here and s == t:
                    block = block + jnp.where(eye, own[4 + s : 5 + s], 0.0)
                line.append(block)
            parts.append(jnp.concatenate(line, axis=1))
        ea[slot] = parts[1] - dot3(split(source[0:128]), split(parts[0]), TN)

    start_block(pack_ref, True, 4)
    mat[...] = ea[4, :, 128:] - dot3(split(ea[4, :, :128]), own_interp, NN)

    def start(n, a, b):
        pack_copy(8 - n, -a, -b).wait_recv()
        start_block(near.at[n], False, n)

    neighbours(start)

    def stage(k):
        @pl.when(my_colour == k)
        def _():
            tx[4] = factor128(mat[...])[1]

            def outgoing(e):
                ea_, eb_ = unslot(e)

                def dispatch(n, a, b):
                    @pl.when(near_pair(ea_ - a, eb_ - b))
                    def _():
                        k_copy(n, e, a, b).start()

                @pl.when(e == 4)
                def _():
                    neighbours(dispatch)

                @pl.when((e != 4) & inside(ea_, eb_) & (colour(ea_, eb_) < k))
                def _():
                    tx[e] = dot3(split(tx[4]), split(g[e]), NT)
                    neighbours(dispatch)

            outgoing(4)
            loop(lambda e: pl.when(e != 4)(lambda: outgoing(e)))

        def arrive(o):
            oa, ob = unslot(o)

            @pl.when(inside(oa, ob) & (colour(oa, ob) == k))
            def _():
                @pl.when(o == 4)
                def _():
                    acc[...] = dot3(split(tx[4]), split(ea[4]), NN)

                @pl.when(o != 4)
                def _():
                    k_copy(8 - o, 4, -oa, -ob).wait_recv()
                    acc[...] = dot3(split(rx[o, 4]), split(ea[o]), NN)

                def term(e):
                    ea_, eb_ = unslot(e)
                    va, vb = oa + ea_, ob + eb_

                    @pl.when((e != 4) & near_pair(va, vb) & inside(va, vb) & (colour(va, vb) < k))
                    def _():
                        right = split(f[(va + 1) * 3 + vb + 1])

                        @pl.when(o == 4)
                        def _():
                            acc[...] -= dot3(split(tx[e]), right, NN)

                        @pl.when(o != 4)
                        def _():
                            k_copy(8 - o, e, -oa, -ob).wait_recv()
                            acc[...] -= dot3(split(rx[o, e]), right, NN)

                loop(term)
                f[o] = acc[...]
                fs[o] = acc[:, :128]

                @pl.when(my_colour > k)
                def _():
                    new = acc[:, 128:] - dot3(split(acc[:, :128]), own_interp, NN)
                    g[o] = new
                    new2 = split(new)
                    mat[...] -= dot3(new2, new2, TN)

                def forward(h):
                    ha, hb = unslot(h)

                    @pl.when(inside(-ha, -hb) & near_pair(oa + ha, ob + hb))
                    def _():
                        x_copy(h, o).start()

                loop(forward, 5, 9)

        loop(arrive)

    loop(stage, 0, 4)

    def centre(o):
        oa, ob = unslot(o)

        @pl.when(inside(oa, ob))
        def _():
            part = split(fs[o])
            acc[:, :128] -= dot3(part, part, TN)

    acc[:, :128] = jnp.where(eye, own[4:5], 0.0)
    loop(centre)
    d_ref[0] = acc[:, :128]

    def pair(h):
        ha, hb = unslot(h)
        acc[:, :128] = jnp.zeros((128, 128), jnp.float32)

        @pl.when(inside(ha, hb))
        def _():
            def term(o):
                oa, ob = unslot(o)
                va, vb = oa - ha, ob - hb

                @pl.when(inside(oa, ob) & near_pair(va, vb))
                def _():
                    e = (va + 1) * 3 + vb + 1
                    x_copy(h, e).wait_recv()
                    acc[:, :128] -= dot3(split(fs[o]), split(fx[h - 5, e]), TN)

            loop(term)

        d_ref[h - 4] = acc[:, :128]

    loop(pair, 5, 9)

    def finish(n, a, b):
        pack_copy(n, a, b).wait_send()

        def each(e):
            ea_, eb_ = unslot(e)
            is_sent = (e == 4) | (inside(ea_, eb_) & (colour(ea_, eb_) < my_colour))

            @pl.when(is_sent & near_pair(ea_ - a, eb_ - b))
            def _():
                k_copy(n, e, a, b).wait_send()

        loop(each)

    neighbours(finish)

    def finish_x(h):
        ha, hb = unslot(h)

        def each(o):
            oa, ob = unslot(o)

            @pl.when(inside(-ha, -hb) & inside(oa, ob) & near_pair(oa + ha, ob + hb))
            def _():
                x_copy(h, o).wait_send()

        loop(each)

    loop(finish_x, 5, 9)


def box_phase(pack):
    block = (128, 128)
    return pl.pallas_call(
        box_kernel,
        out_shape=jax.ShapeDtypeStruct((5,) + block, jnp.float32),
        in_specs=[pl.BlockSpec(memory_space=pltpu.VMEM)],
        out_specs=pl.BlockSpec(memory_space=pltpu.VMEM),
        scratch_shapes=[
            pltpu.VMEM((9, 136, 128), jnp.float32),
            pltpu.VMEM((9, 128, 256), jnp.float32),
            pltpu.VMEM((9, 128, 256), jnp.float32),
            pltpu.VMEM((9,) + block, jnp.float32),
            pltpu.VMEM((9,) + block, jnp.float32),
            pltpu.VMEM(block, jnp.float32),
            pltpu.VMEM((128, 256), jnp.float32),
            pltpu.VMEM((9,) + block, jnp.float32),
            pltpu.VMEM((9, 9) + block, jnp.float32),
            pltpu.VMEM((4, 9) + block, jnp.float32),
            pltpu.SemaphoreType.DMA((9,)),
            pltpu.SemaphoreType.DMA((9,)),
            pltpu.SemaphoreType.DMA((9, 9)),
            pltpu.SemaphoreType.DMA((9, 9)),
            pltpu.SemaphoreType.DMA((4, 9)),
            pltpu.SemaphoreType.DMA((4, 9)),
        ],
        compiler_params=pltpu.CompilerParams(
            collective_id=0, has_side_effects=True, vmem_limit_bytes=40 * 2**20
        ),
    )(pack)


def root_kernel(flag_ref, a_ref, b_ref, z_ref, work, inv_ref, hi_ref, lo_ref):
    count = SB // 128
    chunk = 512
    work[:, :SB] = a_ref[...]
    work[:, SB:] = b_ref[...]

    def rows_of(i):
        return pl.ds(pl.multiple_of(i * 128, 128), 128)

    def cols_of(c):
        return pl.ds(pl.multiple_of(c * chunk, chunk), chunk)

    def step(i, _):
        here = rows_of(i)
        u, w = factor128(work[here, here])
        inv_ref[i] = w
        w2 = split(w)

        def scale(c, _):
            new = dot3(w2, split(work[here, cols_of(c)]), NN)
            hi, lo = split(new)
            work[here, cols_of(c)] = new
            hi_ref[:, cols_of(c)] = hi
            lo_ref[:, cols_of(c)] = lo
            return 0

        lax.fori_loop(i * 128 // chunk, 2 * SB // chunk, scale, 0)

        def trail(j, _):
            there = rows_of(j)
            left = (hi_ref[:, there], lo_ref[:, there])

            def cols(c, _):
                right = (hi_ref[:, cols_of(c)], lo_ref[:, cols_of(c)])
                work[there, cols_of(c)] -= dot3(left, right, TN)
                return 0

            lax.fori_loop(j * 128 // chunk, 2 * SB // chunk, cols, 0)
            return 0

        lax.fori_loop(i + 1, count, trail, 0)
        return 0

    lax.fori_loop(0, count, step, 0)

    @pl.when(flag_ref[0] == 1)
    def _():
        row = lax.broadcasted_iota(jnp.int32, (SB, SB), 0)
        col = lax.broadcasted_iota(jnp.int32, (SB, SB), 1)
        work[:, SB:] = jnp.where(row == col, -1.0, 0.0)

    def back(n, _):
        i = count - 1 - n
        here = rows_of(i)
        w2 = split(inv_ref[i])

        def cols(c, _):
            right = split(work[here, cols_of(c)])
            new = dot3(w2, right, TN)
            z_ref[here, pl.ds(pl.multiple_of(c * chunk - SB, chunk), chunk)] = new
            hi, lo = split(new)

            def above(j, _):
                there = rows_of(j)
                work[there, cols_of(c)] -= dot3(split(work[there, here]), (hi, lo), NN)
                return 0

            lax.fori_loop(0, i, above, 0)
            return 0

        lax.fori_loop(SB // chunk, 2 * SB // chunk, cols, 0)
        return 0

    lax.fori_loop(0, count, back, 0)


def root_solve(flag, a, b):
    return pl.pallas_call(
        root_kernel,
        out_shape=jax.ShapeDtypeStruct((SB, SB), jnp.float32),
        in_specs=[
            pl.BlockSpec(memory_space=pltpu.SMEM),
            pl.BlockSpec(memory_space=pltpu.VMEM),
            pl.BlockSpec(memory_space=pltpu.VMEM),
        ],
        out_specs=pl.BlockSpec(memory_space=pltpu.VMEM),
        scratch_shapes=[
            pltpu.VMEM((SB, 2 * SB), jnp.float32),
            pltpu.VMEM((SB // 128, 128, 128), jnp.float32),
            pltpu.VMEM((128, 2 * SB), jnp.bfloat16),
            pltpu.VMEM((128, 2 * SB), jnp.bfloat16),
        ],
        compiler_params=pltpu.CompilerParams(vmem_limit_bytes=40 * 2**20),
    )(flag, a, b)


def root_phase(deltas, points, row_at, col_at, row_count, col_count):
    skel_count = deltas.shape[1]
    row_width = skel_count // row_count
    col_width = skel_count // col_count
    box_total = row_count * col_count
    lead = SB // box_total
    shape = (row_count, col_count, 9)
    tile = jnp.transpose(
        deltas.reshape(9, col_count, col_width, row_count, row_width), (3, 1, 0, 2, 4)
    ).reshape(shape + (col_width * row_width,))
    rows_piece = jnp.transpose(
        deltas[:, :lead].reshape(9, lead, row_count, row_width), (2, 0, 1, 3)
    ).reshape(row_count, 1, 9, lead * row_width)
    cols_piece = jnp.transpose(
        deltas[:, :, :lead].reshape(9, col_count, col_width, lead), (1, 0, 2, 3)
    ).reshape(1, col_count, 9, col_width * lead)
    corner_piece = deltas[:, :lead, :lead].reshape(1, 1, 9, lead * lead)
    pieces = [tile, rows_piece, cols_piece, corner_piece]
    sizes = [x.shape[3] for x in pieces]
    values = jnp.concatenate(
        [jnp.broadcast_to(x, shape + x.shape[3:]) for x in pieces], axis=3
    ).reshape(row_count, col_count, 9 * sum(sizes))
    skeleton = points[:, :skel_count]
    row_points = jnp.transpose(skeleton.reshape(2, row_count, row_width), (1, 0, 2))
    col_points = jnp.transpose(skeleton.reshape(2, col_count, col_width), (1, 0, 2))
    lead_points = skeleton[:, :lead].reshape(1, 1, 2 * lead)
    places = jnp.concatenate(
        [
            jnp.broadcast_to(
                row_points.reshape(row_count, 1, 2 * row_width), shape[:2] + (2 * row_width,)
            ),
            jnp.broadcast_to(
                col_points.reshape(1, col_count, 2 * col_width), shape[:2] + (2 * col_width,)
            ),
            jnp.broadcast_to(lead_points, shape[:2] + (2 * lead,)),
            jnp.zeros(shape[:2] + (64,), jnp.float32),
        ],
        axis=2,
    )
    outgoing = jnp.concatenate([values, places], axis=2).reshape(box_total, -1, 128)
    arrived = lax.all_to_all(outgoing, ("row", "col"), split_axis=0, concat_axis=0, tiled=True)
    turned = jnp.transpose(arrived.reshape(box_total, -1))
    received = turned[: 9 * sum(sizes)].reshape(9, sum(sizes), box_total)
    where_all = turned[9 * sum(sizes) :]

    box_ids = jnp.arange(box_total, dtype=jnp.int32)
    box_rows = (box_ids // col_count)[None, :]
    box_cols = (box_ids % col_count)[None, :]
    hits = []
    shifts = []
    half = [(0, 0), (0, 1), (1, -1), (1, 0), (1, 1)]
    for a, b in half + [(-x, -y) for x, y in half[1:]]:
        living = (
            (box_rows + a >= 0)
            & (box_rows + a < row_count)
            & (box_cols + b >= 0)
            & (box_cols + b < col_count)
        )
        hits.append((box_ids[:, None] == (box_rows + a) * col_count + box_cols + b) & living)
        shifts.append(-(a * col_count + b))

    def lanes(n, part):
        return part if n < 5 else jnp.roll(part, shifts[n], axis=-1)

    def coords(start, width):
        return where_all[start : start + 2 * width].reshape(2, width * box_total)

    starts = [0]
    for size in sizes:
        starts.append(starts[-1] + size)

    def block(which, row_coords, col_coords):
        rows_n = row_coords.shape[1] // box_total
        cols_n = col_coords.shape[1] // box_total
        part = received[:, starts[which] : starts[which + 1]]
        part = jnp.transpose(part.reshape(9, cols_n, rows_n, box_total), (0, 2, 1, 3))
        placed = jnp.zeros((rows_n, box_total, cols_n, box_total), jnp.float32)
        for n in range(9):
            placed = jnp.where(hits[n][None, :, None, :], lanes(n, part[n])[:, None, :, :], placed)
        return kernel(row_coords, col_coords) + placed.reshape(
            rows_n * box_total, cols_n * box_total
        )

    row_coords = coords(0, row_width)
    col_coords = coords(2 * row_width, col_width)
    lead_coords = coords(2 * row_width + 2 * col_width, lead)
    flag = (col_at == 0).astype(jnp.int32)
    inner = block(3, lead_coords, lead_coords)
    across = block(2, lead_coords, col_coords)
    factor = root_solve(flag[None], inner, across)
    down = block(1, row_coords, lead_coords)
    own = block(0, row_coords, col_coords)
    update = jnp.dot(down, factor, precision=lax.Precision.HIGH)
    result = jnp.where(col_at == 0, 0.0, own) - update
    rows_here, cols_here = result.shape
    global_rows = row_at * rows_here + jnp.arange(rows_here, dtype=jnp.int32)[:, None]
    global_cols = col_at * cols_here + jnp.arange(cols_here, dtype=jnp.int32)[None, :]
    return jnp.where((global_rows < SB) & (global_cols > global_rows), 0.0, result)


def on_device(offsets, point_order, nugget, interp):
    row_at = lax.axis_index("row")
    col_at = lax.axis_index("col")
    row_count = lax.axis_size("row")
    col_count = lax.axis_size("col")
    corner = jnp.stack([row_at, col_at]).astype(jnp.float32)[:, None]
    order = point_order[0, 0]
    points = jnp.take(offsets[0, 0] + corner, order, axis=1)
    weights = jnp.take(nugget[0, 0], order)
    lines = jnp.concatenate([points.reshape(4, 128), weights.reshape(2, 128)])
    pack = jnp.concatenate([interp[0, 0], lines, jnp.zeros((2, 128), jnp.float32)])
    halves = box_phase(pack)
    deltas = jnp.concatenate([halves, jnp.transpose(halves[1:], (0, 2, 1))])
    return root_phase(deltas, points, row_at, col_at, row_count, col_count)


def solution(mesh):
    in_specs = (
        P("row", "col", None, None),
        P("row", "col", None),
        P("row", "col", None),
        P("row", "col", None, None),
    )
    out_specs = P("row", "col")
    return jax.shard_map(
        on_device, mesh=mesh, in_specs=in_specs, out_specs=out_specs, check_vma=False
    )
```

```python
import jax
import jax.numpy as jnp
from jax import lax
from jax.experimental import pallas as pl
from jax.experimental.pallas import tpu as pltpu
from jax.sharding import PartitionSpec as P

SB = 1024


kernel_amp = 0.015625
kernel_len = 0.5


def factor128(a):
    n = a.shape[0]
    G = n // 8
    rows = [a[8*g:8*g+8] for g in range(G)]
    lane = lax.broadcasted_iota(jnp.int32, (8, n), 1)
    sub = lax.broadcasted_iota(jnp.int32, (8, n), 0)
    w = [(lane == sub + 8*g).astype(jnp.float32) for g in range(G)]
    def srow(v, t):
        return jnp.broadcast_to(v[t:t+1], (8, n))
    def lcol(v, t):
        return jnp.broadcast_to(v[:, t:t+1], (8, n))
    us, ws = [], []
    for p in range(G):
        q, qw = rows[p], w[p]
        cols = [lcol(q, 8*p+t) for t in range(8)]
        u, uw, dv = q, qw, None
        for t in range(8):
            pr, pw = srow(q, t), srow(qw, t)
            d = srow(cols[t], t)
            here = sub == t
            u = pr if t == 0 else jnp.where(here, pr, u)
            uw = pw if t == 0 else jnp.where(here, pw, uw)
            dv = d if t == 0 else jnp.where(here, d, dv)
            m = jnp.where(here, 0.0, cols[t]) * (1.0 / d)
            q = q - m * pr
            qw = qw - m * pw
            for v in range(t + 1, 8):
                cols[v] = cols[v] - m * srow(cols[v], t)
        r = lax.rsqrt(dv)
        us.append(jnp.where(lane >= sub + 8*p, u * r, 0.0))
        ws.append(uw * r)
        inv = 1.0 / dv
        z, zw = q * inv, qw * inv
        zs = [srow(z, t) for t in range(8)]
        zws = [srow(zw, t) for t in range(8)]
        for g in range(p + 1, G):
            cg = [lcol(rows[g], 8*p+t) for t in range(8)]
            x = [cg[t] * zs[t] for t in range(8)]
            y = [cg[t] * zws[t] for t in range(8)]
            rows[g] = rows[g] - (((x[0]+x[1])+(x[2]+x[3]))+((x[4]+x[5])+(x[6]+x[7])))
            w[g] = w[g] - (((y[0]+y[1])+(y[2]+y[3]))+((y[4]+y[5])+(y[6]+y[7])))
    return jnp.concatenate(us, 0), jnp.concatenate(ws, 0)


def split(x):
    hi = x.astype(jnp.bfloat16)
    return hi, (x - hi.astype(jnp.float32)).astype(jnp.bfloat16)


def dot3(a, b, dims):
    def one(x, y):
        return lax.dot_general(x, y, (dims, ((), ())), preferred_element_type=jnp.float32)

    return one(a[0], b[1]) + one(a[1], b[0]) + one(a[0], b[0])


NN = ((1,), (0,))
TN = ((0,), (0,))
NT = ((1,), (1,))


def box_kernel(pack_ref, out_ref, near, ea, f, fs, g, mat, acc, tx, rx, fx, dd, ps, pr, ks, kr, xs, xr):
    row_at = lax.axis_index("row")
    col_at = lax.axis_index("col")
    row_count = lax.axis_size("row")
    col_count = lax.axis_size("col")

    def inside(a, b):
        r, c = row_at + a, col_at + b
        return (r >= 0) & (r < row_count) & (c >= 0) & (c < col_count)

    def colour(a, b):
        return 2 * ((row_at + a + 2) % 2) + (col_at + b + 2) % 2

    def unslot(n):
        return n // 3 - 1, n % 3 - 1

    def near_pair(a, b):
        return (a >= -1) & (a <= 1) & (b >= -1) & (b <= 1)

    def loop(body, low=0, high=9):
        def step(n, _):
            body(n)
            return 0

        lax.fori_loop(low, high, step, 0)

    def copy(src, dst, send, recv, a, b):
        return pltpu.make_async_remote_copy(
            src_ref=src,
            dst_ref=dst,
            send_sem=send,
            recv_sem=recv,
            device_id=(row_at + a, col_at + b),
            device_id_type=pl.DeviceIdType.MESH,
        )

    def neighbours(body):
        def each(n):
            a, b = unslot(n)

            @pl.when((n != 4) & inside(a, b))
            def _():
                body(n, a, b)

        loop(each)

    def pack_copy(n, a, b):
        return copy(pack_ref, near.at[8 - n], ps.at[n], pr.at[8 - n], a, b)

    def k_copy(n, e, a, b):
        return copy(tx.at[e], rx.at[8 - n, e], ks.at[n, e], kr.at[8 - n, e], a, b)

    def x_copy(h, o):
        a, b = unslot(h)
        return copy(fs.at[o], fx.at[h - 5, o], xs.at[h - 5, o], xr.at[h - 5, o], -a, -b)

    barrier = pltpu.get_barrier_semaphore()

    def greet(n, a, b):
        pl.semaphore_signal(
            barrier,
            inc=1,
            device_id=(row_at + a, col_at + b),
            device_id_type=pl.DeviceIdType.MESH,
        )

    neighbours(greet)
    tall = 1 + lax.min(row_at, 1) + lax.min(row_count - 1 - row_at, 1)
    wide = 1 + lax.min(col_at, 1) + lax.min(col_count - 1 - col_at, 1)
    pl.semaphore_wait(barrier, tall * wide - 1)
    neighbours(lambda n, a, b: pack_copy(n, a, b).start())

    own = pack_ref[128:136]
    own_interp = split(pack_ref[0:128])
    my_colour = colour(0, 0)
    eye = lax.broadcasted_iota(jnp.int32, (128, 128), 0) == lax.broadcasted_iota(
        jnp.int32, (128, 128), 1
    )

    def start_block(source, here, slot):
        where = source[128:136].T
        parts = []
        for s in range(2):
            line = []
            for t in range(2):
                gap_row = where[:, s : s + 1] - own[t : t + 1]
                gap_col = where[:, 2 + s : 3 + s] - own[2 + t : 3 + t]
                square = gap_row * gap_row + gap_col * gap_col
                block = kernel_amp * jnp.exp(-jnp.sqrt(square) / kernel_len)
                if here and s == t:
                    block = block + jnp.where(eye, own[4 + s : 5 + s], 0.0)
                line.append(block)
            parts.append(jnp.concatenate(line, axis=1))
        ea[slot] = parts[1] - dot3(split(source[0:128]), split(parts[0]), TN)

    start_block(pack_ref, True, 4)
    mat[...] = ea[4, :, 128:] - dot3(split(ea[4, :, :128]), own_interp, NN)

    def start(n, a, b):
        pack_copy(8 - n, -a, -b).wait_recv()
        start_block(near.at[n], False, n)

    neighbours(start)

    def stage(k):
        @pl.when(my_colour == k)
        def _():
            tx[4] = factor128(mat[...])[1]

            def outgoing(e):
                ea_, eb_ = unslot(e)

                def dispatch(n, a, b):
                    @pl.when(near_pair(ea_ - a, eb_ - b))
                    def _():
                        k_copy(n, e, a, b).start()

                @pl.when(e == 4)
                def _():
                    neighbours(dispatch)

                @pl.when((e != 4) & inside(ea_, eb_) & (colour(ea_, eb_) < k))
                def _():
                    tx[e] = dot3(split(tx[4]), split(g[e]), NT)
                    neighbours(dispatch)

            outgoing(4)
            loop(lambda e: pl.when(e != 4)(lambda: outgoing(e)))

        def arrive(o):
            oa, ob = unslot(o)

            @pl.when(inside(oa, ob) & (colour(oa, ob) == k))
            def _():
                @pl.when(o == 4)
                def _():
                    acc[...] = dot3(split(tx[4]), split(ea[4]), NN)

                @pl.when(o != 4)
                def _():
                    k_copy(8 - o, 4, -oa, -ob).wait_recv()
                    acc[...] = dot3(split(rx[o, 4]), split(ea[o]), NN)

                def term(e):
                    ea_, eb_ = unslot(e)
                    va, vb = oa + ea_, ob + eb_

                    @pl.when((e != 4) & near_pair(va, vb) & inside(va, vb) & (colour(va, vb) < k))
                    def _():
                        right = split(f[(va + 1) * 3 + vb + 1])

                        @pl.when(o == 4)
                        def _():
                            acc[...] -= dot3(split(tx[e]), right, NN)

                        @pl.when(o != 4)
                        def _():
                            k_copy(8 - o, e, -oa, -ob).wait_recv()
                            acc[...] -= dot3(split(rx[o, e]), right, NN)

                loop(term)
                f[o] = acc[...]
                fs[o] = acc[:, :128]

                @pl.when(my_colour > k)
                def _():
                    new = acc[:, 128:] - dot3(split(acc[:, :128]), own_interp, NN)
                    g[o] = new
                    new2 = split(new)
                    mat[...] -= dot3(new2, new2, TN)

                def forward(h):
                    ha, hb = unslot(h)

                    @pl.when(inside(-ha, -hb) & near_pair(oa + ha, ob + hb))
                    def _():
                        x_copy(h, o).start()

                loop(forward, 5, 9)

        loop(arrive)

    loop(stage, 0, 4)

    def centre(o):
        oa, ob = unslot(o)

        @pl.when(inside(oa, ob))
        def _():
            part = split(fs[o])
            acc[:, :128] -= dot3(part, part, TN)

    acc[:, :128] = jnp.where(eye, own[4:5], 0.0)
    loop(centre)
    dd[0] = acc[:, :128]

    def pair(h):
        ha, hb = unslot(h)
        acc[:, :128] = jnp.zeros((128, 128), jnp.float32)

        @pl.when(inside(ha, hb))
        def _():
            def term(o):
                oa, ob = unslot(o)
                va, vb = oa - ha, ob - hb

                @pl.when(inside(oa, ob) & near_pair(va, vb))
                def _():
                    e = (va + 1) * 3 + vb + 1
                    x_copy(h, e).wait_recv()
                    acc[:, :128] -= dot3(split(fs[o]), split(fx[h - 5, e]), TN)

            loop(term)

        dd[h - 4] = acc[:, :128]
        dd[h] = acc[:, :128].T

    loop(pair, 5, 9)

    lane = lax.broadcasted_iota(jnp.int32, (8, 128), 1)

    def gather(items):
        value = jnp.zeros((8, 128), jnp.float32)
        for source, start, place, size in items:
            moved = pltpu.roll(source, (place - start) % 128, 1)
            value = jnp.where((lane >= place) & (lane < place + size), moved, value)
        return value

    heads = [dd[n, 0:8] for n in range(9)]
    corner = [(heads[n], 0, 8 + 8 * n, 8) for n in range(9)]
    wide_rows = [
        gather([(heads[n], 16 * r, 16 + 16 * n, 16) for n in range(7)]) for r in range(8)
    ]
    more_rows = [
        gather(
            [(heads[7 + n], 16 * r, 16 * n, 16) for n in range(2)]
            + [(own, 16 * r, 32, 16), (own, 0, 56, 8)]
        )
        for r in range(8)
    ]
    corner = gather(corner)
    for c in range(16):
        rows = slice(8 * c, 8 * c + 8)
        group = [dd[n, rows] for n in range(9)]
        turn = group[1:]
        for bit in range(3):
            step = 1 << bit
            upper = ((lane // 16) // step) % 2 == 1
            for n in range(8):
                if n & step:
                    continue
                low, high = turn[n], turn[n + step]
                turn[n] = jnp.where(upper, pltpu.roll(high, 16 * step, 1), low)
                turn[n + step] = jnp.where(upper, high, pltpu.roll(low, 128 - 16 * step, 1))
        side = gather([(own, 8 * c, 48, 8)] + [(group[n], 0, 64 + 8 * n, 8) for n in range(8)])
        tail = jnp.where(lane < 8, group[8], corner)
        for r in range(8):
            dest = 16 * r + c
            out_ref[dest, 0] = turn[r]
            first = group[0] if r == 0 else pltpu.roll(group[0], 128 - 16 * r, 1)
            out_ref[dest, 1] = jnp.where(lane < 16, first, wide_rows[r])
            out_ref[dest, 2] = jnp.where((lane < 48) | ((lane >= 56) & (lane < 64)), more_rows[r], side)
            out_ref[dest, 3] = tail

    def finish(n, a, b):
        pack_copy(n, a, b).wait_send()

        def each(e):
            ea_, eb_ = unslot(e)
            is_sent = (e == 4) | (inside(ea_, eb_) & (colour(ea_, eb_) < my_colour))

            @pl.when(is_sent & near_pair(ea_ - a, eb_ - b))
            def _():
                k_copy(n, e, a, b).wait_send()

        loop(each)

    neighbours(finish)

    def finish_x(h):
        ha, hb = unslot(h)

        def each(o):
            oa, ob = unslot(o)

            @pl.when(inside(-ha, -hb) & inside(oa, ob) & near_pair(oa + ha, ob + hb))
            def _():
                x_copy(h, o).wait_send()

        loop(each)

    loop(finish_x, 5, 9)


def box_phase(pack):
    block = (128, 128)
    return pl.pallas_call(
        box_kernel,
        out_shape=jax.ShapeDtypeStruct((128, 4, 8, 128), jnp.float32),
        in_specs=[pl.BlockSpec(memory_space=pltpu.VMEM)],
        out_specs=pl.BlockSpec(memory_space=pltpu.VMEM),
        scratch_shapes=[
            pltpu.VMEM((9, 136, 128), jnp.float32),
            pltpu.VMEM((9, 128, 256), jnp.float32),
            pltpu.VMEM((9, 128, 256), jnp.float32),
            pltpu.VMEM((9,) + block, jnp.float32),
            pltpu.VMEM((9,) + block, jnp.float32),
            pltpu.VMEM(block, jnp.float32),
            pltpu.VMEM((128, 256), jnp.float32),
            pltpu.VMEM((9,) + block, jnp.float32),
            pltpu.VMEM((9, 9) + block, jnp.float32),
            pltpu.VMEM((4, 9) + block, jnp.float32),
            pltpu.VMEM((9,) + block, jnp.float32),
            pltpu.SemaphoreType.DMA((9,)),
            pltpu.SemaphoreType.DMA((9,)),
            pltpu.SemaphoreType.DMA((9, 9)),
            pltpu.SemaphoreType.DMA((9, 9)),
            pltpu.SemaphoreType.DMA((4, 9)),
            pltpu.SemaphoreType.DMA((4, 9)),
        ],
        compiler_params=pltpu.CompilerParams(
            collective_id=0, has_side_effects=True, vmem_limit_bytes=40 * 2**20
        ),
    )(pack)


def cat_right(x):
    hi, lo = split(x)
    return jnp.concatenate([hi, hi, lo], axis=0)


def cat_left(x):
    hi, lo = split(x)
    return jnp.concatenate([hi, lo, hi], axis=1)


def mm(a, b):
    return lax.dot_general(a, b, (NN, ((), ())), preferred_element_type=jnp.float32)


OFFSETS = [0, 1, 15, 16, 17, -1, -15, -16, -17]


def apart():
    return lax.broadcasted_iota(jnp.int32, (128, 128), 0) - lax.broadcasted_iota(
        jnp.int32, (128, 128), 1
    )


def root_block(row_x, row_y, col_x, col_y, lines):
    gap_x = row_x - col_x
    gap_y = row_y - col_y
    square = gap_x * gap_x + gap_y * gap_y
    distance = square * lax.rsqrt(jnp.maximum(square, 1e-36))
    value = jnp.exp2(distance * (-1.4426950408889634 / kernel_len) - 6.0)
    gap = apart()
    extra = jnp.zeros((128, 128), jnp.float32)
    for n in range(9):
        extra = jnp.where(gap == OFFSETS[n], lines[n], extra)
    return value + extra


def shifted_line(line, n):
    return pltpu.roll(line, -OFFSETS[n] % 128, 1) if n > 4 else line


def root_kernel(flag_ref, turned, lead_ref, hi_ref, lo_ref, work, diag, wcur, left, right, wt, tab):
    count = SB // 128
    width = 3 * SB
    chunk = 256
    row = lax.broadcasted_iota(jnp.int32, (128, SB), 0)
    col = lax.broadcasted_iota(jnp.int32, (128, SB), 1)

    def rows_of(i):
        return pl.ds(pl.multiple_of(i * 128, 128), 128)

    for l in range(8):
        for n in range(9):
            place = 64 + 8 * n
            line = turned[16 + l, place : place + 8] if n < 8 else turned[24 + l, 0:8]
            tab[0, l, n] = shifted_line(line, n)
            tab[1, l, n] = shifted_line(turned[24 + l, 8 + 8 * n : 16 + 8 * n], n)

    def assemble(k, _):
        for l in range(8):
            for which in range(2):
                place = 48 + 8 * which + l
                lines = [tab[which, l, n, pl.ds(k, 1)] for n in range(9)]
                start = SB * (1 - which) + 128 * l
                work[rows_of(k), start : start + 128] = root_block(
                    lead_ref[k, 0],
                    lead_ref[k, 1],
                    turned[16, place : place + 1],
                    turned[18, place : place + 1],
                    lines,
                )
        return 0

    lax.fori_loop(0, count, assemble, 0)
    for i in range(count):
        work[128 * i : 128 * i + 128, 2 * SB :] = jnp.where(col == row + 128 * i, 1.0, 0.0)
    work[SB:] = jnp.zeros((128, width), jnp.float32)
    diag[...] = work[:128, :128]
    wcur[...] = jnp.zeros((128, 384), jnp.bfloat16)

    def scale(p):
        here = rows_of(p)
        for c in range(width // chunk):
            cols = slice(c * chunk, c * chunk + chunk)
            new = mm(wcur[...], cat_right(work[here, cols]))
            work[here, cols] = new
            right[:, cols] = cat_right(new)
            for j in range(chunk // 128):
                n = c * (chunk // 128) + j
                if n < count:
                    part = jnp.where(p < n, new[:, 128 * j : 128 * j + 128], 0.0)
                    left[128 * n : 128 * n + 128] = cat_left(part.T)

    def step(i, _):
        p = jnp.where(i == 0, count, i - 1)
        scale(p)
        for c in range(width // chunk):
            cols = slice(c * chunk, c * chunk + chunk)
            work[:SB, cols] -= mm(left[...], right[:, cols])
        w = factor128(diag[...])[1]
        wcur[...] = cat_left(w)
        here, after = rows_of(i), rows_of(i + 1)
        u = mm(wcur[...], cat_right(work[here, after]))
        diag[...] = work[after, after] - mm(cat_left(u.T), cat_right(u))
        return 0

    lax.fori_loop(0, count, step, 0)
    last = rows_of(count - 1)
    for c in range(SB // chunk, width // chunk):
        cols = slice(c * chunk, c * chunk + chunk)
        work[last, cols] = mm(wcur[...], cat_right(work[last, cols]))

    def flip(i, _):
        here = rows_of(i)

        @pl.when(flag_ref[0] == 1)
        def _():
            work[here, SB : 2 * SB] = jnp.where(col == row + 128 * i, -1.0, 0.0)

        hi, lo = split(work[here, SB : 2 * SB])
        right[0:128, :SB] = hi
        hi_ref[here] = hi
        lo_ref[here] = lo
        for j in range(count):
            hi, lo = split(work[here, 2 * SB + 128 * j : 2 * SB + 128 * j + 128].T)
            there = slice(128 * j, 128 * j + 128)
            wt[0, there, here] = hi
            wt[1, there, here] = lo
        return 0

    lax.fori_loop(0, count, flip, 0)
    for c in range(SB // chunk):
        cols = slice(c * chunk, c * chunk + chunk)
        y_hi, y_lo = hi_ref[:, cols], lo_ref[:, cols]
        for m in range(4):
            some = slice(m * 256, m * 256 + 256)
            deep = slice(m * 256, SB)
            w_hi, w_lo = wt[0, some, deep], wt[1, some, deep]
            work[some, cols] = (
                mm(w_hi, y_lo[m * 256 :]) + mm(w_lo, y_hi[m * 256 :]) + mm(w_hi, y_hi[m * 256 :])
            )
        for m in range(4):
            some = slice(m * 256, m * 256 + 256)
            hi, lo = split(work[some, cols])
            hi_ref[some, cols] = hi
            lo_ref[some, cols] = lo


def root_solve(flag, turned, lead):
    return pl.pallas_call(
        root_kernel,
        out_shape=[jax.ShapeDtypeStruct((SB, SB), jnp.bfloat16)] * 2,
        in_specs=[
            pl.BlockSpec(memory_space=pltpu.SMEM),
            pl.BlockSpec(memory_space=pltpu.VMEM),
            pl.BlockSpec(memory_space=pltpu.VMEM),
        ],
        out_specs=[pl.BlockSpec(memory_space=pltpu.VMEM)] * 2,
        scratch_shapes=[
            pltpu.VMEM((SB + 128, 3 * SB), jnp.float32),
            pltpu.VMEM((128, 128), jnp.float32),
            pltpu.VMEM((128, 384), jnp.bfloat16),
            pltpu.VMEM((SB, 384), jnp.bfloat16),
            pltpu.VMEM((384, 3 * SB), jnp.bfloat16),
            pltpu.VMEM((2, SB, SB), jnp.bfloat16),
            pltpu.VMEM((2, 8, 9, 8, 128), jnp.float32),
        ],
        compiler_params=pltpu.CompilerParams(vmem_limit_bytes=48 * 2**20),
    )(flag, turned, lead)


def final_kernel(at_ref, turned, rows_ref, hi_ref, lo_ref, out_ref, tab, buffer):
    rows, cols = out_ref.shape
    s = pl.program_id(0)

    @pl.when(s == 0)
    def _():
        for l in range(8):
            for n in range(9):
                place = 16 * (n - 1)
                line = turned[l, place : place + 16] if n else turned[8 + l, 0:16]
                tab[0, l, n] = shifted_line(line, n)
                place = 16 * n + 16
                line = turned[8 + l, place : place + 16] if n < 7 else turned[16 + l, place - 128 : place - 112]
                tab[1, l, n] = shifted_line(line, n)

    def piece(which, k, l):
        place = 48 + 8 * which + l
        lines = [tab[which, l, n, pl.ds(k, 1)] for n in range(9)]
        return root_block(
            rows_ref[k, 0],
            rows_ref[k, 1],
            turned[16, place : place + 1],
            turned[18, place : place + 1],
            lines,
        )

    ahead = lax.min(s, pl.num_programs(0) - 2)
    now = lax.max(s - 1, 0)
    slot, other = s % 2, (s + 1) % 2
    first = at_ref[0] * (rows * (pl.num_programs(0) - 1)) + now * rows
    start = at_ref[1] * cols
    row = lax.broadcasted_iota(jnp.int32, (128, 128), 0)
    col = lax.broadcasted_iota(jnp.int32, (128, 128), 1)
    for c in range(cols // 256):
        some = slice(c * 256, c * 256 + 256)
        for half in range(2):
            for l in (2 * c, 2 * c + 1):
                hi, lo = split(piece(1, 2 * ahead + half, l))
                buffer[slot, 0, 128 * half : 128 * half + 128, 128 * l : 128 * l + 128] = hi
                buffer[slot, 1, 128 * half : 128 * half + 128, 128 * l : 128 * l + 128] = lo
        x_hi, x_lo = buffer[other, 0], buffer[other, 1]
        hi, lo = hi_ref[:, some], lo_ref[:, some]
        product = mm(x_hi, lo) + mm(x_lo, hi) + mm(x_hi, hi)
        for half in range(2):
            for l in (2 * c, 2 * c + 1):
                base = piece(0, 2 * now + half, l)
                part = product[128 * half : 128 * half + 128, 128 * (l % 2) : 128 * (l % 2) + 128]
                value = jnp.where(at_ref[1] == 0, 0.0, base) - part
                here = first + 128 * half + row
                there = start + 128 * l + col
                out_ref[128 * half : 128 * half + 128, 128 * l : 128 * l + 128] = jnp.where(
                    (here < SB) & (there > here), 0.0, value
                )


def final_product(at, turned, rows_wide, hi, lo):
    block = 256
    steps = 2048 // block
    cols = hi.shape[1]

    def whole(x):
        return pl.BlockSpec(x.shape, lambda i: (0,) * x.ndim)

    return pl.pallas_call(
        final_kernel,
        grid=(steps + 1,),
        out_shape=jax.ShapeDtypeStruct((steps * block, cols), jnp.float32),
        in_specs=[
            pl.BlockSpec(memory_space=pltpu.SMEM),
            whole(turned),
            whole(rows_wide),
            whole(hi),
            whole(lo),
        ],
        out_specs=pl.BlockSpec((block, cols), lambda i: (lax.max(i - 1, 0), 0)),
        scratch_shapes=[
            pltpu.VMEM((2, 8, 9, 16, 128), jnp.float32),
            pltpu.VMEM((2, 2, block, SB), jnp.bfloat16),
        ],
        compiler_params=pltpu.CompilerParams(vmem_limit_bytes=48 * 2**20),
    )(at, turned, rows_wide, hi, lo)


def root_phase(outgoing, row_at, col_at):
    arrived = lax.all_to_all(
        outgoing.reshape(128, 32, 128), ("row", "col"), split_axis=0, concat_axis=0, tiled=True
    )
    turned = jnp.transpose(arrived, (1, 2, 0))

    def wide(start, size):
        part = jnp.stack([turned[16, start : start + size], turned[18, start : start + size]], axis=1)
        return jnp.broadcast_to(part[:, :, :, None], part.shape + (128,))

    flag = (col_at == 0).astype(jnp.int32)
    hi, lo = root_solve(flag[None], turned, wide(56, 8))
    return final_product(jnp.stack([row_at, col_at]), turned, wide(32, 16), hi, lo)


def on_device(offsets, point_order, nugget, interp):
    row_at = lax.axis_index("row")
    col_at = lax.axis_index("col")
    corner = jnp.stack([row_at, col_at]).astype(jnp.float32)[:, None]
    order = point_order[0, 0]
    points = jnp.take(offsets[0, 0] + corner, order, axis=1)
    weights = jnp.take(nugget[0, 0], order)
    lines = jnp.concatenate([points.reshape(4, 128), weights.reshape(2, 128)])
    pack = jnp.concatenate([interp[0, 0], lines, jnp.zeros((2, 128), jnp.float32)])
    return root_phase(box_phase(pack), row_at, col_at)


def solution(mesh):
    in_specs = (
        P("row", "col", None, None),
        P("row", "col", None),
        P("row", "col", None),
        P("row", "col", None, None),
    )
    out_specs = P("row", "col")
    return jax.shard_map(
        on_device, mesh=mesh, in_specs=in_specs, out_specs=out_specs, check_vma=False
    )
```

```python
import jax
import jax.numpy as jnp
from jax import lax
from jax.experimental import pallas as pl
from jax.experimental.pallas import tpu as pltpu
from jax.sharding import PartitionSpec as P

SB = 1024


kernel_len = 0.5


def factor128(a):
    n = a.shape[0]
    G = n // 8
    rows = [a[8*g:8*g+8] for g in range(G)]
    lane = lax.broadcasted_iota(jnp.int32, (8, n), 1)
    sub = lax.broadcasted_iota(jnp.int32, (8, n), 0)
    w = [(lane == sub + 8*g).astype(jnp.float32) for g in range(G)]
    def srow(v, t):
        return jnp.broadcast_to(v[t:t+1], (8, n))
    def lcol(v, t):
        return jnp.broadcast_to(v[:, t:t+1], (8, n))
    us, ws = [], []
    for p in range(G):
        q, qw = rows[p], w[p]
        cols = [lcol(q, 8*p+t) for t in range(8)]
        u, uw, dv = q, qw, None
        for t in range(8):
            pr, pw = srow(q, t), srow(qw, t)
            d = srow(cols[t], t)
            here = sub == t
            u = pr if t == 0 else jnp.where(here, pr, u)
            uw = pw if t == 0 else jnp.where(here, pw, uw)
            dv = d if t == 0 else jnp.where(here, d, dv)
            m = jnp.where(here, 0.0, cols[t]) * (1.0 / d)
            q = q - m * pr
            qw = qw - m * pw
            for v in range(t + 1, 8):
                cols[v] = cols[v] - m * srow(cols[v], t)
        r = lax.rsqrt(dv)
        us.append(jnp.where(lane >= sub + 8*p, u * r, 0.0))
        ws.append(uw * r)
        inv = 1.0 / dv
        z, zw = q * inv, qw * inv
        zs = [srow(z, t) for t in range(8)]
        zws = [srow(zw, t) for t in range(8)]
        for g in range(p + 1, G):
            cg = [lcol(rows[g], 8*p+t) for t in range(8)]
            x = [cg[t] * zs[t] for t in range(8)]
            y = [cg[t] * zws[t] for t in range(8)]
            rows[g] = rows[g] - (((x[0]+x[1])+(x[2]+x[3]))+((x[4]+x[5])+(x[6]+x[7])))
            w[g] = w[g] - (((y[0]+y[1])+(y[2]+y[3]))+((y[4]+y[5])+(y[6]+y[7])))
    return jnp.concatenate(us, 0), jnp.concatenate(ws, 0)


def kappa(gap_x, gap_y):
    square = gap_x * gap_x + gap_y * gap_y
    distance = square * lax.rsqrt(jnp.maximum(square, 1e-36))
    return jnp.exp2(distance * (-1.4426950408889634 / kernel_len) - 6.0)


def split(x):
    hi = x.astype(jnp.bfloat16)
    return hi, (x - hi.astype(jnp.float32)).astype(jnp.bfloat16)


def dot3(a, b, dims):
    def one(x, y):
        return lax.dot_general(x, y, (dims, ((), ())), preferred_element_type=jnp.float32)

    return one(a[0], b[1]) + one(a[1], b[0]) + one(a[0], b[0])


NN = ((1,), (0,))
TN = ((0,), (0,))
NT = ((1,), (1,))


def box_kernel(off_ref, order_ref, nug_ref, interp_ref, out_ref, pack_ref, near, ea, f, fs, g, mat, acc, tx, rx, fx, dd, ps, pr, ks, kr, xs, xr):
    row_at = lax.axis_index("row")
    col_at = lax.axis_index("col")
    row_count = lax.axis_size("row")
    col_count = lax.axis_size("col")

    def inside(a, b):
        r, c = row_at + a, col_at + b
        return (r >= 0) & (r < row_count) & (c >= 0) & (c < col_count)

    def colour(a, b):
        return 2 * ((row_at + a + 2) % 2) + (col_at + b + 2) % 2

    def unslot(n):
        return n // 3 - 1, n % 3 - 1

    def near_pair(a, b):
        return (a >= -1) & (a <= 1) & (b >= -1) & (b <= 1)

    def loop(body, low=0, high=9):
        def step(n, _):
            body(n)
            return 0

        lax.fori_loop(low, high, step, 0)

    def copy(src, dst, send, recv, a, b):
        return pltpu.make_async_remote_copy(
            src_ref=src,
            dst_ref=dst,
            send_sem=send,
            recv_sem=recv,
            device_id=(row_at + a, col_at + b),
            device_id_type=pl.DeviceIdType.MESH,
        )

    def neighbours(body):
        def each(n):
            a, b = unslot(n)

            @pl.when((n != 4) & inside(a, b))
            def _():
                body(n, a, b)

        loop(each)

    def pack_copy(n, a, b):
        return copy(pack_ref, near.at[8 - n], ps.at[n], pr.at[8 - n], a, b)

    def k_copy(n, e, a, b):
        source = tx if isinstance(e, int) else g.at[e]
        return copy(source, rx.at[8 - n, e], ks.at[n, e], kr.at[8 - n, e], a, b)

    def x_copy(h, o):
        a, b = unslot(h)
        return copy(fs.at[o], fx.at[h - 5, o], xs.at[h - 5, o], xr.at[h - 5, o], -a, -b)

    barrier = pltpu.get_barrier_semaphore()

    def greet(n, a, b):
        pl.semaphore_signal(
            barrier,
            inc=1,
            device_id=(row_at + a, col_at + b),
            device_id_type=pl.DeviceIdType.MESH,
        )

    neighbours(greet)
    line = lax.broadcasted_iota(jnp.int32, (16, 256), 0)
    plain = jnp.where(
        line == 0,
        off_ref[0:1] + row_at.astype(jnp.float32),
        jnp.where(
            line == 1,
            off_ref[1:2] + col_at.astype(jnp.float32),
            jnp.where(line == 2, nug_ref[...], 0.0),
        ),
    )
    pick = lax.broadcasted_iota(jnp.int32, (256, 256), 0) == order_ref[...]
    pick = jnp.where(pick, 1.0, 0.0).astype(jnp.bfloat16)
    high = plain.astype(jnp.bfloat16)
    middle, low = split(plain - high.astype(jnp.float32))
    placed = mm(high, pick) + mm(middle, pick) + mm(low, pick)
    level = lax.broadcasted_iota(jnp.int32, (8, 128), 0)
    own = jnp.zeros((8, 128), jnp.float32)
    for n in range(6):
        half = slice(128 * (n % 2), 128 * (n % 2) + 128)
        own = jnp.where(level == n, placed[n // 2 : n // 2 + 1, half], own)
    pack_ref[0:128] = interp_ref[...]
    pack_ref[128:136] = own
    tall = 1 + lax.min(row_at, 1) + lax.min(row_count - 1 - row_at, 1)
    wide = 1 + lax.min(col_at, 1) + lax.min(col_count - 1 - col_at, 1)
    pl.semaphore_wait(barrier, tall * wide - 1)
    neighbours(lambda n, a, b: pack_copy(n, a, b).start())

    own_interp = split(pack_ref[0:128])
    my_colour = colour(0, 0)
    eye = lax.broadcasted_iota(jnp.int32, (128, 128), 0) == lax.broadcasted_iota(
        jnp.int32, (128, 128), 1
    )

    def start_block(source, here, slot):
        where = source[128:136].T
        parts = []
        for s in range(2):
            line = []
            for t in range(2):
                gap_row = where[:, s : s + 1] - own[t : t + 1]
                gap_col = where[:, 2 + s : 3 + s] - own[2 + t : 3 + t]
                block = kappa(gap_row, gap_col)
                if here and s == t:
                    block = block + jnp.where(eye, own[4 + s : 5 + s], 0.0)
                line.append(block)
            parts.append(jnp.concatenate(line, axis=1))
        ea[slot] = parts[1] - dot3(split(source[0:128]), split(parts[0]), TN)

    start_block(pack_ref, True, 4)
    mat[...] = ea[4, :, 128:] - dot3(split(ea[4, :, :128]), own_interp, NN)

    def start(n, a, b):
        pack_copy(8 - n, -a, -b).wait_recv()
        start_block(near.at[n], False, n)

    neighbours(start)

    def stage(k):
        @pl.when(my_colour == k)
        def _():
            tx[...] = factor128(mat[...])[1]
            neighbours(lambda n, a, b: k_copy(n, 4, a, b).start())

        def gather_terms(o):
            oa, ob = unslot(o)

            @pl.when(inside(oa, ob) & (colour(oa, ob) == k))
            def _():
                def term(e):
                    ea_, eb_ = unslot(e)
                    va, vb = oa + ea_, ob + eb_

                    @pl.when((e != 4) & near_pair(va, vb) & inside(va, vb) & (colour(va, vb) < k))
                    def _():
                        right = split(f[(va + 1) * 3 + vb + 1])

                        @pl.when(o == 4)
                        def _():
                            ea[o] -= dot3(split(g[e]), right, NN)

                        @pl.when(o != 4)
                        def _():
                            k_copy(8 - o, e, -oa, -ob).wait_recv()
                            ea[o] -= dot3(split(rx[o, e]), right, NN)

                loop(term)

        loop(gather_terms)

        def arrive(o):
            oa, ob = unslot(o)

            @pl.when(inside(oa, ob) & (colour(oa, ob) == k))
            def _():
                @pl.when(o == 4)
                def _():
                    acc[...] = dot3(split(tx[...]), split(ea[4]), NN)

                @pl.when(o != 4)
                def _():
                    k_copy(8 - o, 4, -oa, -ob).wait_recv()
                    acc[...] = dot3(split(rx[o, 4]), split(ea[o]), NN)

                f[o] = acc[...]
                fs[o] = acc[:, :128]

                @pl.when(my_colour > k)
                def _():
                    new = acc[:, 128:] - dot3(split(acc[:, :128]), own_interp, NN)
                    flip = new.T
                    g[o] = flip
                    mat[...] -= dot3(split(flip), split(new), NN)

                    def early(n, a, b):
                        @pl.when(near_pair(oa - a, ob - b))
                        def _():
                            k_copy(n, o, a, b).start()

                    neighbours(early)

                def forward(h):
                    ha, hb = unslot(h)

                    @pl.when(inside(-ha, -hb) & near_pair(oa + ha, ob + hb))
                    def _():
                        x_copy(h, o).start()

                loop(forward, 5, 9)

        loop(arrive)

    loop(stage, 0, 4)

    def centre(o):
        oa, ob = unslot(o)

        @pl.when(inside(oa, ob))
        def _():
            part = split(fs[o])
            acc[:, :128] -= dot3(part, part, TN)

    acc[:, :128] = jnp.where(eye, own[4:5], 0.0)
    loop(centre)
    dd[0] = acc[:, :128]

    def pair(h):
        ha, hb = unslot(h)
        acc[:, :128] = jnp.zeros((128, 128), jnp.float32)

        @pl.when(inside(ha, hb))
        def _():
            def term(o):
                oa, ob = unslot(o)
                va, vb = oa - ha, ob - hb

                @pl.when(inside(oa, ob) & near_pair(va, vb))
                def _():
                    e = (va + 1) * 3 + vb + 1
                    x_copy(h, e).wait_recv()
                    acc[:, :128] -= dot3(split(fs[o]), split(fx[h - 5, e]), TN)

            loop(term)

        dd[h - 4] = acc[:, :128]
        dd[h] = acc[:, :128].T

    loop(pair, 5, 9)

    lane = lax.broadcasted_iota(jnp.int32, (8, 128), 1)

    def gather(items):
        value = jnp.zeros((8, 128), jnp.float32)
        for source, start, place, size in items:
            moved = pltpu.roll(source, (place - start) % 128, 1)
            value = jnp.where((lane >= place) & (lane < place + size), moved, value)
        return value

    heads = [dd[n, 0:8] for n in range(9)]
    corner = [(heads[n], 0, 8 + 8 * n, 8) for n in range(9)]
    wide_rows = [
        gather([(heads[n], 16 * r, 16 + 16 * n, 16) for n in range(7)]) for r in range(8)
    ]
    more_rows = [
        gather(
            [(heads[7 + n], 16 * r, 16 * n, 16) for n in range(2)]
            + [(own, 16 * r, 32, 16), (own, 0, 56, 8)]
        )
        for r in range(8)
    ]
    corner = gather(corner)
    for c in range(16):
        rows = slice(8 * c, 8 * c + 8)
        group = [dd[n, rows] for n in range(9)]
        turn = group[1:]
        for bit in range(3):
            step = 1 << bit
            upper = ((lane // 16) // step) % 2 == 1
            for n in range(8):
                if n & step:
                    continue
                low, high = turn[n], turn[n + step]
                turn[n] = jnp.where(upper, pltpu.roll(high, 16 * step, 1), low)
                turn[n + step] = jnp.where(upper, high, pltpu.roll(low, 128 - 16 * step, 1))
        side = gather([(own, 8 * c, 48, 8)] + [(group[n], 0, 64 + 8 * n, 8) for n in range(8)])
        tail = jnp.where(lane < 8, group[8], corner)
        for r in range(8):
            dest = 16 * r + c
            out_ref[dest, 0] = turn[r]
            first = group[0] if r == 0 else pltpu.roll(group[0], 128 - 16 * r, 1)
            out_ref[dest, 1] = jnp.where(lane < 16, first, wide_rows[r])
            out_ref[dest, 2] = jnp.where((lane < 48) | ((lane >= 56) & (lane < 64)), more_rows[r], side)
            out_ref[dest, 3] = tail

    def finish(n, a, b):
        pack_copy(n, a, b).wait_send()

        def each(e):
            ea_, eb_ = unslot(e)
            is_sent = (e == 4) | (inside(ea_, eb_) & (colour(ea_, eb_) < my_colour))

            @pl.when(is_sent & near_pair(ea_ - a, eb_ - b))
            def _():
                k_copy(n, e, a, b).wait_send()

        loop(each)

    neighbours(finish)

    def finish_x(h):
        ha, hb = unslot(h)

        def each(o):
            oa, ob = unslot(o)

            @pl.when(inside(-ha, -hb) & inside(oa, ob) & near_pair(oa + ha, ob + hb))
            def _():
                x_copy(h, o).wait_send()

        loop(each)

    loop(finish_x, 5, 9)


def box_phase(off, order, nug, interp):
    block = (128, 128)
    return pl.pallas_call(
        box_kernel,
        out_shape=jax.ShapeDtypeStruct((128, 4, 8, 128), jnp.float32),
        in_specs=[pl.BlockSpec(memory_space=pltpu.VMEM)] * 4,
        out_specs=pl.BlockSpec(memory_space=pltpu.VMEM),
        scratch_shapes=[
            pltpu.VMEM((136, 128), jnp.float32),
            pltpu.VMEM((9, 136, 128), jnp.float32),
            pltpu.VMEM((9, 128, 256), jnp.float32),
            pltpu.VMEM((9, 128, 256), jnp.float32),
            pltpu.VMEM((9,) + block, jnp.float32),
            pltpu.VMEM((9,) + block, jnp.float32),
            pltpu.VMEM(block, jnp.float32),
            pltpu.VMEM((128, 256), jnp.float32),
            pltpu.VMEM(block, jnp.float32),
            pltpu.VMEM((9, 9) + block, jnp.float32),
            pltpu.VMEM((4, 9) + block, jnp.float32),
            pltpu.VMEM((9,) + block, jnp.float32),
            pltpu.SemaphoreType.DMA((9,)),
            pltpu.SemaphoreType.DMA((9,)),
            pltpu.SemaphoreType.DMA((9, 9)),
            pltpu.SemaphoreType.DMA((9, 9)),
            pltpu.SemaphoreType.DMA((4, 9)),
            pltpu.SemaphoreType.DMA((4, 9)),
        ],
        compiler_params=pltpu.CompilerParams(
            collective_id=0, has_side_effects=True, vmem_limit_bytes=40 * 2**20
        ),
    )(off, order, nug, interp)


def cat_right(x):
    hi, lo = split(x)
    return jnp.concatenate([hi, hi, lo], axis=0)


def cat_left(x):
    hi, lo = split(x)
    return jnp.concatenate([hi, lo, hi], axis=1)


def mm(a, b):
    return lax.dot_general(a, b, (NN, ((), ())), preferred_element_type=jnp.float32)


OFFSETS = [0, 1, 15, 16, 17, -1, -15, -16, -17]


def apart():
    return lax.broadcasted_iota(jnp.int32, (128, 128), 0) - lax.broadcasted_iota(
        jnp.int32, (128, 128), 1
    )


def root_block(row_x, row_y, col_x, col_y, lines):
    gap_x = row_x - col_x
    gap_y = row_y - col_y
    value = kappa(gap_x, gap_y)
    gap = apart()
    extra = jnp.zeros((128, 128), jnp.float32)
    for n in range(9):
        extra = jnp.where(gap == OFFSETS[n], lines[n], extra)
    return value + extra


def shifted_line(line, n):
    return pltpu.roll(line, -OFFSETS[n] % 128, 1) if n > 4 else line


def root_kernel(flag_ref, turned, lead_ref, hi_ref, lo_ref, work, diag, wcur, left, right, wt, tab):
    count = SB // 128
    width = 3 * SB
    chunk = 256
    row = lax.broadcasted_iota(jnp.int32, (128, SB), 0)
    col = lax.broadcasted_iota(jnp.int32, (128, SB), 1)

    def rows_of(i):
        return pl.ds(pl.multiple_of(i * 128, 128), 128)

    for l in range(8):
        for n in range(9):
            place = 64 + 8 * n
            line = turned[16 + l, place : place + 8] if n < 8 else turned[24 + l, 0:8]
            tab[0, l, n] = shifted_line(line, n)
            tab[1, l, n] = shifted_line(turned[24 + l, 8 + 8 * n : 16 + 8 * n], n)

    def assemble(k, _):
        for l in range(8):
            for which in range(2):
                place = 48 + 8 * which + l
                lines = [tab[which, l, n, pl.ds(k, 1)] for n in range(9)]
                start = SB * (1 - which) + 128 * l
                work[rows_of(k), start : start + 128] = root_block(
                    lead_ref[k, 0],
                    lead_ref[k, 1],
                    turned[16, place : place + 1],
                    turned[18, place : place + 1],
                    lines,
                )
        return 0

    lax.fori_loop(0, count, assemble, 0)
    for i in range(count):
        work[128 * i : 128 * i + 128, 2 * SB :] = jnp.where(col == row + 128 * i, 1.0, 0.0)
    work[SB:] = jnp.zeros((128, width), jnp.float32)
    diag[...] = work[:128, :128]
    wcur[...] = jnp.zeros((128, 384), jnp.bfloat16)

    def scale(p):
        here = rows_of(p)
        for c in range(width // chunk):
            cols = slice(c * chunk, c * chunk + chunk)
            new = mm(wcur[...], cat_right(work[here, cols]))
            work[here, cols] = new
            right[:, cols] = cat_right(new)
            for j in range(chunk // 128):
                n = c * (chunk // 128) + j
                if n < count:
                    part = jnp.where(p < n, new[:, 128 * j : 128 * j + 128], 0.0)
                    left[128 * n : 128 * n + 128] = cat_left(part.T)

    def step(i, _):
        p = jnp.where(i == 0, count, i - 1)
        scale(p)
        for c in range(width // chunk):
            cols = slice(c * chunk, c * chunk + chunk)
            work[:SB, cols] -= mm(left[...], right[:, cols])
        w = factor128(diag[...])[1]
        wcur[...] = cat_left(w)
        here, after = rows_of(i), rows_of(i + 1)
        u = mm(wcur[...], cat_right(work[here, after]))
        diag[...] = work[after, after] - mm(cat_left(u.T), cat_right(u))
        return 0

    lax.fori_loop(0, count, step, 0)
    last = rows_of(count - 1)
    for c in range(SB // chunk, width // chunk):
        cols = slice(c * chunk, c * chunk + chunk)
        work[last, cols] = mm(wcur[...], cat_right(work[last, cols]))

    def flip(i, _):
        here = rows_of(i)

        @pl.when(flag_ref[0] == 1)
        def _():
            work[here, SB : 2 * SB] = jnp.where(col == row + 128 * i, -1.0, 0.0)

        hi, lo = split(work[here, SB : 2 * SB])
        right[0:128, :SB] = hi
        hi_ref[here] = hi
        lo_ref[here] = lo
        for j in range(count):
            hi, lo = split(work[here, 2 * SB + 128 * j : 2 * SB + 128 * j + 128].T)
            there = slice(128 * j, 128 * j + 128)
            wt[0, there, here] = hi
            wt[1, there, here] = lo
        return 0

    lax.fori_loop(0, count, flip, 0)
    for c in range(SB // chunk):
        cols = slice(c * chunk, c * chunk + chunk)
        y_hi, y_lo = hi_ref[:, cols], lo_ref[:, cols]
        for m in range(4):
            some = slice(m * 256, m * 256 + 256)
            deep = slice(m * 256, SB)
            w_hi, w_lo = wt[0, some, deep], wt[1, some, deep]
            work[some, cols] = (
                mm(w_hi, y_lo[m * 256 :]) + mm(w_lo, y_hi[m * 256 :]) + mm(w_hi, y_hi[m * 256 :])
            )
        for m in range(4):
            some = slice(m * 256, m * 256 + 256)
            hi, lo = split(work[some, cols])
            hi_ref[some, cols] = hi
            lo_ref[some, cols] = lo


def root_solve(flag, turned, lead):
    return pl.pallas_call(
        root_kernel,
        out_shape=[jax.ShapeDtypeStruct((SB, SB), jnp.bfloat16)] * 2,
        in_specs=[
            pl.BlockSpec(memory_space=pltpu.SMEM),
            pl.BlockSpec(memory_space=pltpu.VMEM),
            pl.BlockSpec(memory_space=pltpu.VMEM),
        ],
        out_specs=[pl.BlockSpec(memory_space=pltpu.VMEM)] * 2,
        scratch_shapes=[
            pltpu.VMEM((SB + 128, 3 * SB), jnp.float32),
            pltpu.VMEM((128, 128), jnp.float32),
            pltpu.VMEM((128, 384), jnp.bfloat16),
            pltpu.VMEM((SB, 384), jnp.bfloat16),
            pltpu.VMEM((384, 3 * SB), jnp.bfloat16),
            pltpu.VMEM((2, SB, SB), jnp.bfloat16),
            pltpu.VMEM((2, 8, 9, 8, 128), jnp.float32),
        ],
        compiler_params=pltpu.CompilerParams(vmem_limit_bytes=48 * 2**20),
    )(flag, turned, lead)


def final_kernel(at_ref, turned, rows_ref, hi_ref, lo_ref, out_ref, tab, buf_a, buf_b):
    rows, cols = out_ref.shape
    s = pl.program_id(0)

    @pl.when(s == 0)
    def _():
        for l in range(8):
            for n in range(9):
                place = 16 * (n - 1)
                line = turned[l, place : place + 16] if n else turned[8 + l, 0:16]
                tab[0, l, n] = shifted_line(line, n)
                place = 16 * n + 16
                line = turned[8 + l, place : place + 16] if n < 7 else turned[16 + l, place - 128 : place - 112]
                tab[1, l, n] = shifted_line(line, n)

    def piece(which, k, l):
        place = 48 + 8 * which + l
        lines = [tab[which, l, n, pl.ds(k, 1)] for n in range(9)]
        return root_block(
            rows_ref[k, 0],
            rows_ref[k, 1],
            turned[16, place : place + 1],
            turned[18, place : place + 1],
            lines,
        )

    def fill(buffer, block, l):
        for half in range(2):
            hi, lo = split(piece(1, 2 * block + half, l))
            buffer[0, 128 * half : 128 * half + 128, 128 * l : 128 * l + 128] = hi
            buffer[1, 128 * half : 128 * half + 128, 128 * l : 128 * l + 128] = lo

    @pl.when(s == 0)
    def _():
        for l in range(8):
            fill(buf_a, 0, l)

    blocks = pl.num_programs(0) * 2
    row = lax.broadcasted_iota(jnp.int32, (128, 128), 0)
    col = lax.broadcasted_iota(jnp.int32, (128, 128), 1)
    start = at_ref[1] * cols
    for turn in range(2):
        now = 2 * s + turn
        mine, other = (buf_a, buf_b) if turn == 0 else (buf_b, buf_a)
        first = (at_ref[0] * blocks + now) * 256
        ahead = lax.min(now + 1, blocks - 1)
        for c in range(cols // 256):
            some = slice(c * 256, c * 256 + 256)
            hi, lo = hi_ref[:, some], lo_ref[:, some]
            x_hi, x_lo = mine[0], mine[1]
            product = mm(x_hi, lo) + mm(x_lo, hi) + mm(x_hi, hi)
            for l in (2 * c, 2 * c + 1):
                fill(other, ahead, l)
                for half in range(2):
                    base = piece(0, 2 * now + half, l)
                    part = product[
                        128 * half : 128 * half + 128, 128 * (l % 2) : 128 * (l % 2) + 128
                    ]
                    value = jnp.where(at_ref[1] == 0, 0.0, base) - part
                    here = first + 128 * half + row
                    there = start + 128 * l + col
                    place = 256 * turn + 128 * half
                    out_ref[place : place + 128, 128 * l : 128 * l + 128] = jnp.where(
                        (here < SB) & (there > here), 0.0, value
                    )


def final_product(at, turned, rows_wide, hi, lo):
    block = 512
    steps = 2048 // block
    cols = hi.shape[1]

    def whole(x):
        return pl.BlockSpec(x.shape, lambda i: (0,) * x.ndim)

    return pl.pallas_call(
        final_kernel,
        grid=(steps,),
        out_shape=jax.ShapeDtypeStruct((steps * block, cols), jnp.float32),
        in_specs=[
            pl.BlockSpec(memory_space=pltpu.SMEM),
            whole(turned),
            whole(rows_wide),
            whole(hi),
            whole(lo),
        ],
        out_specs=pl.BlockSpec((block, cols), lambda i: (i, 0)),
        scratch_shapes=[
            pltpu.VMEM((2, 8, 9, 16, 128), jnp.float32),
            pltpu.VMEM((2, block // 2, SB), jnp.bfloat16),
            pltpu.VMEM((2, block // 2, SB), jnp.bfloat16),
        ],
        compiler_params=pltpu.CompilerParams(vmem_limit_bytes=48 * 2**20),
    )(at, turned, rows_wide, hi, lo)


def root_phase(outgoing, row_at, col_at):
    arrived = lax.all_to_all(
        outgoing.reshape(128, 32, 128), ("row", "col"), split_axis=0, concat_axis=0, tiled=True
    )
    turned = jnp.transpose(arrived, (1, 2, 0))

    def wide(start, size):
        part = jnp.stack([turned[16, start : start + size], turned[18, start : start + size]], axis=1)
        return jnp.broadcast_to(part[:, :, :, None], part.shape + (128,))

    flag = (col_at == 0).astype(jnp.int32)
    hi, lo = root_solve(flag[None], turned, wide(56, 8))
    return final_product(jnp.stack([row_at, col_at]), turned, wide(32, 16), hi, lo)


def on_device(offsets, point_order, nugget, interp):
    outgoing = box_phase(offsets[0, 0], point_order[0], nugget[0], interp[0, 0])
    return root_phase(outgoing, lax.axis_index("row"), lax.axis_index("col"))


def solution(mesh):
    in_specs = (
        P("row", "col", None, None),
        P("row", "col", None),
        P("row", "col", None),
        P("row", "col", None, None),
    )
    out_specs = P("row", "col")
    return jax.shard_map(
        on_device, mesh=mesh, in_specs=in_specs, out_specs=out_specs, check_vma=False
    )
```

```python
import jax
import jax.numpy as jnp
from jax import lax
from jax.experimental import pallas as pl
from jax.experimental.pallas import tpu as pltpu
from jax.sharding import PartitionSpec as P

SB = 1024


kernel_len = 0.5


def factor128(a):
    n = a.shape[0]
    G = n // 8
    rows = [a[8*g:8*g+8] for g in range(G)]
    lane = lax.broadcasted_iota(jnp.int32, (8, n), 1)
    sub = lax.broadcasted_iota(jnp.int32, (8, n), 0)
    w = [(lane == sub + 8*g).astype(jnp.float32) for g in range(G)]
    def srow(v, t):
        return jnp.broadcast_to(v[t:t+1], (8, n))
    def lcol(v, t):
        return jnp.broadcast_to(v[:, t:t+1], (8, n))
    us, ws = [], []
    for p in range(G):
        q, qw = rows[p], w[p]
        cols = [lcol(q, 8*p+t) for t in range(8)]
        u, uw, dv = q, qw, None
        for t in range(8):
            pr, pw = srow(q, t), srow(qw, t)
            d = srow(cols[t], t)
            here = sub == t
            u = pr if t == 0 else jnp.where(here, pr, u)
            uw = pw if t == 0 else jnp.where(here, pw, uw)
            dv = d if t == 0 else jnp.where(here, d, dv)
            m = jnp.where(here, 0.0, cols[t]) * (1.0 / d)
            q = q - m * pr
            qw = qw - m * pw
            for v in range(t + 1, 8):
                cols[v] = cols[v] - m * srow(cols[v], t)
        r = lax.rsqrt(dv)
        us.append(jnp.where(lane >= sub + 8*p, u * r, 0.0))
        ws.append(uw * r)
        inv = 1.0 / dv
        z, zw = q * inv, qw * inv
        zs = [srow(z, t) for t in range(8)]
        zws = [srow(zw, t) for t in range(8)]
        for g in range(p + 1, G):
            cg = [lcol(rows[g], 8*p+t) for t in range(8)]
            x = [cg[t] * zs[t] for t in range(8)]
            y = [cg[t] * zws[t] for t in range(8)]
            rows[g] = rows[g] - (((x[0]+x[1])+(x[2]+x[3]))+((x[4]+x[5])+(x[6]+x[7])))
            w[g] = w[g] - (((y[0]+y[1])+(y[2]+y[3]))+((y[4]+y[5])+(y[6]+y[7])))
    return jnp.concatenate(us, 0), jnp.concatenate(ws, 0)


def kappa(gap_x, gap_y):
    square = gap_x * gap_x + gap_y * gap_y
    distance = square * lax.rsqrt(jnp.maximum(square, 1e-36))
    return jnp.exp2(distance * (-1.4426950408889634 / kernel_len) - 6.0)


def split(x):
    hi = x.astype(jnp.bfloat16)
    return hi, (x - hi.astype(jnp.float32)).astype(jnp.bfloat16)


def dot3(a, b, dims):
    def one(x, y):
        return lax.dot_general(x, y, (dims, ((), ())), preferred_element_type=jnp.float32)

    return one(a[0], b[1]) + one(a[1], b[0]) + one(a[0], b[0])


NN = ((1,), (0,))
TN = ((0,), (0,))
NT = ((1,), (1,))


def box_kernel(off_ref, order_ref, nug_ref, interp_ref, out_ref, pack_ref, near, ea, f, fs, g, mat, acc, tx, rx, fx, dd, ps, pr, ks, kr, xs, xr):
    row_at = lax.axis_index("row")
    col_at = lax.axis_index("col")
    row_count = lax.axis_size("row")
    col_count = lax.axis_size("col")

    def inside(a, b):
        r, c = row_at + a, col_at + b
        return (r >= 0) & (r < row_count) & (c >= 0) & (c < col_count)

    def colour(a, b):
        return 2 * ((row_at + a + 2) % 2) + (col_at + b + 2) % 2

    def unslot(n):
        return n // 3 - 1, n % 3 - 1

    def near_pair(a, b):
        return (a >= -1) & (a <= 1) & (b >= -1) & (b <= 1)

    def loop(body, low=0, high=9):
        def step(n, _):
            body(n)
            return 0

        lax.fori_loop(low, high, step, 0)

    def copy(src, dst, send, recv, a, b):
        return pltpu.make_async_remote_copy(
            src_ref=src,
            dst_ref=dst,
            send_sem=send,
            recv_sem=recv,
            device_id=(row_at + a, col_at + b),
            device_id_type=pl.DeviceIdType.MESH,
        )

    def neighbours(body):
        def each(n):
            a, b = unslot(n)

            @pl.when((n != 4) & inside(a, b))
            def _():
                body(n, a, b)

        loop(each)

    def pack_copy(n, a, b):
        return copy(pack_ref, near.at[8 - n], ps.at[n], pr.at[8 - n], a, b)

    def k_copy(n, e, a, b):
        source = tx if isinstance(e, int) else g.at[e]
        return copy(source, rx.at[8 - n, e], ks.at[n, e], kr.at[8 - n, e], a, b)

    def x_copy(h, o):
        a, b = unslot(h)
        return copy(fs.at[o], fx.at[h - 5, o], xs.at[h - 5, o], xr.at[h - 5, o], -a, -b)

    barrier = pltpu.get_barrier_semaphore()

    def greet(n, a, b):
        pl.semaphore_signal(
            barrier,
            inc=1,
            device_id=(row_at + a, col_at + b),
            device_id_type=pl.DeviceIdType.MESH,
        )

    neighbours(greet)
    line = lax.broadcasted_iota(jnp.int32, (16, 256), 0)
    plain = jnp.where(
        line == 0,
        off_ref[0:1] + row_at.astype(jnp.float32),
        jnp.where(
            line == 1,
            off_ref[1:2] + col_at.astype(jnp.float32),
            jnp.where(line == 2, nug_ref[...], 0.0),
        ),
    )
    pick = lax.broadcasted_iota(jnp.int32, (256, 256), 0) == order_ref[...]
    pick = jnp.where(pick, 1.0, 0.0).astype(jnp.bfloat16)
    high = plain.astype(jnp.bfloat16)
    middle, low = split(plain - high.astype(jnp.float32))
    placed = mm(high, pick) + mm(middle, pick) + mm(low, pick)
    level = lax.broadcasted_iota(jnp.int32, (8, 128), 0)
    own = jnp.zeros((8, 128), jnp.float32)
    for n in range(6):
        half = slice(128 * (n % 2), 128 * (n % 2) + 128)
        own = jnp.where(level == n, placed[n // 2 : n // 2 + 1, half], own)
    pack_ref[0:128] = interp_ref[...]
    pack_ref[128:136] = own
    tall = 1 + lax.min(row_at, 1) + lax.min(row_count - 1 - row_at, 1)
    wide = 1 + lax.min(col_at, 1) + lax.min(col_count - 1 - col_at, 1)
    pl.semaphore_wait(barrier, tall * wide - 1)
    neighbours(lambda n, a, b: pack_copy(n, a, b).start())

    own_interp = split(pack_ref[0:128])
    my_colour = colour(0, 0)
    eye = lax.broadcasted_iota(jnp.int32, (128, 128), 0) == lax.broadcasted_iota(
        jnp.int32, (128, 128), 1
    )

    def start_block(source, here, slot):
        where = source[128:136].T
        parts = []
        for s in range(2):
            line = []
            for t in range(2):
                gap_row = where[:, s : s + 1] - own[t : t + 1]
                gap_col = where[:, 2 + s : 3 + s] - own[2 + t : 3 + t]
                block = kappa(gap_row, gap_col)
                if here and s == t:
                    block = block + jnp.where(eye, own[4 + s : 5 + s], 0.0)
                line.append(block)
            parts.append(jnp.concatenate(line, axis=1))
        ea[slot] = parts[1] - dot3(split(source[0:128]), split(parts[0]), TN)

    start_block(pack_ref, True, 4)
    mat[...] = ea[4, :, 128:] - dot3(split(ea[4, :, :128]), own_interp, NN)

    def start(n, a, b):
        pack_copy(8 - n, -a, -b).wait_recv()
        start_block(near.at[n], False, n)

    neighbours(start)

    def stage(k):
        @pl.when(my_colour == k)
        def _():
            tx[...] = factor128(mat[...])[1]
            neighbours(lambda n, a, b: k_copy(n, 4, a, b).start())

        def gather_terms(o):
            oa, ob = unslot(o)

            @pl.when(inside(oa, ob) & (colour(oa, ob) == k))
            def _():
                def term(e):
                    ea_, eb_ = unslot(e)
                    va, vb = oa + ea_, ob + eb_

                    @pl.when((e != 4) & near_pair(va, vb) & inside(va, vb) & (colour(va, vb) < k))
                    def _():
                        right = split(f[(va + 1) * 3 + vb + 1])

                        @pl.when(o == 4)
                        def _():
                            ea[o] -= dot3(split(g[e]), right, NN)

                        @pl.when(o != 4)
                        def _():
                            k_copy(8 - o, e, -oa, -ob).wait_recv()
                            ea[o] -= dot3(split(rx[o, e]), right, NN)

                loop(term)

        loop(gather_terms)

        def arrive(o):
            oa, ob = unslot(o)

            @pl.when(inside(oa, ob) & (colour(oa, ob) == k))
            def _():
                @pl.when(o == 4)
                def _():
                    acc[...] = dot3(split(tx[...]), split(ea[4]), NN)

                @pl.when(o != 4)
                def _():
                    k_copy(8 - o, 4, -oa, -ob).wait_recv()
                    acc[...] = dot3(split(rx[o, 4]), split(ea[o]), NN)

                f[o] = acc[...]
                fs[o] = acc[:, :128]

                @pl.when(my_colour > k)
                def _():
                    new = acc[:, 128:] - dot3(split(acc[:, :128]), own_interp, NN)
                    flip = new.T
                    g[o] = flip
                    mat[...] -= dot3(split(flip), split(new), NN)

                    def early(n, a, b):
                        @pl.when(near_pair(oa - a, ob - b))
                        def _():
                            k_copy(n, o, a, b).start()

                    neighbours(early)

                def forward(h):
                    ha, hb = unslot(h)

                    @pl.when(inside(-ha, -hb) & near_pair(oa + ha, ob + hb))
                    def _():
                        x_copy(h, o).start()

                loop(forward, 5, 9)

        loop(arrive)

    loop(stage, 0, 4)

    def centre(o):
        oa, ob = unslot(o)

        @pl.when(inside(oa, ob))
        def _():
            part = split(fs[o])
            acc[:, :128] -= dot3(part, part, TN)

    acc[:, :128] = jnp.where(eye, own[4:5], 0.0)
    loop(centre)
    dd[0] = acc[:, :128]

    def pair(h):
        ha, hb = unslot(h)
        acc[:, :128] = jnp.zeros((128, 128), jnp.float32)

        @pl.when(inside(ha, hb))
        def _():
            def term(o):
                oa, ob = unslot(o)
                va, vb = oa - ha, ob - hb

                @pl.when(inside(oa, ob) & near_pair(va, vb))
                def _():
                    e = (va + 1) * 3 + vb + 1
                    x_copy(h, e).wait_recv()
                    acc[:, :128] -= dot3(split(fs[o]), split(fx[h - 5, e]), TN)

            loop(term)

        dd[h - 4] = acc[:, :128]
        dd[h] = acc[:, :128].T

    loop(pair, 5, 9)

    lane = lax.broadcasted_iota(jnp.int32, (8, 128), 1)

    def gather(items):
        value = jnp.zeros((8, 128), jnp.float32)
        for source, start, place, size in items:
            moved = pltpu.roll(source, (place - start) % 128, 1)
            value = jnp.where((lane >= place) & (lane < place + size), moved, value)
        return value

    heads = [dd[n, 0:8] for n in range(9)]
    corner = [(heads[n], 0, 8 + 8 * n, 8) for n in range(9)]
    wide_rows = [
        gather([(heads[n], 16 * r, 16 + 16 * n, 16) for n in range(7)]) for r in range(8)
    ]
    more_rows = [
        gather(
            [(heads[7 + n], 16 * r, 16 * n, 16) for n in range(2)]
            + [(own, 16 * r, 32, 16), (own, 0, 56, 8)]
        )
        for r in range(8)
    ]
    corner = gather(corner)
    for c in range(16):
        rows = slice(8 * c, 8 * c + 8)
        group = [dd[n, rows] for n in range(9)]
        turn = group[1:]
        for bit in range(3):
            step = 1 << bit
            upper = ((lane // 16) // step) % 2 == 1
            for n in range(8):
                if n & step:
                    continue
                low, high = turn[n], turn[n + step]
                turn[n] = jnp.where(upper, pltpu.roll(high, 16 * step, 1), low)
                turn[n + step] = jnp.where(upper, high, pltpu.roll(low, 128 - 16 * step, 1))
        side = gather([(own, 8 * c, 48, 8)] + [(group[n], 0, 64 + 8 * n, 8) for n in range(8)])
        tail = jnp.where(lane < 8, group[8], corner)
        for r in range(8):
            dest = 16 * r + c
            out_ref[dest, 0] = turn[r]
            first = group[0] if r == 0 else pltpu.roll(group[0], 128 - 16 * r, 1)
            out_ref[dest, 1] = jnp.where(lane < 16, first, wide_rows[r])
            out_ref[dest, 2] = jnp.where((lane < 48) | ((lane >= 56) & (lane < 64)), more_rows[r], side)
            out_ref[dest, 3] = tail

    def finish(n, a, b):
        pack_copy(n, a, b).wait_send()

        def each(e):
            ea_, eb_ = unslot(e)
            is_sent = (e == 4) | (inside(ea_, eb_) & (colour(ea_, eb_) < my_colour))

            @pl.when(is_sent & near_pair(ea_ - a, eb_ - b))
            def _():
                k_copy(n, e, a, b).wait_send()

        loop(each)

    neighbours(finish)

    def finish_x(h):
        ha, hb = unslot(h)

        def each(o):
            oa, ob = unslot(o)

            @pl.when(inside(-ha, -hb) & inside(oa, ob) & near_pair(oa + ha, ob + hb))
            def _():
                x_copy(h, o).wait_send()

        loop(each)

    loop(finish_x, 5, 9)


def box_phase(off, order, nug, interp):
    block = (128, 128)
    return pl.pallas_call(
        box_kernel,
        out_shape=jax.ShapeDtypeStruct((128, 4, 8, 128), jnp.float32),
        in_specs=[pl.BlockSpec(memory_space=pltpu.VMEM)] * 4,
        out_specs=pl.BlockSpec(memory_space=pltpu.VMEM),
        scratch_shapes=[
            pltpu.VMEM((136, 128), jnp.float32),
            pltpu.VMEM((9, 136, 128), jnp.float32),
            pltpu.VMEM((9, 128, 256), jnp.float32),
            pltpu.VMEM((9, 128, 256), jnp.float32),
            pltpu.VMEM((9,) + block, jnp.float32),
            pltpu.VMEM((9,) + block, jnp.float32),
            pltpu.VMEM(block, jnp.float32),
            pltpu.VMEM((128, 256), jnp.float32),
            pltpu.VMEM(block, jnp.float32),
            pltpu.VMEM((9, 9) + block, jnp.float32),
            pltpu.VMEM((4, 9) + block, jnp.float32),
            pltpu.VMEM((9,) + block, jnp.float32),
            pltpu.SemaphoreType.DMA((9,)),
            pltpu.SemaphoreType.DMA((9,)),
            pltpu.SemaphoreType.DMA((9, 9)),
            pltpu.SemaphoreType.DMA((9, 9)),
            pltpu.SemaphoreType.DMA((4, 9)),
            pltpu.SemaphoreType.DMA((4, 9)),
        ],
        compiler_params=pltpu.CompilerParams(
            collective_id=0, has_side_effects=True, vmem_limit_bytes=40 * 2**20
        ),
    )(off, order, nug, interp)


def cat_right(x):
    hi, lo = split(x)
    return jnp.concatenate([hi, hi, lo], axis=0)


def cat_left(x):
    hi, lo = split(x)
    return jnp.concatenate([hi, lo, hi], axis=1)


def mm(a, b):
    return lax.dot_general(a, b, (NN, ((), ())), preferred_element_type=jnp.float32)


OFFSETS = [0, 1, 15, 16, 17, -1, -15, -16, -17]


def apart():
    return lax.broadcasted_iota(jnp.int32, (128, 128), 0) - lax.broadcasted_iota(
        jnp.int32, (128, 128), 1
    )


def root_block(row_x, row_y, col_x, col_y, lines):
    gap_x = row_x - col_x
    gap_y = row_y - col_y
    value = kappa(gap_x, gap_y)
    gap = apart()
    extra = jnp.zeros((128, 128), jnp.float32)
    for n in range(9):
        extra = jnp.where(gap == OFFSETS[n], lines[n], extra)
    return value + extra


def shifted_line(line, n):
    return pltpu.roll(line, -OFFSETS[n] % 128, 1) if n > 4 else line


def tail_kernel(
    at_ref,
    turned,
    lead_ref,
    rows_ref,
    out_ref,
    work,
    diag,
    wcur,
    left,
    right,
    wt,
    z_hi,
    z_lo,
    x_hi,
    x_lo,
    base,
    tab,
    table,
    sems,
):
    count = SB // 128
    width = 3 * SB
    chunk = 256
    row = lax.broadcasted_iota(jnp.int32, (128, SB), 0)
    col = lax.broadcasted_iota(jnp.int32, (128, SB), 1)

    def rows_of(i):
        return pl.ds(pl.multiple_of(i * 128, 128), 128)

    for l in range(8):
        for n in range(9):
            place = 64 + 8 * n
            line = turned[16 + l, place : place + 8] if n < 8 else turned[24 + l, 0:8]
            tab[0, l, n] = shifted_line(line, n)
            tab[1, l, n] = shifted_line(turned[24 + l, 8 + 8 * n : 16 + 8 * n], n)
            place = 16 * (n - 1)
            line = turned[l, place : place + 16] if n else turned[8 + l, 0:16]
            table[0, l, n] = shifted_line(line, n)
            place = 16 * n + 16
            if n < 7:
                line = turned[8 + l, place : place + 16]
            else:
                line = turned[16 + l, place - 128 : place - 112]
            table[1, l, n] = shifted_line(line, n)

    def piece(values, wide, which, k, l):
        place = 48 + 8 * which + l
        return root_block(
            wide[k, 0],
            wide[k, 1],
            turned[16, place : place + 1],
            turned[18, place : place + 1],
            [values[which, l, n, pl.ds(k, 1)] for n in range(9)],
        )

    def assemble(k, _):
        for l in range(8):
            work[rows_of(k), SB + 128 * l : SB + 128 * l + 128] = piece(tab, lead_ref, 0, k, l)

            @pl.when(k <= l)
            def _():
                work[rows_of(k), 128 * l : 128 * l + 128] = piece(tab, lead_ref, 1, k, l)

            @pl.when(k > l)
            def _():
                work[rows_of(k), 128 * l : 128 * l + 128] = jnp.zeros((128, 128), jnp.float32)

        return 0

    lax.fori_loop(0, count, assemble, 0)
    for i in range(count):
        work[128 * i : 128 * i + 128, 2 * SB :] = jnp.where(col == row + 128 * i, 1.0, 0.0)
    work[SB:] = jnp.zeros((128, width), jnp.float32)
    diag[...] = work[:128, :128]
    wcur[...] = jnp.zeros((128, 384), jnp.bfloat16)

    def build(k):
        for l in range(8):
            cols = slice(128 * l, 128 * l + 128)
            hi, lo = split(piece(table, rows_ref, 1, k, l))
            x_hi[rows_of(k), cols] = hi
            x_lo[rows_of(k), cols] = lo
            base[rows_of(k), cols] = piece(table, rows_ref, 0, k, l)

    def scale(p):
        here = rows_of(p)
        for c in range(width // chunk):
            cols = slice(c * chunk, c * chunk + chunk)
            new = mm(wcur[...], cat_right(work[here, cols]))
            work[here, cols] = new
            right[:, cols] = cat_right(new)
            for j in range(chunk // 128):
                n = c * (chunk // 128) + j
                if n < count:
                    part = jnp.where(p < n, new[:, 128 * j : 128 * j + 128], 0.0)
                    left[128 * n : 128 * n + 128] = cat_left(part.T)

    def step(i, _):
        p = jnp.where(i == 0, count, i - 1)
        scale(p)
        for c in range(width // chunk):
            cols = slice(c * chunk, c * chunk + chunk)
            work[:SB, cols] -= mm(left[...], right[:, cols])
        build(2 * i)
        build(2 * i + 1)
        w = factor128(diag[...])[1]
        wcur[...] = cat_left(w)
        here, after = rows_of(i), rows_of(i + 1)
        u = mm(wcur[...], cat_right(work[here, after]))
        diag[...] = work[after, after] - mm(cat_left(u.T), cat_right(u))
        return 0

    lax.fori_loop(0, count, step, 0)
    last = rows_of(count - 1)
    for c in range(SB // chunk, width // chunk):
        cols = slice(c * chunk, c * chunk + chunk)
        work[last, cols] = mm(wcur[...], cat_right(work[last, cols]))

    def flip(i, _):
        here = rows_of(i)

        @pl.when(at_ref[1] == 0)
        def _():
            work[here, SB : 2 * SB] = jnp.where(col == row + 128 * i, -1.0, 0.0)

        hi, lo = split(work[here, SB : 2 * SB])
        right[0:128, :SB] = hi
        z_hi[here] = hi
        z_lo[here] = lo
        for j in range(count):
            hi, lo = split(work[here, 2 * SB + 128 * j : 2 * SB + 128 * j + 128].T)
            there = slice(128 * j, 128 * j + 128)
            wt[0, there, here] = hi
            wt[1, there, here] = lo
        return 0

    lax.fori_loop(0, count, flip, 0)
    for c in range(SB // chunk):
        cols = slice(c * chunk, c * chunk + chunk)
        y_hi, y_lo = z_hi[:, cols], z_lo[:, cols]
        for m in range(4):
            some = slice(m * 256, m * 256 + 256)
            deep = slice(m * 256, SB)
            w_hi, w_lo = wt[0, some, deep], wt[1, some, deep]
            work[some, cols] = (
                mm(w_hi, y_lo[m * 256 :]) + mm(w_lo, y_hi[m * 256 :]) + mm(w_hi, y_hi[m * 256 :])
            )
        for m in range(4):
            some = slice(m * 256, m * 256 + 256)
            hi, lo = split(work[some, cols])
            z_hi[some, cols] = hi
            z_lo[some, cols] = lo

    tall = 512

    def product(r, _):
        here = pl.ds(pl.multiple_of(r * tall, tall), tall)
        for c in range(SB // chunk):
            cols = slice(c * chunk, c * chunk + chunk)
            part = (
                mm(x_hi[here], z_lo[:, cols])
                + mm(x_lo[here], z_hi[:, cols])
                + mm(x_hi[here], z_hi[:, cols])
            )
            value = jnp.where(at_ref[1] == 0, 0.0, base[here, cols]) - part
            down = (at_ref[0] * 4 + r) * tall + lax.broadcasted_iota(jnp.int32, value.shape, 0)
            over = at_ref[1] * SB + c * chunk + lax.broadcasted_iota(jnp.int32, value.shape, 1)
            base[here, cols] = jnp.where((down < SB) & (over > down), 0.0, value)
        pltpu.make_async_copy(base.at[here], out_ref.at[here], sems.at[r]).start()
        return 0

    lax.fori_loop(0, 4, product, 0)
    for r in range(4):
        here = slice(r * tall, r * tall + tall)
        pltpu.make_async_copy(base.at[here], out_ref.at[here], sems.at[r]).wait()


def tail_solve(at, turned, lead, rows_wide):
    vmem = pl.BlockSpec(memory_space=pltpu.VMEM)
    return pl.pallas_call(
        tail_kernel,
        out_shape=jax.ShapeDtypeStruct((2048, SB), jnp.float32),
        in_specs=[pl.BlockSpec(memory_space=pltpu.SMEM), vmem, vmem, vmem],
        out_specs=pl.BlockSpec(memory_space=pl.ANY),
        scratch_shapes=[
            pltpu.VMEM((SB + 128, 3 * SB), jnp.float32),
            pltpu.VMEM((128, 128), jnp.float32),
            pltpu.VMEM((128, 384), jnp.bfloat16),
            pltpu.VMEM((SB, 384), jnp.bfloat16),
            pltpu.VMEM((384, 3 * SB), jnp.bfloat16),
            pltpu.VMEM((2, SB, SB), jnp.bfloat16),
            pltpu.VMEM((SB, SB), jnp.bfloat16),
            pltpu.VMEM((SB, SB), jnp.bfloat16),
            pltpu.VMEM((2048, SB), jnp.bfloat16),
            pltpu.VMEM((2048, SB), jnp.bfloat16),
            pltpu.VMEM((2048, SB), jnp.float32),
            pltpu.VMEM((2, 8, 9, 8, 128), jnp.float32),
            pltpu.VMEM((2, 8, 9, 16, 128), jnp.float32),
            pltpu.SemaphoreType.DMA((4,)),
        ],
        compiler_params=pltpu.CompilerParams(vmem_limit_bytes=60 * 2**20),
    )(at, turned, lead, rows_wide)


def root_phase(outgoing, row_at, col_at):
    arrived = lax.all_to_all(
        outgoing.reshape(128, 32, 128), ("row", "col"), split_axis=0, concat_axis=0, tiled=True
    )
    turned = jnp.transpose(arrived, (1, 2, 0))

    def wide(start, size):
        part = jnp.stack([turned[16, start : start + size], turned[18, start : start + size]], axis=1)
        return jnp.broadcast_to(part[:, :, :, None], part.shape + (128,))

    return tail_solve(jnp.stack([row_at, col_at]), turned, wide(56, 8), wide(32, 16))


def on_device(offsets, point_order, nugget, interp):
    outgoing = box_phase(offsets[0, 0], point_order[0], nugget[0], interp[0, 0])
    return root_phase(outgoing, lax.axis_index("row"), lax.axis_index("col"))


def solution(mesh):
    in_specs = (
        P("row", "col", None, None),
        P("row", "col", None),
        P("row", "col", None),
        P("row", "col", None, None),
    )
    out_specs = P("row", "col")
    return jax.shard_map(
        on_device, mesh=mesh, in_specs=in_specs, out_specs=out_specs, check_vma=False
    )
```

```python
import jax
import jax.numpy as jnp
from jax import lax
from jax.experimental import pallas as pl
from jax.experimental.pallas import tpu as pltpu
from jax.sharding import PartitionSpec as P

SB = 1024


kernel_len = 0.5


def factor128(a, side=None):
    n = a.shape[0]
    G = n // 8
    rows = [a[8*g:8*g+8] for g in range(G)]
    lane = lax.broadcasted_iota(jnp.int32, (8, n), 1)
    sub = lax.broadcasted_iota(jnp.int32, (8, n), 0)
    w = [(lane == sub + 8*g).astype(jnp.float32) for g in range(G)]
    def srow(v, t):
        return jnp.broadcast_to(v[t:t+1], (8, n))
    def lcol(v, t):
        return jnp.broadcast_to(v[:, t:t+1], (8, n))
    us, ws = [], []
    for p in range(G):
        q, qw = rows[p], w[p]
        cols = [lcol(q, 8*p+t) for t in range(8)]
        u, uw, dv = q, qw, None
        for t in range(8):
            pr, pw = srow(q, t), srow(qw, t)
            d = srow(cols[t], t)
            here = sub == t
            u = pr if t == 0 else jnp.where(here, pr, u)
            uw = pw if t == 0 else jnp.where(here, pw, uw)
            dv = d if t == 0 else jnp.where(here, d, dv)
            m = jnp.where(here, 0.0, cols[t]) * (1.0 / d)
            q = q - m * pr
            qw = qw - m * pw
            for v in range(t + 1, 8):
                cols[v] = cols[v] - m * srow(cols[v], t)
        if side is not None:
            side(p, jnp.minimum(jnp.abs(dv[0:1]), 0.0))
        r = lax.rsqrt(dv)
        us.append(jnp.where(lane >= sub + 8*p, u * r, 0.0))
        ws.append(uw * r)
        inv = 1.0 / dv
        z, zw = q * inv, qw * inv
        zs = [srow(z, t) for t in range(8)]
        zws = [srow(zw, t) for t in range(8)]
        for g in range(p + 1, G):
            cg = [lcol(rows[g], 8*p+t) for t in range(8)]
            x = [cg[t] * zs[t] for t in range(8)]
            y = [cg[t] * zws[t] for t in range(8)]
            rows[g] = rows[g] - (((x[0]+x[1])+(x[2]+x[3]))+((x[4]+x[5])+(x[6]+x[7])))
            w[g] = w[g] - (((y[0]+y[1])+(y[2]+y[3]))+((y[4]+y[5])+(y[6]+y[7])))
    return jnp.concatenate(us, 0), jnp.concatenate(ws, 0)


def kappa(gap_x, gap_y):
    square = gap_x * gap_x + gap_y * gap_y
    distance = square * lax.rsqrt(jnp.maximum(square, 1e-36))
    return jnp.exp2(distance * (-1.4426950408889634 / kernel_len) - 6.0)


def split(x):
    hi = x.astype(jnp.bfloat16)
    return hi, (x - hi.astype(jnp.float32)).astype(jnp.bfloat16)


def dot3(a, b, dims):
    def one(x, y):
        return lax.dot_general(x, y, (dims, ((), ())), preferred_element_type=jnp.float32)

    return one(a[0], b[1]) + one(a[1], b[0]) + one(a[0], b[0])


NN = ((1,), (0,))
TN = ((0,), (0,))
NT = ((1,), (1,))


def box_kernel(off_ref, order_ref, nug_ref, interp_ref, out_ref, pack_ref, near, ea, f, fs, g, mat, acc, tx, rx, fx, dd, ps, pr, ks, kr, xs, xr):
    row_at = lax.axis_index("row")
    col_at = lax.axis_index("col")
    row_count = lax.axis_size("row")
    col_count = lax.axis_size("col")

    def inside(a, b):
        r, c = row_at + a, col_at + b
        return (r >= 0) & (r < row_count) & (c >= 0) & (c < col_count)

    def colour(a, b):
        return 2 * ((row_at + a + 2) % 2) + (col_at + b + 2) % 2

    def unslot(n):
        return n // 3 - 1, n % 3 - 1

    def near_pair(a, b):
        return (a >= -1) & (a <= 1) & (b >= -1) & (b <= 1)

    def loop(body, low=0, high=9):
        def step(n, _):
            body(n)
            return 0

        lax.fori_loop(low, high, step, 0)

    def copy(src, dst, send, recv, a, b):
        return pltpu.make_async_remote_copy(
            src_ref=src,
            dst_ref=dst,
            send_sem=send,
            recv_sem=recv,
            device_id=(row_at + a, col_at + b),
            device_id_type=pl.DeviceIdType.MESH,
        )

    def neighbours(body):
        def each(n):
            a, b = unslot(n)

            @pl.when((n != 4) & inside(a, b))
            def _():
                body(n, a, b)

        loop(each)

    def pack_copy(n, a, b):
        return copy(pack_ref, near.at[8 - n], ps.at[n], pr.at[8 - n], a, b)

    def k_copy(n, e, a, b, inverse):
        source = tx if inverse else g.at[e]
        return copy(source, rx.at[8 - n, e], ks.at[n, e], kr.at[8 - n, e], a, b)

    def x_copy(h, o):
        a, b = unslot(h)
        return copy(fs.at[o], fx.at[h - 5, o], xs.at[h - 5, o], xr.at[h - 5, o], -a, -b)

    barrier = pltpu.get_barrier_semaphore()

    def greet(n, a, b):
        pl.semaphore_signal(
            barrier,
            inc=1,
            device_id=(row_at + a, col_at + b),
            device_id_type=pl.DeviceIdType.MESH,
        )

    def shared(o):
        oa, ob = unslot(o)
        found = []
        for v in range(9):
            va, vb = unslot(v)
            if v != o and abs(va - oa) <= 1 and abs(vb - ob) <= 1:
                found.append((v, (va - oa + 1) * 3 + vb - ob + 1))
        return found

    empty = jnp.zeros((128, 128), jnp.float32)
    f[...] = jnp.zeros(f.shape, jnp.float32)
    g[...] = jnp.zeros(g.shape, jnp.float32)
    fs[...] = jnp.zeros(fs.shape, jnp.float32)
    near[...] = jnp.zeros(near.shape, jnp.float32)
    for o in range(9):
        if o != 4:
            rx[o, 4] = empty
            for _, e in shared(o):
                rx[o, e] = empty
    for h in range(5, 9):
        fx[h - 5, 4] = empty
        for _, e in shared(h):
            fx[h - 5, e] = empty
    neighbours(greet)
    line = lax.broadcasted_iota(jnp.int32, (16, 256), 0)
    plain = jnp.where(
        line == 0,
        off_ref[0:1] + row_at.astype(jnp.float32),
        jnp.where(
            line == 1,
            off_ref[1:2] + col_at.astype(jnp.float32),
            jnp.where(line == 2, nug_ref[...], 0.0),
        ),
    )
    pick = lax.broadcasted_iota(jnp.int32, (256, 256), 0) == order_ref[...]
    pick = jnp.where(pick, 1.0, 0.0).astype(jnp.bfloat16)
    high = plain.astype(jnp.bfloat16)
    middle, low = split(plain - high.astype(jnp.float32))
    placed = mm(high, pick) + mm(middle, pick) + mm(low, pick)
    level = lax.broadcasted_iota(jnp.int32, (8, 128), 0)
    own = jnp.zeros((8, 128), jnp.float32)
    for n in range(6):
        half = slice(128 * (n % 2), 128 * (n % 2) + 128)
        own = jnp.where(level == n, placed[n // 2 : n // 2 + 1, half], own)
    pack_ref[0:128] = interp_ref[...]
    pack_ref[128:136] = own
    tall = 1 + lax.min(row_at, 1) + lax.min(row_count - 1 - row_at, 1)
    wide = 1 + lax.min(col_at, 1) + lax.min(col_count - 1 - col_at, 1)
    pl.semaphore_wait(barrier, tall * wide - 1)
    neighbours(lambda n, a, b: pack_copy(n, a, b).start())

    own_interp = split(pack_ref[0:128])
    my_colour = colour(0, 0)
    eye = lax.broadcasted_iota(jnp.int32, (128, 128), 0) == lax.broadcasted_iota(
        jnp.int32, (128, 128), 1
    )

    def start_block(source, here):
        where = source[128:136].T
        parts = []
        for s in range(2):
            line = []
            for t in range(2):
                gap_row = where[:, s : s + 1] - own[t : t + 1]
                gap_col = where[:, 2 + s : 3 + s] - own[2 + t : 3 + t]
                block = kappa(gap_row, gap_col)
                if here and s == t:
                    block = block + jnp.where(eye, own[4 + s : 5 + s], 0.0)
                line.append(block)
            parts.append(jnp.concatenate(line, axis=1))
        return parts[1] - dot3(split(source[0:128].T), split(parts[0]), NN)

    ea[4] = start_block(pack_ref, True)
    mat[...] = ea[4, :, 128:] - dot3(split(ea[4, :, :128]), own_interp, NN)
    neighbours(lambda n, a, b: pack_copy(8 - n, -a, -b).wait_recv())
    for o in range(9):
        if o != 4:
            ea[o] = jnp.where(inside(*unslot(o)), start_block(near.at[o], False), 0.0)

    def stage(k):
        @pl.when(my_colour == k)
        def _():
            tx[...] = factor128(mat[...])[1]
            neighbours(lambda n, a, b: k_copy(n, 4, a, b, True).start())

        def process(sources):
            for o in sources:
                oa, ob = unslot(o)
                if o != 4:
                    for v, e in shared(o):
                        va, vb = unslot(v)

                        @pl.when(inside(oa, ob) & inside(va, vb) & (colour(va, vb) < k))
                        def _():
                            k_copy(8 - o, e, -oa, -ob, False).wait_recv()

            for o in sources:
                total = ea[o]
                for v, e in shared(o):
                    value = g[e] if o == 4 else rx[o, e]
                    total = total - mm(cat_left(value), cat_right(f[v]))
                ea[o] = total
            for o in sources:
                oa, ob = unslot(o)
                if o != 4:

                    @pl.when(inside(oa, ob))
                    def _():
                        k_copy(8 - o, 4, -oa, -ob, False).wait_recv()

            for o in sources:
                factor = tx[...] if o == 4 else rx[o, 4]
                new = mm(cat_left(factor), cat_right(ea[o]))
                f[o] = new
                fs[o] = new[:, :128]
            if sources != [4]:

                @pl.when(my_colour > k)
                def _():
                    total = mat[...]
                    right = cat_right(pack_ref[0:128])
                    for o in sources:
                        new = f[o, :, 128:] - mm(cat_left(f[o, :, :128]), right)
                        flip = new.T
                        g[o] = flip
                        total = total - mm(cat_left(flip), cat_right(new))
                    mat[...] = total
                    for o in sources:
                        oa, ob = unslot(o)
                        for n in range(9):
                            a, b = unslot(n)
                            if n != 4 and abs(oa - a) <= 1 and abs(ob - b) <= 1:

                                @pl.when(inside(a, b) & inside(oa, ob))
                                def _():
                                    k_copy(n, o, a, b, False).start()

            for o in sources:
                oa, ob = unslot(o)
                for h in range(5, 9):
                    ha, hb = unslot(h)
                    if abs(oa + ha) <= 1 and abs(ob + hb) <= 1:

                        @pl.when(inside(-ha, -hb) & inside(oa, ob))
                        def _():
                            x_copy(h, o).start()

        for tall_odd in range(2):
            for wide_odd in range(2):
                sources = [
                    (a + 1) * 3 + b + 1
                    for a in ((-1, 1) if tall_odd else (0,))
                    for b in ((-1, 1) if wide_odd else (0,))
                ]

                @pl.when(((row_at + k // 2) % 2 == tall_odd) & ((col_at + k) % 2 == wide_odd))
                def _():
                    process(sources)

    loop(stage, 0, 4)

    for h in range(5, 9):
        ha, hb = unslot(h)
        for v in range(9):
            va, vb = unslot(v)
            if abs(va - ha) <= 1 and abs(vb - hb) <= 1:

                @pl.when(inside(ha, hb) & inside(va, vb))
                def _():
                    x_copy(h, (va - ha + 1) * 3 + vb - hb + 1).wait_recv()

    flips = [cat_left(fs[v].T) for v in range(9)]
    total = jnp.where(eye, own[4:5], 0.0)
    for v in range(9):
        total = total - mm(flips[v], cat_right(fs[v]))
    dd[0] = total
    for h in range(5, 9):
        ha, hb = unslot(h)
        total = empty
        for v in range(9):
            va, vb = unslot(v)
            if abs(va - ha) <= 1 and abs(vb - hb) <= 1:
                e = (va - ha + 1) * 3 + vb - hb + 1
                total = total - mm(flips[v], cat_right(fx[h - 5, e]))
        dd[h - 4] = total
        dd[h] = total.T

    lane = lax.broadcasted_iota(jnp.int32, (8, 128), 1)

    def gather(items):
        value = jnp.zeros((8, 128), jnp.float32)
        for source, start, place, size in items:
            moved = pltpu.roll(source, (place - start) % 128, 1)
            value = jnp.where((lane >= place) & (lane < place + size), moved, value)
        return value

    heads = [dd[n, 0:8] for n in range(9)]
    corner = [(heads[n], 0, 8 + 8 * n, 8) for n in range(9)]
    wide_rows = [
        gather([(heads[n], 16 * r, 16 + 16 * n, 16) for n in range(7)]) for r in range(8)
    ]
    more_rows = [
        gather(
            [(heads[7 + n], 16 * r, 16 * n, 16) for n in range(2)]
            + [(own, 16 * r, 32, 16), (own, 0, 56, 8)]
        )
        for r in range(8)
    ]
    corner = gather(corner)
    for c in range(16):
        rows = slice(8 * c, 8 * c + 8)
        group = [dd[n, rows] for n in range(9)]
        turn = group[1:]
        for bit in range(3):
            step = 1 << bit
            upper = ((lane // 16) // step) % 2 == 1
            for n in range(8):
                if n & step:
                    continue
                low, high = turn[n], turn[n + step]
                turn[n] = jnp.where(upper, pltpu.roll(high, 16 * step, 1), low)
                turn[n + step] = jnp.where(upper, high, pltpu.roll(low, 128 - 16 * step, 1))
        side = gather([(own, 8 * c, 48, 8)] + [(group[n], 0, 64 + 8 * n, 8) for n in range(8)])
        tail = jnp.where(lane < 8, group[8], corner)
        for r in range(8):
            dest = 16 * r + c
            out_ref[dest, 0] = turn[r]
            first = group[0] if r == 0 else pltpu.roll(group[0], 128 - 16 * r, 1)
            out_ref[dest, 1] = jnp.where(lane < 16, first, wide_rows[r])
            out_ref[dest, 2] = jnp.where((lane < 48) | ((lane >= 56) & (lane < 64)), more_rows[r], side)
            out_ref[dest, 3] = tail

    def finish(n, a, b):
        pack_copy(n, a, b).wait_send()

        def each(e):
            ea_, eb_ = unslot(e)
            is_sent = (e == 4) | (inside(ea_, eb_) & (colour(ea_, eb_) < my_colour))

            @pl.when(is_sent & near_pair(ea_ - a, eb_ - b))
            def _():
                k_copy(n, e, a, b, False).wait_send()

        loop(each)

    neighbours(finish)

    def finish_x(h):
        ha, hb = unslot(h)

        def each(o):
            oa, ob = unslot(o)

            @pl.when(inside(-ha, -hb) & inside(oa, ob) & near_pair(oa + ha, ob + hb))
            def _():
                x_copy(h, o).wait_send()

        loop(each)

    loop(finish_x, 5, 9)


def box_phase(off, order, nug, interp):
    block = (128, 128)
    return pl.pallas_call(
        box_kernel,
        out_shape=jax.ShapeDtypeStruct((128, 4, 8, 128), jnp.float32),
        in_specs=[pl.BlockSpec(memory_space=pltpu.VMEM)] * 4,
        out_specs=pl.BlockSpec(memory_space=pltpu.VMEM),
        scratch_shapes=[
            pltpu.VMEM((136, 128), jnp.float32),
            pltpu.VMEM((9, 136, 128), jnp.float32),
            pltpu.VMEM((9, 128, 256), jnp.float32),
            pltpu.VMEM((9, 128, 256), jnp.float32),
            pltpu.VMEM((9,) + block, jnp.float32),
            pltpu.VMEM((9,) + block, jnp.float32),
            pltpu.VMEM(block, jnp.float32),
            pltpu.VMEM((128, 256), jnp.float32),
            pltpu.VMEM(block, jnp.float32),
            pltpu.VMEM((9, 9) + block, jnp.float32),
            pltpu.VMEM((4, 9) + block, jnp.float32),
            pltpu.VMEM((9,) + block, jnp.float32),
            pltpu.SemaphoreType.DMA((9,)),
            pltpu.SemaphoreType.DMA((9,)),
            pltpu.SemaphoreType.DMA((9, 9)),
            pltpu.SemaphoreType.DMA((9, 9)),
            pltpu.SemaphoreType.DMA((4, 9)),
            pltpu.SemaphoreType.DMA((4, 9)),
        ],
        compiler_params=pltpu.CompilerParams(
            collective_id=0, has_side_effects=True, vmem_limit_bytes=40 * 2**20
        ),
    )(off, order, nug, interp)


def cat_right(x):
    hi, lo = split(x)
    return jnp.concatenate([hi, hi, lo], axis=0)


def cat_left(x):
    hi, lo = split(x)
    return jnp.concatenate([hi, lo, hi], axis=1)


def mm(a, b):
    return lax.dot_general(a, b, (NN, ((), ())), preferred_element_type=jnp.float32)


OFFSETS = [0, 1, 15, 16, 17, -1, -15, -16, -17]


def apart():
    return lax.broadcasted_iota(jnp.int32, (128, 128), 0) - lax.broadcasted_iota(
        jnp.int32, (128, 128), 1
    )


def root_block(row_x, row_y, col_x, col_y, lines):
    gap_x = row_x - col_x
    gap_y = row_y - col_y
    value = kappa(gap_x, gap_y)
    gap = apart()
    extra = jnp.zeros((128, 128), jnp.float32)
    for n in range(9):
        extra = jnp.where(gap == OFFSETS[n], lines[n], extra)
    return value + extra


def shifted_line(line, n):
    return pltpu.roll(line, -OFFSETS[n] % 128, 1) if n > 4 else line


def tail_kernel(
    at_ref,
    turned,
    lead_ref,
    rows_ref,
    out_ref,
    work,
    diag,
    wcur,
    left,
    right,
    wt,
    z_hi,
    z_lo,
    x_hi,
    x_lo,
    base,
    tab,
    table,
    sems,
):
    count = SB // 128
    width = 2 * SB
    chunk = 256
    row = lax.broadcasted_iota(jnp.int32, (128, SB), 0)
    col = lax.broadcasted_iota(jnp.int32, (128, SB), 1)

    def rows_of(i):
        return pl.ds(pl.multiple_of(i * 128, 128), 128)

    for l in range(8):
        for n in range(9):
            place = 64 + 8 * n
            line = turned[16 + l, place : place + 8] if n < 8 else turned[24 + l, 0:8]
            tab[0, l, n] = shifted_line(line, n)
            tab[1, l, n] = shifted_line(turned[24 + l, 8 + 8 * n : 16 + 8 * n], n)
            place = 16 * (n - 1)
            line = turned[l, place : place + 16] if n else turned[8 + l, 0:16]
            table[0, l, n] = shifted_line(line, n)
            place = 16 * n + 16
            if n < 7:
                line = turned[8 + l, place : place + 16]
            else:
                line = turned[16 + l, place - 128 : place - 112]
            table[1, l, n] = shifted_line(line, n)

    def piece(values, wide, which, k, l, token=0.0):
        place = 48 + 8 * which + l
        return root_block(
            wide[k, 0],
            wide[k, 1],
            turned[16, place : place + 1] + token,
            turned[18, place : place + 1],
            [values[which, l, n, pl.ds(k, 1)] for n in range(9)],
        )

    def assemble(k, _):
        for l in range(8):
            work[rows_of(k), SB + 128 * l : SB + 128 * l + 128] = piece(tab, lead_ref, 0, k, l)

            @pl.when(k <= l)
            def _():
                work[rows_of(k), 128 * l : 128 * l + 128] = piece(tab, lead_ref, 1, k, l)

            @pl.when(k > l)
            def _():
                work[rows_of(k), 128 * l : 128 * l + 128] = jnp.zeros((128, 128), jnp.float32)

        return 0

    lax.fori_loop(0, count, assemble, 0)
    work[SB:] = jnp.zeros((128, width + 128), jnp.float32)
    eye = jnp.where(apart() == 0, 1.0, 0.0)
    diag[...] = work[:128, :128]
    wcur[...] = jnp.zeros((128, 384), jnp.bfloat16)

    def build(k, l, token):
        cols = slice(128 * l, 128 * l + 128)
        hi, lo = split(piece(table, rows_ref, 1, k, l, token))
        x_hi[rows_of(k), cols] = hi
        x_lo[rows_of(k), cols] = lo
        base[rows_of(k), cols] = piece(table, rows_ref, 0, k, l, token)

    def scale(p):
        here = rows_of(p)
        spot = rows_of(jnp.where(p == count, 2 * count, p))
        work[:SB, spot] = jnp.zeros((SB, 128), jnp.float32)
        work[here, spot] = eye
        for c in range(width // chunk):
            cols = slice(c * chunk, c * chunk + chunk)
            new = mm(wcur[...], cat_right(work[here, cols]))
            work[here, cols] = new
            right[:, cols] = cat_right(new)
            for j in range(chunk // 128):
                n = c * (chunk // 128) + j
                if n < count:
                    part = jnp.where(p < n, new[:, 128 * j : 128 * j + 128], 0.0)
                    left[128 * n : 128 * n + 128] = cat_left(part.T)

    def step(i, _):
        p = jnp.where(i == 0, count, i - 1)
        scale(p)
        for c in range(width // chunk):
            cols = slice(c * chunk, c * chunk + chunk)
            work[:SB, cols] -= mm(left[...], right[:, cols])
        w = factor128(diag[...], lambda p, t: build(2 * i + p // 8, p % 8, t))[1]
        wcur[...] = cat_left(w)
        here, after = rows_of(i), rows_of(i + 1)
        u = mm(wcur[...], cat_right(work[here, after]))
        diag[...] = work[after, after] - mm(cat_left(u.T), cat_right(u))
        return 0

    lax.fori_loop(0, count, step, 0)
    last = rows_of(count - 1)
    work[last, SB - 128 : SB] = eye
    for c in range(width // chunk):
        cols = slice(c * chunk, c * chunk + chunk)
        work[last, cols] = mm(wcur[...], cat_right(work[last, cols]))

    def flip(i, _):
        here = rows_of(i)

        @pl.when(at_ref[1] == 0)
        def _():
            work[here, SB : 2 * SB] = jnp.where(col == row + 128 * i, -1.0, 0.0)

        hi, lo = split(work[here, SB : 2 * SB])
        right[0:128, :SB] = hi
        z_hi[here] = hi
        z_lo[here] = lo
        for j in range(count):
            hi, lo = split(jnp.where(j <= i, work[here, 128 * j : 128 * j + 128], 0.0).T)
            there = slice(128 * j, 128 * j + 128)
            wt[0, there, here] = hi
            wt[1, there, here] = lo
        return 0

    lax.fori_loop(0, count, flip, 0)
    for c in range(SB // chunk):
        cols = slice(c * chunk, c * chunk + chunk)
        y_hi, y_lo = z_hi[:, cols], z_lo[:, cols]
        for m in range(4):
            some = slice(m * 256, m * 256 + 256)
            deep = slice(m * 256, SB)
            w_hi, w_lo = wt[0, some, deep], wt[1, some, deep]
            work[some, cols] = (
                mm(w_hi, y_lo[m * 256 :]) + mm(w_lo, y_hi[m * 256 :]) + mm(w_hi, y_hi[m * 256 :])
            )
        for m in range(4):
            some = slice(m * 256, m * 256 + 256)
            hi, lo = split(work[some, cols])
            z_hi[some, cols] = hi
            z_lo[some, cols] = lo

    tall = 512

    def product(r, _):
        here = pl.ds(pl.multiple_of(r * tall, tall), tall)
        for c in range(SB // chunk):
            cols = slice(c * chunk, c * chunk + chunk)
            part = (
                mm(x_hi[here], z_lo[:, cols])
                + mm(x_lo[here], z_hi[:, cols])
                + mm(x_hi[here], z_hi[:, cols])
            )
            value = jnp.where(at_ref[1] == 0, 0.0, base[here, cols]) - part
            down = (at_ref[0] * 4 + r) * tall + lax.broadcasted_iota(jnp.int32, value.shape, 0)
            over = at_ref[1] * SB + c * chunk + lax.broadcasted_iota(jnp.int32, value.shape, 1)
            base[here, cols] = jnp.where((down < SB) & (over > down), 0.0, value)
        pltpu.make_async_copy(base.at[here], out_ref.at[here], sems.at[r]).start()
        return 0

    lax.fori_loop(0, 4, product, 0)
    for r in range(4):
        here = slice(r * tall, r * tall + tall)
        pltpu.make_async_copy(base.at[here], out_ref.at[here], sems.at[r]).wait()


def tail_solve(at, turned, lead, rows_wide):
    vmem = pl.BlockSpec(memory_space=pltpu.VMEM)
    return pl.pallas_call(
        tail_kernel,
        out_shape=jax.ShapeDtypeStruct((2048, SB), jnp.float32),
        in_specs=[pl.BlockSpec(memory_space=pltpu.SMEM), vmem, vmem, vmem],
        out_specs=pl.BlockSpec(memory_space=pl.ANY),
        scratch_shapes=[
            pltpu.VMEM((SB + 128, 2 * SB + 128), jnp.float32),
            pltpu.VMEM((128, 128), jnp.float32),
            pltpu.VMEM((128, 384), jnp.bfloat16),
            pltpu.VMEM((SB, 384), jnp.bfloat16),
            pltpu.VMEM((384, 2 * SB), jnp.bfloat16),
            pltpu.VMEM((2, SB, SB), jnp.bfloat16),
            pltpu.VMEM((SB, SB), jnp.bfloat16),
            pltpu.VMEM((SB, SB), jnp.bfloat16),
            pltpu.VMEM((2048, SB), jnp.bfloat16),
            pltpu.VMEM((2048, SB), jnp.bfloat16),
            pltpu.VMEM((2048, SB), jnp.float32),
            pltpu.VMEM((2, 8, 9, 8, 128), jnp.float32),
            pltpu.VMEM((2, 8, 9, 16, 128), jnp.float32),
            pltpu.SemaphoreType.DMA((4,)),
        ],
        compiler_params=pltpu.CompilerParams(vmem_limit_bytes=60 * 2**20),
    )(at, turned, lead, rows_wide)


def root_phase(outgoing, row_at, col_at):
    arrived = lax.all_to_all(
        outgoing.reshape(128, 32, 128), ("row", "col"), split_axis=0, concat_axis=0, tiled=True
    )
    turned = jnp.transpose(arrived, (1, 2, 0))

    def wide(start, size):
        part = jnp.stack([turned[16, start : start + size], turned[18, start : start + size]], axis=1)
        return jnp.broadcast_to(part[:, :, :, None], part.shape + (128,))

    return tail_solve(jnp.stack([row_at, col_at]), turned, wide(56, 8), wide(32, 16))


def on_device(offsets, point_order, nugget, interp):
    outgoing = box_phase(offsets[0, 0], point_order[0], nugget[0], interp[0, 0])
    return root_phase(outgoing, lax.axis_index("row"), lax.axis_index("col"))


def solution(mesh):
    in_specs = (
        P("row", "col", None, None),
        P("row", "col", None),
        P("row", "col", None),
        P("row", "col", None, None),
    )
    out_specs = P("row", "col")
    return jax.shard_map(
        on_device, mesh=mesh, in_specs=in_specs, out_specs=out_specs, check_vma=False
    )
```

```python
import jax
import jax.numpy as jnp
from jax import lax
from jax.experimental import pallas as pl
from jax.experimental.pallas import tpu as pltpu
from jax.sharding import PartitionSpec as P

SB = 1024


kernel_len = 0.5


def factor128(a, side=None):
    n = a.shape[0]
    G = n // 8
    rows = [a[8*g:8*g+8] for g in range(G)]
    lane = lax.broadcasted_iota(jnp.int32, (8, n), 1)
    sub = lax.broadcasted_iota(jnp.int32, (8, n), 0)
    w = [(lane == sub + 8*g).astype(jnp.float32) for g in range(G)]
    def srow(v, t):
        return jnp.broadcast_to(v[t:t+1], (8, n))
    def lcol(v, t):
        return jnp.broadcast_to(v[:, t:t+1], (8, n))
    us, ws = [], []
    for p in range(G):
        q, qw = rows[p], w[p]
        cols = [lcol(q, 8*p+t) for t in range(8)]
        u, uw, dv = q, qw, None
        for t in range(8):
            pr, pw = srow(q, t), srow(qw, t)
            d = srow(cols[t], t)
            here = sub == t
            u = pr if t == 0 else jnp.where(here, pr, u)
            uw = pw if t == 0 else jnp.where(here, pw, uw)
            dv = d if t == 0 else jnp.where(here, d, dv)
            m = jnp.where(here, 0.0, cols[t]) * (1.0 / d)
            q = q - m * pr
            qw = qw - m * pw
            for v in range(t + 1, 8):
                cols[v] = cols[v] - m * srow(cols[v], t)
        if side is not None:
            side(p, jnp.minimum(jnp.abs(dv[0:1]), 0.0))
        r = lax.rsqrt(dv)
        us.append(jnp.where(lane >= sub + 8*p, u * r, 0.0))
        ws.append(uw * r)
        inv = 1.0 / dv
        z, zw = q * inv, qw * inv
        zs = [srow(z, t) for t in range(8)]
        zws = [srow(zw, t) for t in range(8)]
        for g in range(p + 1, G):
            cg = [lcol(rows[g], 8*p+t) for t in range(8)]
            x = [cg[t] * zs[t] for t in range(8)]
            y = [cg[t] * zws[t] for t in range(8)]
            rows[g] = rows[g] - (((x[0]+x[1])+(x[2]+x[3]))+((x[4]+x[5])+(x[6]+x[7])))
            w[g] = w[g] - (((y[0]+y[1])+(y[2]+y[3]))+((y[4]+y[5])+(y[6]+y[7])))
    return jnp.concatenate(us, 0), jnp.concatenate(ws, 0)


def kappa(gap_x, gap_y):
    square = gap_x * gap_x + gap_y * gap_y
    distance = square * lax.rsqrt(jnp.maximum(square, 1e-36))
    return jnp.exp2(distance * (-1.4426950408889634 / kernel_len) - 6.0)


def split(x):
    hi = x.astype(jnp.bfloat16)
    return hi, (x - hi.astype(jnp.float32)).astype(jnp.bfloat16)


def dot3(a, b, dims):
    def one(x, y):
        return lax.dot_general(x, y, (dims, ((), ())), preferred_element_type=jnp.float32)

    return one(a[0], b[1]) + one(a[1], b[0]) + one(a[0], b[0])


NN = ((1,), (0,))
TN = ((0,), (0,))
NT = ((1,), (1,))


def box_kernel(off_ref, order_ref, nug_ref, interp_ref, out_ref, pack_ref, upper, near, ea, f, fs, g, mat, acc, tx, rx, fx, dd, ps, pr, ks, kr, xs, xr):
    row_at = lax.axis_index("row")
    col_at = lax.axis_index("col")
    row_count = lax.axis_size("row")
    col_count = lax.axis_size("col")

    def inside(a, b):
        r, c = row_at + a, col_at + b
        return (r >= 0) & (r < row_count) & (c >= 0) & (c < col_count)

    def colour(a, b):
        return 2 * ((row_at + a + 2) % 2) + (col_at + b + 2) % 2

    def unslot(n):
        return n // 3 - 1, n % 3 - 1

    def near_pair(a, b):
        return (a >= -1) & (a <= 1) & (b >= -1) & (b <= 1)

    def loop(body, low=0, high=9):
        def step(n, _):
            body(n)
            return 0

        lax.fori_loop(low, high, step, 0)

    def copy(src, dst, send, recv, a, b):
        return pltpu.make_async_remote_copy(
            src_ref=src,
            dst_ref=dst,
            send_sem=send,
            recv_sem=recv,
            device_id=(row_at + a, col_at + b),
            device_id_type=pl.DeviceIdType.MESH,
        )

    def neighbours(body):
        def each(n):
            a, b = unslot(n)

            @pl.when((n != 4) & inside(a, b))
            def _():
                body(n, a, b)

        loop(each)

    def place_copy(n, a, b):
        part = pl.ds(128, 8)
        return copy(
            pack_ref.at[part], near.at[8 - n, part], ps.at[0, n], pr.at[0, 8 - n], a, b
        )

    def interp_copy(n, a, b):
        part = pl.ds(0, 128)
        return copy(interp_ref, near.at[8 - n, part], ps.at[1, n], pr.at[1, 8 - n], a, b)

    def k_copy(n, e, a, b, inverse):
        source = tx if inverse else g.at[e]
        return copy(source, rx.at[8 - n, e], ks.at[n, e], kr.at[8 - n, e], a, b)

    def x_copy(h, o):
        a, b = unslot(h)
        return copy(fs.at[o], fx.at[h - 5, o], xs.at[h - 5, o], xr.at[h - 5, o], -a, -b)

    barrier = pltpu.get_barrier_semaphore()

    def greet(n, a, b):
        pl.semaphore_signal(
            barrier,
            inc=1,
            device_id=(row_at + a, col_at + b),
            device_id_type=pl.DeviceIdType.MESH,
        )

    def shared(o):
        oa, ob = unslot(o)
        found = []
        for v in range(9):
            va, vb = unslot(v)
            if v != o and abs(va - oa) <= 1 and abs(vb - ob) <= 1:
                found.append((v, (va - oa + 1) * 3 + vb - ob + 1))
        return found

    empty = jnp.zeros((128, 128), jnp.float32)
    f[...] = jnp.zeros(f.shape, jnp.float32)
    g[...] = jnp.zeros(g.shape, jnp.float32)
    fs[...] = jnp.zeros(fs.shape, jnp.float32)
    near[...] = jnp.zeros(near.shape, jnp.float32)
    for o in range(9):
        if o != 4:
            rx[o, 4] = empty
            for _, e in shared(o):
                rx[o, e] = empty
    for h in range(5, 9):
        fx[h - 5, 4] = empty
        for _, e in shared(h):
            fx[h - 5, e] = empty
    neighbours(greet)
    line = lax.broadcasted_iota(jnp.int32, (16, 256), 0)
    plain = jnp.where(
        line == 0,
        off_ref[0:1] + row_at.astype(jnp.float32),
        jnp.where(
            line == 1,
            off_ref[1:2] + col_at.astype(jnp.float32),
            jnp.where(line == 2, nug_ref[...], 0.0),
        ),
    )
    pick = lax.broadcasted_iota(jnp.int32, (256, 256), 0) == order_ref[...]
    pick = jnp.where(pick, 1.0, 0.0).astype(jnp.bfloat16)
    high = plain.astype(jnp.bfloat16)
    middle, low = split(plain - high.astype(jnp.float32))
    placed = mm(high, pick) + mm(middle, pick) + mm(low, pick)
    level = lax.broadcasted_iota(jnp.int32, (8, 128), 0)
    own = jnp.zeros((8, 128), jnp.float32)
    for n in range(6):
        half = slice(128 * (n % 2), 128 * (n % 2) + 128)
        own = jnp.where(level == n, placed[n // 2 : n // 2 + 1, half], own)
    pack_ref[0:128] = interp_ref[...]
    pack_ref[128:136] = own
    tall = 1 + lax.min(row_at, 1) + lax.min(row_count - 1 - row_at, 1)
    wide = 1 + lax.min(col_at, 1) + lax.min(col_count - 1 - col_at, 1)
    pl.semaphore_wait(barrier, tall * wide - 1)
    neighbours(lambda n, a, b: place_copy(n, a, b).start())
    neighbours(lambda n, a, b: interp_copy(n, a, b).start())

    own_interp = split(pack_ref[0:128])
    my_colour = colour(0, 0)
    eye = lax.broadcasted_iota(jnp.int32, (128, 128), 0) == lax.broadcasted_iota(
        jnp.int32, (128, 128), 1
    )

    def start_block(source, here):
        where = source[128:136].T
        parts = []
        for s in range(2):
            line = []
            for t in range(2):
                gap_row = where[:, s : s + 1] - own[t : t + 1]
                gap_col = where[:, 2 + s : 3 + s] - own[2 + t : 3 + t]
                block = kappa(gap_row, gap_col)
                if here and s == t:
                    block = block + jnp.where(eye, own[4 + s : 5 + s], 0.0)
                line.append(block)
            parts.append(jnp.concatenate(line, axis=1))
        return parts

    def reduce_rows(upper, lower, source):
        return lower - mm(cat_left(source[0:128].T), cat_right(upper))

    ea[4] = reduce_rows(*start_block(pack_ref, True), pack_ref)
    mat[...] = ea[4, :, 128:] - dot3(split(ea[4, :, :128]), own_interp, NN)

    @pl.when(my_colour == 0)
    def _():
        tx[...] = factor128(mat[...])[1]
        neighbours(lambda n, a, b: k_copy(n, 4, a, b, True).start())

    neighbours(lambda n, a, b: place_copy(8 - n, -a, -b).wait_recv())
    for o in range(9):
        if o != 4:
            upper[o], ea[o] = start_block(near.at[o], False)
    neighbours(lambda n, a, b: interp_copy(8 - n, -a, -b).wait_recv())
    for o in range(9):
        if o != 4:
            value = reduce_rows(upper[o], ea[o], near.at[o])
            ea[o] = jnp.where(inside(*unslot(o)), value, 0.0)

    def stage(k):
        @pl.when((my_colour == k) & (k > 0))
        def _():
            tx[...] = factor128(mat[...])[1]
            neighbours(lambda n, a, b: k_copy(n, 4, a, b, True).start())

        def process(sources):
            for o in sources:
                oa, ob = unslot(o)
                if o != 4:
                    for v, e in shared(o):
                        va, vb = unslot(v)

                        @pl.when(inside(oa, ob) & inside(va, vb) & (colour(va, vb) < k))
                        def _():
                            k_copy(8 - o, e, -oa, -ob, False).wait_recv()

            for o in sources:
                total = ea[o]
                for v, e in shared(o):
                    value = g[e] if o == 4 else rx[o, e]
                    total = total - mm(cat_left(value), cat_right(f[v]))
                ea[o] = total
            for o in sources:
                oa, ob = unslot(o)
                if o != 4:

                    @pl.when(inside(oa, ob))
                    def _():
                        k_copy(8 - o, 4, -oa, -ob, False).wait_recv()

            for o in sources:
                factor = tx[...] if o == 4 else rx[o, 4]
                new = mm(cat_left(factor), cat_right(ea[o]))
                f[o] = new
                fs[o] = new[:, :128]
            if sources != [4]:

                @pl.when(my_colour > k)
                def _():
                    total = mat[...]
                    right = cat_right(pack_ref[0:128])
                    for o in sources:
                        new = f[o, :, 128:] - mm(cat_left(f[o, :, :128]), right)
                        flip = new.T
                        g[o] = flip
                        total = total - mm(cat_left(flip), cat_right(new))
                    mat[...] = total
                    for o in sources:
                        oa, ob = unslot(o)
                        for n in range(9):
                            a, b = unslot(n)
                            if n != 4 and abs(oa - a) <= 1 and abs(ob - b) <= 1:

                                @pl.when(inside(a, b) & inside(oa, ob))
                                def _():
                                    k_copy(n, o, a, b, False).start()

            for o in sources:
                oa, ob = unslot(o)
                for h in range(5, 9):
                    ha, hb = unslot(h)
                    if abs(oa + ha) <= 1 and abs(ob + hb) <= 1:

                        @pl.when(inside(-ha, -hb) & inside(oa, ob))
                        def _():
                            x_copy(h, o).start()

        for tall_odd in range(2):
            for wide_odd in range(2):
                sources = [
                    (a + 1) * 3 + b + 1
                    for a in ((-1, 1) if tall_odd else (0,))
                    for b in ((-1, 1) if wide_odd else (0,))
                ]

                @pl.when(((row_at + k // 2) % 2 == tall_odd) & ((col_at + k) % 2 == wide_odd))
                def _():
                    process(sources)

    loop(stage, 0, 4)

    for h in range(5, 9):
        ha, hb = unslot(h)
        for v in range(9):
            va, vb = unslot(v)
            if abs(va - ha) <= 1 and abs(vb - hb) <= 1:

                @pl.when(inside(ha, hb) & inside(va, vb))
                def _():
                    x_copy(h, (va - ha + 1) * 3 + vb - hb + 1).wait_recv()

    flips = [cat_left(fs[v].T) for v in range(9)]
    total = jnp.where(eye, own[4:5], 0.0)
    for v in range(9):
        total = total - mm(flips[v], cat_right(fs[v]))
    dd[0] = total
    for h in range(5, 9):
        ha, hb = unslot(h)
        total = empty
        for v in range(9):
            va, vb = unslot(v)
            if abs(va - ha) <= 1 and abs(vb - hb) <= 1:
                e = (va - ha + 1) * 3 + vb - hb + 1
                total = total - mm(flips[v], cat_right(fx[h - 5, e]))
        dd[h - 4] = total
        dd[h] = total.T

    lane = lax.broadcasted_iota(jnp.int32, (8, 128), 1)

    def gather(items):
        value = jnp.zeros((8, 128), jnp.float32)
        for source, start, place, size in items:
            moved = pltpu.roll(source, (place - start) % 128, 1)
            value = jnp.where((lane >= place) & (lane < place + size), moved, value)
        return value

    heads = [dd[n, 0:8] for n in range(9)]
    corner = [(heads[n], 0, 8 + 8 * n, 8) for n in range(9)]
    wide_rows = [
        gather([(heads[n], 16 * r, 16 + 16 * n, 16) for n in range(7)]) for r in range(8)
    ]
    more_rows = [
        gather(
            [(heads[7 + n], 16 * r, 16 * n, 16) for n in range(2)]
            + [(own, 16 * r, 32, 16), (own, 0, 56, 8)]
        )
        for r in range(8)
    ]
    corner = gather(corner)
    for c in range(16):
        rows = slice(8 * c, 8 * c + 8)
        group = [dd[n, rows] for n in range(9)]
        turn = group[1:]
        for bit in range(3):
            step = 1 << bit
            upper = ((lane // 16) // step) % 2 == 1
            for n in range(8):
                if n & step:
                    continue
                low, high = turn[n], turn[n + step]
                turn[n] = jnp.where(upper, pltpu.roll(high, 16 * step, 1), low)
                turn[n + step] = jnp.where(upper, high, pltpu.roll(low, 128 - 16 * step, 1))
        side = gather([(own, 8 * c, 48, 8)] + [(group[n], 0, 64 + 8 * n, 8) for n in range(8)])
        tail = jnp.where(lane < 8, group[8], corner)
        for r in range(8):
            dest = 16 * r + c
            out_ref[dest, 0] = turn[r]
            first = group[0] if r == 0 else pltpu.roll(group[0], 128 - 16 * r, 1)
            out_ref[dest, 1] = jnp.where(lane < 16, first, wide_rows[r])
            out_ref[dest, 2] = jnp.where((lane < 48) | ((lane >= 56) & (lane < 64)), more_rows[r], side)
            out_ref[dest, 3] = tail

    def finish(n, a, b):
        place_copy(n, a, b).wait_send()
        interp_copy(n, a, b).wait_send()

        def each(e):
            ea_, eb_ = unslot(e)
            is_sent = (e == 4) | (inside(ea_, eb_) & (colour(ea_, eb_) < my_colour))

            @pl.when(is_sent & near_pair(ea_ - a, eb_ - b))
            def _():
                k_copy(n, e, a, b, False).wait_send()

        loop(each)

    neighbours(finish)

    def finish_x(h):
        ha, hb = unslot(h)

        def each(o):
            oa, ob = unslot(o)

            @pl.when(inside(-ha, -hb) & inside(oa, ob) & near_pair(oa + ha, ob + hb))
            def _():
                x_copy(h, o).wait_send()

        loop(each)

    loop(finish_x, 5, 9)


def box_phase(off, order, nug, interp):
    block = (128, 128)
    return pl.pallas_call(
        box_kernel,
        out_shape=jax.ShapeDtypeStruct((128, 4, 8, 128), jnp.float32),
        in_specs=[pl.BlockSpec(memory_space=pltpu.VMEM)] * 4,
        out_specs=pl.BlockSpec(memory_space=pltpu.VMEM),
        scratch_shapes=[
            pltpu.VMEM((136, 128), jnp.float32),
            pltpu.VMEM((9, 128, 256), jnp.float32),
            pltpu.VMEM((9, 136, 128), jnp.float32),
            pltpu.VMEM((9, 128, 256), jnp.float32),
            pltpu.VMEM((9, 128, 256), jnp.float32),
            pltpu.VMEM((9,) + block, jnp.float32),
            pltpu.VMEM((9,) + block, jnp.float32),
            pltpu.VMEM(block, jnp.float32),
            pltpu.VMEM((128, 256), jnp.float32),
            pltpu.VMEM(block, jnp.float32),
            pltpu.VMEM((9, 9) + block, jnp.float32),
            pltpu.VMEM((4, 9) + block, jnp.float32),
            pltpu.VMEM((9,) + block, jnp.float32),
            pltpu.SemaphoreType.DMA((2, 9)),
            pltpu.SemaphoreType.DMA((2, 9)),
            pltpu.SemaphoreType.DMA((9, 9)),
            pltpu.SemaphoreType.DMA((9, 9)),
            pltpu.SemaphoreType.DMA((4, 9)),
            pltpu.SemaphoreType.DMA((4, 9)),
        ],
        compiler_params=pltpu.CompilerParams(
            collective_id=0, has_side_effects=True, vmem_limit_bytes=40 * 2**20
        ),
    )(off, order, nug, interp)


def cat_right(x):
    hi, lo = split(x)
    return jnp.concatenate([hi, hi, lo], axis=0)


def cat_left(x):
    hi, lo = split(x)
    return jnp.concatenate([hi, lo, hi], axis=1)


def mm(a, b):
    return lax.dot_general(a, b, (NN, ((), ())), preferred_element_type=jnp.float32)


OFFSETS = [0, 1, 15, 16, 17, -1, -15, -16, -17]


def apart():
    return lax.broadcasted_iota(jnp.int32, (128, 128), 0) - lax.broadcasted_iota(
        jnp.int32, (128, 128), 1
    )


def root_block(row_x, row_y, col_x, col_y, lines):
    gap_x = row_x - col_x
    gap_y = row_y - col_y
    value = kappa(gap_x, gap_y)
    gap = apart()
    extra = jnp.zeros((128, 128), jnp.float32)
    for n in range(9):
        extra = jnp.where(gap == OFFSETS[n], lines[n], extra)
    return value + extra


def shifted_line(line, n):
    return pltpu.roll(line, -OFFSETS[n] % 128, 1) if n > 4 else line


def tail_kernel(
    at_ref,
    turned,
    out_ref,
    lead_ref,
    rows_ref,
    work,
    diag,
    wcur,
    left,
    right,
    wt,
    z_hi,
    z_lo,
    x_hi,
    x_lo,
    base,
    tab,
    table,
    sems,
):
    count = SB // 128
    width = 2 * SB
    chunk = 256
    row = lax.broadcasted_iota(jnp.int32, (128, SB), 0)
    col = lax.broadcasted_iota(jnp.int32, (128, SB), 1)

    def rows_of(i):
        return pl.ds(pl.multiple_of(i * 128, 128), 128)

    for l in range(8):
        for n in range(9):
            place = 64 + 8 * n
            line = turned[16 + l, place : place + 8] if n < 8 else turned[24 + l, 0:8]
            tab[0, l, n] = shifted_line(line, n)
            tab[1, l, n] = shifted_line(turned[24 + l, 8 + 8 * n : 16 + 8 * n], n)
            place = 16 * (n - 1)
            line = turned[l, place : place + 16] if n else turned[8 + l, 0:16]
            table[0, l, n] = shifted_line(line, n)
            place = 16 * n + 16
            if n < 7:
                line = turned[8 + l, place : place + 16]
            else:
                line = turned[16 + l, place - 128 : place - 112]
            table[1, l, n] = shifted_line(line, n)

    def piece(values, wide, which, k, l, token=0.0):
        place = 48 + 8 * which + l
        return root_block(
            wide[k, 0],
            wide[k, 1],
            turned[16, place : place + 1] + token,
            turned[18, place : place + 1],
            [values[which, l, n, pl.ds(k, 1)] for n in range(9)],
        )

    xs = turned[16, 32:64].T
    ys = turned[18, 32:64].T
    for k in range(16):
        rows_ref[k, 0] = jnp.broadcast_to(xs[:, k : k + 1], (128, 128))
        rows_ref[k, 1] = jnp.broadcast_to(ys[:, k : k + 1], (128, 128))
    for k in range(8):
        lead_ref[k, 0] = jnp.broadcast_to(xs[:, 24 + k : 25 + k], (128, 128))
        lead_ref[k, 1] = jnp.broadcast_to(ys[:, 24 + k : 25 + k], (128, 128))

    def assemble(k, _):
        for l in range(8):
            work[rows_of(k), SB + 128 * l : SB + 128 * l + 128] = piece(tab, lead_ref, 0, k, l)

            @pl.when(k <= l)
            def _():
                work[rows_of(k), 128 * l : 128 * l + 128] = piece(tab, lead_ref, 1, k, l)

            @pl.when(k > l)
            def _():
                work[rows_of(k), 128 * l : 128 * l + 128] = jnp.zeros((128, 128), jnp.float32)

        return 0

    lax.fori_loop(0, count, assemble, 0)
    work[SB:] = jnp.zeros((128, width + 128), jnp.float32)
    eye = jnp.where(apart() == 0, 1.0, 0.0)
    diag[...] = work[:128, :128]
    wcur[...] = jnp.zeros((128, 384), jnp.bfloat16)

    def build(k, l, token):
        cols = slice(128 * l, 128 * l + 128)
        hi, lo = split(piece(table, rows_ref, 1, k, l, token))
        x_hi[rows_of(k), cols] = hi
        x_lo[rows_of(k), cols] = lo
        base[rows_of(k), cols] = piece(table, rows_ref, 0, k, l, token)

    def scale(p):
        here = rows_of(p)
        spot = rows_of(jnp.where(p == count, 2 * count, p))
        work[:SB, spot] = jnp.zeros((SB, 128), jnp.float32)
        work[here, spot] = eye
        for c in range(width // chunk):
            cols = slice(c * chunk, c * chunk + chunk)
            new = mm(wcur[...], cat_right(work[here, cols]))
            work[here, cols] = new
            right[:, cols] = cat_right(new)
            for j in range(chunk // 128):
                n = c * (chunk // 128) + j
                if n < count:
                    flip = new[:, 128 * j : 128 * j + 128].T
                    there = slice(128 * n, 128 * n + 128)
                    left[there] = cat_left(jnp.where(p < n, flip, 0.0))
                    hi, lo = split(jnp.where(p < n, 0.0, flip))
                    wt[0, there, here] = hi
                    wt[1, there, here] = lo
            if c * chunk >= SB:
                hi, lo = split(new)
                z_hi[here, c * chunk - SB : c * chunk - SB + chunk] = hi
                z_lo[here, c * chunk - SB : c * chunk - SB + chunk] = lo

    def step(i, _):
        p = jnp.where(i == 0, count, i - 1)
        scale(p)
        for c in range(width // chunk):
            cols = slice(c * chunk, c * chunk + chunk)
            work[:SB, cols] -= mm(left[...], right[:, cols])
        w = factor128(diag[...], lambda p, t: build(2 * i + p // 8, p % 8, t))[1]
        wcur[...] = cat_left(w)
        here, after = rows_of(i), rows_of(i + 1)
        u = mm(wcur[...], cat_right(work[here, after]))
        diag[...] = work[after, after] - mm(cat_left(u.T), cat_right(u))
        return 0

    lax.fori_loop(0, count, step, 0)
    scale(count - 1)

    @pl.when(at_ref[1] == 0)
    def _():
        for i in range(count):
            here = slice(128 * i, 128 * i + 128)
            z_hi[here] = jnp.where(col == row + 128 * i, -1.0, 0.0).astype(jnp.bfloat16)
            z_lo[here] = jnp.zeros((128, SB), jnp.bfloat16)

    for c in range(SB // chunk):
        cols = slice(c * chunk, c * chunk + chunk)
        y_hi, y_lo = z_hi[:SB, cols], z_lo[:SB, cols]
        for m in range(4):
            some = slice(m * 256, m * 256 + 256)
            deep = slice(m * 256, SB)
            w_hi, w_lo = wt[0, some, deep], wt[1, some, deep]
            work[some, cols] = (
                mm(w_hi, y_lo[m * 256 :]) + mm(w_lo, y_hi[m * 256 :]) + mm(w_hi, y_hi[m * 256 :])
            )
        for m in range(4):
            some = slice(m * 256, m * 256 + 256)
            hi, lo = split(work[some, cols])
            z_hi[some, cols] = hi
            z_lo[some, cols] = lo

    tall = 512

    def product(r, _):
        here = pl.ds(pl.multiple_of(r * tall, tall), tall)
        for c in range(SB // chunk):
            cols = slice(c * chunk, c * chunk + chunk)
            part = (
                mm(x_hi[here], z_lo[:SB, cols])
                + mm(x_lo[here], z_hi[:SB, cols])
                + mm(x_hi[here], z_hi[:SB, cols])
            )
            value = jnp.where(at_ref[1] == 0, 0.0, base[here, cols]) - part
            down = (at_ref[0] * 4 + r) * tall + lax.broadcasted_iota(jnp.int32, value.shape, 0)
            over = at_ref[1] * SB + c * chunk + lax.broadcasted_iota(jnp.int32, value.shape, 1)
            base[here, cols] = jnp.where((down < SB) & (over > down), 0.0, value)
        pltpu.make_async_copy(base.at[here], out_ref.at[here], sems.at[r]).start()
        return 0

    lax.fori_loop(0, 4, product, 0)
    for r in range(4):
        here = slice(r * tall, r * tall + tall)
        pltpu.make_async_copy(base.at[here], out_ref.at[here], sems.at[r]).wait()


def tail_solve(at, turned):
    vmem = pl.BlockSpec(memory_space=pltpu.VMEM)
    return pl.pallas_call(
        tail_kernel,
        out_shape=jax.ShapeDtypeStruct((2048, SB), jnp.float32),
        in_specs=[pl.BlockSpec(memory_space=pltpu.SMEM), vmem],
        out_specs=pl.BlockSpec(memory_space=pl.ANY),
        scratch_shapes=[
            pltpu.VMEM((8, 2, 128, 128), jnp.float32),
            pltpu.VMEM((16, 2, 128, 128), jnp.float32),
            pltpu.VMEM((SB + 128, 2 * SB + 128), jnp.float32),
            pltpu.VMEM((128, 128), jnp.float32),
            pltpu.VMEM((128, 384), jnp.bfloat16),
            pltpu.VMEM((SB, 384), jnp.bfloat16),
            pltpu.VMEM((384, 2 * SB), jnp.bfloat16),
            pltpu.VMEM((2, SB, SB + 128), jnp.bfloat16),
            pltpu.VMEM((SB + 128, SB), jnp.bfloat16),
            pltpu.VMEM((SB + 128, SB), jnp.bfloat16),
            pltpu.VMEM((2048, SB), jnp.bfloat16),
            pltpu.VMEM((2048, SB), jnp.bfloat16),
            pltpu.VMEM((2048, SB), jnp.float32),
            pltpu.VMEM((2, 8, 9, 8, 128), jnp.float32),
            pltpu.VMEM((2, 8, 9, 16, 128), jnp.float32),
            pltpu.SemaphoreType.DMA((4,)),
        ],
        compiler_params=pltpu.CompilerParams(vmem_limit_bytes=60 * 2**20),
    )(at, turned)


def root_phase(outgoing, row_at, col_at):
    arrived = lax.all_to_all(
        outgoing.reshape(128, 32, 128), ("row", "col"), split_axis=0, concat_axis=0, tiled=True
    )
    turned = jnp.transpose(arrived, (1, 2, 0))

    return tail_solve(jnp.stack([row_at, col_at]), turned)


def on_device(offsets, point_order, nugget, interp):
    outgoing = box_phase(offsets[0, 0], point_order[0], nugget[0], interp[0, 0])
    return root_phase(outgoing, lax.axis_index("row"), lax.axis_index("col"))


def solution(mesh):
    in_specs = (
        P("row", "col", None, None),
        P("row", "col", None),
        P("row", "col", None),
        P("row", "col", None, None),
    )
    out_specs = P("row", "col")
    return jax.shard_map(
        on_device, mesh=mesh, in_specs=in_specs, out_specs=out_specs, check_vma=False
    )
```

```python
import jax
import jax.numpy as jnp
from jax import lax
from jax.experimental import pallas as pl
from jax.experimental.pallas import tpu as pltpu
from jax.sharding import PartitionSpec as P

SB = 1024


kernel_len = 0.5


def factor128(a, side=None):
    n = a.shape[0]
    G = n // 8
    rows = [a[8*g:8*g+8] for g in range(G)]
    lane = lax.broadcasted_iota(jnp.int32, (8, n), 1)
    sub = lax.broadcasted_iota(jnp.int32, (8, n), 0)
    w = [(lane == sub + 8*g).astype(jnp.float32) for g in range(G)]
    def srow(v, t):
        return jnp.broadcast_to(v[t:t+1], (8, n))
    def lcol(v, t):
        return jnp.broadcast_to(v[:, t:t+1], (8, n))
    us, ws = [], []
    for p in range(G):
        q, qw = rows[p], w[p]
        cols = [lcol(q, 8*p+t) for t in range(8)]
        first = jnp.where(sub == 8, q, srow(q, 0))
        tops = [lcol(first, 8*p+t) for t in range(8)]
        u, uw, dv = q, qw, None
        for t in range(8):
            pr, pw = srow(q, t), srow(qw, t)
            d = tops[0] if t == 0 else srow(cols[t], t)
            here = sub == t
            u = pr if t == 0 else jnp.where(here, pr, u)
            uw = pw if t == 0 else jnp.where(here, pw, uw)
            dv = d if t == 0 else jnp.where(here, d, dv)
            m = jnp.where(here, 0.0, cols[t]) * (1.0 / d)
            q = q - m * pr
            qw = qw - m * pw
            for v in range(t + 1, 8):
                cols[v] = cols[v] - m * (tops[v] if t == 0 else srow(cols[v], t))
        if side is not None:
            side(p, jnp.minimum(jnp.abs(dv[0:1]), 0.0))
        r = lax.rsqrt(dv)
        us.append(jnp.where(lane >= sub + 8*p, u * r, 0.0))
        ws.append(uw * r)
        inv = 1.0 / dv
        z, zw = q * inv, qw * inv
        zs = [srow(z, t) for t in range(8)]
        zws = [srow(zw, t) for t in range(8)]
        for g in range(p + 1, G):
            cg = [lcol(rows[g], 8*p+t) for t in range(8)]
            x = [cg[t] * zs[t] for t in range(8)]
            y = [cg[t] * zws[t] for t in range(8)]
            rows[g] = rows[g] - (((x[0]+x[1])+(x[2]+x[3]))+((x[4]+x[5])+(x[6]+x[7])))
            w[g] = w[g] - (((y[0]+y[1])+(y[2]+y[3]))+((y[4]+y[5])+(y[6]+y[7])))
    return jnp.concatenate(us, 0), jnp.concatenate(ws, 0)


def kappa(gap_x, gap_y):
    square = gap_x * gap_x + gap_y * gap_y
    distance = square * lax.rsqrt(jnp.maximum(square, 1e-36))
    return jnp.exp2(distance * (-1.4426950408889634 / kernel_len) - 6.0)


def split(x):
    hi = x.astype(jnp.bfloat16)
    return hi, (x - hi.astype(jnp.float32)).astype(jnp.bfloat16)


def dot3(a, b, dims):
    def one(x, y):
        return lax.dot_general(x, y, (dims, ((), ())), preferred_element_type=jnp.float32)

    return one(a[0], b[1]) + one(a[1], b[0]) + one(a[0], b[0])


NN = ((1,), (0,))
TN = ((0,), (0,))
NT = ((1,), (1,))


def box_kernel(
    off_in, order_in, nug_in, interp_in, out_ref, off_ref, order_ref, nug_ref, interp_ref, arrive_sem, pack_ref, upper, near, ea, f, fs, g, mat, acc, tx, rx, fx, dd, ps, pr, ks, kr, xs, xr):
    row_at = lax.axis_index("row")
    col_at = lax.axis_index("col")
    row_count = lax.axis_size("row")
    col_count = lax.axis_size("col")

    def inside(a, b):
        r, c = row_at + a, col_at + b
        return (r >= 0) & (r < row_count) & (c >= 0) & (c < col_count)

    def colour(a, b):
        return 2 * ((row_at + a + 2) % 2) + (col_at + b + 2) % 2

    def unslot(n):
        return n // 3 - 1, n % 3 - 1

    def near_pair(a, b):
        return (a >= -1) & (a <= 1) & (b >= -1) & (b <= 1)

    def loop(body, low=0, high=9):
        def step(n, _):
            body(n)
            return 0

        lax.fori_loop(low, high, step, 0)

    def copy(src, dst, send, recv, a, b):
        return pltpu.make_async_remote_copy(
            src_ref=src,
            dst_ref=dst,
            send_sem=send,
            recv_sem=recv,
            device_id=(row_at + a, col_at + b),
            device_id_type=pl.DeviceIdType.MESH,
        )

    def neighbours(body):
        def each(n):
            a, b = unslot(n)

            @pl.when((n != 4) & inside(a, b))
            def _():
                body(n, a, b)

        loop(each)

    def place_copy(n, a, b):
        part = pl.ds(128, 8)
        return copy(
            pack_ref.at[part], near.at[8 - n, part], ps.at[0, n], pr.at[0, 8 - n], a, b
        )

    def interp_copy(n, a, b):
        part = pl.ds(0, 128)
        return copy(interp_ref, near.at[8 - n, part], ps.at[1, n], pr.at[1, 8 - n], a, b)

    def k_copy(n, e, a, b, inverse):
        source = tx if inverse else g.at[e]
        return copy(source, rx.at[8 - n, e], ks.at[n, e], kr.at[8 - n, e], a, b)

    def x_copy(h, o):
        a, b = unslot(h)
        return copy(fs.at[o], fx.at[h - 5, o], xs.at[h - 5, o], xr.at[h - 5, o], -a, -b)

    barrier = pltpu.get_barrier_semaphore()

    def greet(n, a, b):
        pl.semaphore_signal(
            barrier,
            inc=1,
            device_id=(row_at + a, col_at + b),
            device_id_type=pl.DeviceIdType.MESH,
        )

    def shared(o):
        oa, ob = unslot(o)
        found = []
        for v in range(9):
            va, vb = unslot(v)
            if v != o and abs(va - oa) <= 1 and abs(vb - ob) <= 1:
                found.append((v, (va - oa + 1) * 3 + vb - ob + 1))
        return found

    loads = [
        pltpu.make_async_copy(source, target, arrive_sem.at[n])
        for n, (source, target) in enumerate(
            [
                (off_in, off_ref),
                (order_in, order_ref),
                (nug_in, nug_ref),
                (interp_in, interp_ref),
            ]
        )
    ]
    for load in loads:
        load.start()
    empty = jnp.zeros((128, 128), jnp.float32)
    f[...] = jnp.zeros(f.shape, jnp.float32)
    g[...] = jnp.zeros(g.shape, jnp.float32)
    fs[...] = jnp.zeros(fs.shape, jnp.float32)
    near[...] = jnp.zeros(near.shape, jnp.float32)
    for o in range(9):
        if o != 4:
            rx[o, 4] = empty
            for _, e in shared(o):
                rx[o, e] = empty
    for h in range(5, 9):
        fx[h - 5, 4] = empty
        for _, e in shared(h):
            fx[h - 5, e] = empty
    neighbours(greet)
    for load in loads:
        load.wait()
    line = lax.broadcasted_iota(jnp.int32, (16, 256), 0)
    plain = jnp.where(
        line == 0,
        off_ref[0:1] + row_at.astype(jnp.float32),
        jnp.where(
            line == 1,
            off_ref[1:2] + col_at.astype(jnp.float32),
            jnp.where(line == 2, nug_ref[...], 0.0),
        ),
    )
    pick = lax.broadcasted_iota(jnp.int32, (256, 256), 0) == order_ref[...]
    pick = jnp.where(pick, 1.0, 0.0).astype(jnp.bfloat16)
    high = plain.astype(jnp.bfloat16)
    middle, low = split(plain - high.astype(jnp.float32))
    placed = mm(high, pick) + mm(middle, pick) + mm(low, pick)
    level = lax.broadcasted_iota(jnp.int32, (8, 128), 0)
    own = jnp.zeros((8, 128), jnp.float32)
    for n in range(6):
        half = slice(128 * (n % 2), 128 * (n % 2) + 128)
        own = jnp.where(level == n, placed[n // 2 : n // 2 + 1, half], own)
    pack_ref[0:128] = interp_ref[...]
    pack_ref[128:136] = own
    tall = 1 + lax.min(row_at, 1) + lax.min(row_count - 1 - row_at, 1)
    wide = 1 + lax.min(col_at, 1) + lax.min(col_count - 1 - col_at, 1)
    pl.semaphore_wait(barrier, tall * wide - 1)
    neighbours(lambda n, a, b: place_copy(n, a, b).start())
    neighbours(lambda n, a, b: interp_copy(n, a, b).start())

    own_interp = split(pack_ref[0:128])
    my_colour = colour(0, 0)
    eye = lax.broadcasted_iota(jnp.int32, (128, 128), 0) == lax.broadcasted_iota(
        jnp.int32, (128, 128), 1
    )

    def start_block(source, here):
        where = source[128:136].T
        parts = []
        for s in range(2):
            line = []
            for t in range(2):
                gap_row = where[:, s : s + 1] - own[t : t + 1]
                gap_col = where[:, 2 + s : 3 + s] - own[2 + t : 3 + t]
                block = kappa(gap_row, gap_col)
                if here and s == t:
                    block = block + jnp.where(eye, own[4 + s : 5 + s], 0.0)
                line.append(block)
            parts.append(jnp.concatenate(line, axis=1))
        return parts

    def reduce_rows(upper, lower, source):
        return lower - mm(cat_left(source[0:128].T), cat_right(upper))

    ea[4] = reduce_rows(*start_block(pack_ref, True), pack_ref)
    mat[...] = ea[4, :, 128:] - dot3(split(ea[4, :, :128]), own_interp, NN)

    @pl.when(my_colour == 0)
    def _():
        tx[...] = factor128(mat[...])[1]
        neighbours(lambda n, a, b: k_copy(n, 4, a, b, True).start())

    neighbours(lambda n, a, b: place_copy(8 - n, -a, -b).wait_recv())
    for o in range(9):
        if o != 4:
            upper[o], ea[o] = start_block(near.at[o], False)
    neighbours(lambda n, a, b: interp_copy(8 - n, -a, -b).wait_recv())
    for o in range(9):
        if o != 4:
            value = reduce_rows(upper[o], ea[o], near.at[o])
            ea[o] = jnp.where(inside(*unslot(o)), value, 0.0)

    def stage(k):
        @pl.when((my_colour == k) & (k > 0))
        def _():
            tx[...] = factor128(mat[...])[1]
            neighbours(lambda n, a, b: k_copy(n, 4, a, b, True).start())

        def process(sources):
            for o in sources:
                oa, ob = unslot(o)
                if o != 4:
                    for v, e in shared(o):
                        va, vb = unslot(v)

                        @pl.when(inside(oa, ob) & inside(va, vb) & (colour(va, vb) < k))
                        def _():
                            k_copy(8 - o, e, -oa, -ob, False).wait_recv()

            for o in sources:
                total = ea[o]
                for v, e in shared(o):
                    value = g[e] if o == 4 else rx[o, e]
                    total = total - mm(cat_left(value), cat_right(f[v]))
                ea[o] = total
            for o in sources:
                oa, ob = unslot(o)
                if o != 4:

                    @pl.when(inside(oa, ob))
                    def _():
                        k_copy(8 - o, 4, -oa, -ob, False).wait_recv()

            for o in sources:
                factor = tx[...] if o == 4 else rx[o, 4]
                new = mm(cat_left(factor), cat_right(ea[o]))
                f[o] = new
                fs[o] = new[:, :128]
            if sources != [4]:

                @pl.when(my_colour > k)
                def _():
                    total = mat[...]
                    right = cat_right(pack_ref[0:128])
                    for o in sources:
                        new = f[o, :, 128:] - mm(cat_left(f[o, :, :128]), right)
                        flip = new.T
                        g[o] = flip
                        total = total - mm(cat_left(flip), cat_right(new))
                    mat[...] = total
                    for o in sources:
                        oa, ob = unslot(o)
                        for n in range(9):
                            a, b = unslot(n)
                            if n != 4 and abs(oa - a) <= 1 and abs(ob - b) <= 1:

                                @pl.when(inside(a, b) & inside(oa, ob))
                                def _():
                                    k_copy(n, o, a, b, False).start()

            for o in sources:
                oa, ob = unslot(o)
                for h in range(5, 9):
                    ha, hb = unslot(h)
                    if abs(oa + ha) <= 1 and abs(ob + hb) <= 1:

                        @pl.when(inside(-ha, -hb) & inside(oa, ob))
                        def _():
                            x_copy(h, o).start()

        for tall_odd in range(2):
            for wide_odd in range(2):
                sources = [
                    (a + 1) * 3 + b + 1
                    for a in ((-1, 1) if tall_odd else (0,))
                    for b in ((-1, 1) if wide_odd else (0,))
                ]

                @pl.when(((row_at + k // 2) % 2 == tall_odd) & ((col_at + k) % 2 == wide_odd))
                def _():
                    process(sources)

    loop(stage, 0, 4)

    for h in range(5, 9):
        ha, hb = unslot(h)
        for v in range(9):
            va, vb = unslot(v)
            if abs(va - ha) <= 1 and abs(vb - hb) <= 1:

                @pl.when(inside(ha, hb) & inside(va, vb))
                def _():
                    x_copy(h, (va - ha + 1) * 3 + vb - hb + 1).wait_recv()

    flips = [cat_left(fs[v].T) for v in range(9)]
    total = jnp.where(eye, own[4:5], 0.0)
    for v in range(9):
        total = total - mm(flips[v], cat_right(fs[v]))
    dd[0] = total
    for h in range(5, 9):
        ha, hb = unslot(h)
        total = empty
        for v in range(9):
            va, vb = unslot(v)
            if abs(va - ha) <= 1 and abs(vb - hb) <= 1:
                e = (va - ha + 1) * 3 + vb - hb + 1
                total = total - mm(flips[v], cat_right(fx[h - 5, e]))
        dd[h - 4] = total
        dd[h] = total.T

    lane = lax.broadcasted_iota(jnp.int32, (8, 128), 1)

    def gather(items):
        value = jnp.zeros((8, 128), jnp.float32)
        for source, start, place, size in items:
            moved = pltpu.roll(source, (place - start) % 128, 1)
            value = jnp.where((lane >= place) & (lane < place + size), moved, value)
        return value

    heads = [dd[n, 0:8] for n in range(9)]
    corner = [(heads[n], 0, 8 + 8 * n, 8) for n in range(9)]
    wide_rows = [
        gather([(heads[n], 16 * r, 16 + 16 * n, 16) for n in range(7)]) for r in range(8)
    ]
    more_rows = [
        gather(
            [(heads[7 + n], 16 * r, 16 * n, 16) for n in range(2)]
            + [(own, 16 * r, 32, 16), (own, 0, 56, 8)]
        )
        for r in range(8)
    ]
    corner = gather(corner)
    for c in range(16):
        rows = slice(8 * c, 8 * c + 8)
        group = [dd[n, rows] for n in range(9)]
        turn = group[1:]
        for bit in range(3):
            step = 1 << bit
            upper = ((lane // 16) // step) % 2 == 1
            for n in range(8):
                if n & step:
                    continue
                low, high = turn[n], turn[n + step]
                turn[n] = jnp.where(upper, pltpu.roll(high, 16 * step, 1), low)
                turn[n + step] = jnp.where(upper, high, pltpu.roll(low, 128 - 16 * step, 1))
        side = gather([(own, 8 * c, 48, 8)] + [(group[n], 0, 64 + 8 * n, 8) for n in range(8)])
        tail = jnp.where(lane < 8, group[8], corner)
        for r in range(8):
            dest = 16 * r + c
            out_ref[dest, 0] = turn[r]
            first = group[0] if r == 0 else pltpu.roll(group[0], 128 - 16 * r, 1)
            out_ref[dest, 1] = jnp.where(lane < 16, first, wide_rows[r])
            out_ref[dest, 2] = jnp.where((lane < 48) | ((lane >= 56) & (lane < 64)), more_rows[r], side)
            out_ref[dest, 3] = tail

    def finish(n, a, b):
        place_copy(n, a, b).wait_send()
        interp_copy(n, a, b).wait_send()

        def each(e):
            ea_, eb_ = unslot(e)
            is_sent = (e == 4) | (inside(ea_, eb_) & (colour(ea_, eb_) < my_colour))

            @pl.when(is_sent & near_pair(ea_ - a, eb_ - b))
            def _():
                k_copy(n, e, a, b, False).wait_send()

        loop(each)

    neighbours(finish)

    def finish_x(h):
        ha, hb = unslot(h)

        def each(o):
            oa, ob = unslot(o)

            @pl.when(inside(-ha, -hb) & inside(oa, ob) & near_pair(oa + ha, ob + hb))
            def _():
                x_copy(h, o).wait_send()

        loop(each)

    loop(finish_x, 5, 9)


def box_phase(off, order, nug, interp):
    block = (128, 128)
    return pl.pallas_call(
        box_kernel,
        out_shape=jax.ShapeDtypeStruct((128, 4, 8, 128), jnp.float32),
        in_specs=[pl.BlockSpec(memory_space=pltpu.HBM)] * 4,
        out_specs=pl.BlockSpec(memory_space=pltpu.VMEM),
        scratch_shapes=[
            pltpu.VMEM((2, 256), jnp.float32),
            pltpu.VMEM((1, 256), jnp.int32),
            pltpu.VMEM((1, 256), jnp.float32),
            pltpu.VMEM(block, jnp.float32),
            pltpu.SemaphoreType.DMA((4,)),
            pltpu.VMEM((136, 128), jnp.float32),
            pltpu.VMEM((9, 128, 256), jnp.float32),
            pltpu.VMEM((9, 136, 128), jnp.float32),
            pltpu.VMEM((9, 128, 256), jnp.float32),
            pltpu.VMEM((9, 128, 256), jnp.float32),
            pltpu.VMEM((9,) + block, jnp.float32),
            pltpu.VMEM((9,) + block, jnp.float32),
            pltpu.VMEM(block, jnp.float32),
            pltpu.VMEM((128, 256), jnp.float32),
            pltpu.VMEM(block, jnp.float32),
            pltpu.VMEM((9, 9) + block, jnp.float32),
            pltpu.VMEM((4, 9) + block, jnp.float32),
            pltpu.VMEM((9,) + block, jnp.float32),
            pltpu.SemaphoreType.DMA((2, 9)),
            pltpu.SemaphoreType.DMA((2, 9)),
            pltpu.SemaphoreType.DMA((9, 9)),
            pltpu.SemaphoreType.DMA((9, 9)),
            pltpu.SemaphoreType.DMA((4, 9)),
            pltpu.SemaphoreType.DMA((4, 9)),
        ],
        compiler_params=pltpu.CompilerParams(
            collective_id=0, has_side_effects=True, vmem_limit_bytes=67043328
        ),
    )(off, order, nug, interp)


def cat_right(x):
    hi, lo = split(x)
    return jnp.concatenate([hi, hi, lo], axis=0)


def cat_left(x):
    hi, lo = split(x)
    return jnp.concatenate([hi, lo, hi], axis=1)


def mm(a, b):
    return lax.dot_general(a, b, (NN, ((), ())), preferred_element_type=jnp.float32)


OFFSETS = [0, 1, 15, 16, 17, -1, -15, -16, -17]


def apart():
    return lax.broadcasted_iota(jnp.int32, (128, 128), 0) - lax.broadcasted_iota(
        jnp.int32, (128, 128), 1
    )


def root_block(row_x, row_y, col_x, col_y, lines):
    gap_x = row_x - col_x
    gap_y = row_y - col_y
    value = kappa(gap_x, gap_y)
    gap = apart()
    extra = jnp.zeros((128, 128), jnp.float32)
    for n in range(9):
        extra = jnp.where(gap == OFFSETS[n], lines[n], extra)
    return value + extra


def shifted_line(line, n):
    return pltpu.roll(line, -OFFSETS[n] % 128, 1) if n > 4 else line


def tail_kernel(
    at_ref,
    turned,
    out_ref,
    lead_ref,
    rows_ref,
    work,
    diag,
    wcur,
    left,
    right,
    wt,
    z_hi,
    z_lo,
    x_hi,
    x_lo,
    base,
    tab,
    table,
    sems,
):
    count = SB // 128
    width = 2 * SB
    chunk = 256
    row = lax.broadcasted_iota(jnp.int32, (128, SB), 0)
    col = lax.broadcasted_iota(jnp.int32, (128, SB), 1)

    def rows_of(i):
        return pl.ds(pl.multiple_of(i * 128, 128), 128)

    for l in range(8):
        for n in range(9):
            place = 64 + 8 * n
            line = turned[16 + l, place : place + 8] if n < 8 else turned[24 + l, 0:8]
            tab[0, l, n] = shifted_line(line, n)
            tab[1, l, n] = shifted_line(turned[24 + l, 8 + 8 * n : 16 + 8 * n], n)
            place = 16 * (n - 1)
            line = turned[l, place : place + 16] if n else turned[8 + l, 0:16]
            table[0, l, n] = shifted_line(line, n)
            place = 16 * n + 16
            if n < 7:
                line = turned[8 + l, place : place + 16]
            else:
                line = turned[16 + l, place - 128 : place - 112]
            table[1, l, n] = shifted_line(line, n)

    def piece(values, wide, which, k, l, token=0.0):
        place = 48 + 8 * which + l
        return root_block(
            wide[k, 0],
            wide[k, 1],
            turned[16, place : place + 1] + token,
            turned[18, place : place + 1],
            [values[which, l, n, pl.ds(k, 1)] for n in range(9)],
        )

    xs = turned[16, 32:64].T
    ys = turned[18, 32:64].T
    for k in range(16):
        rows_ref[k, 0] = jnp.broadcast_to(xs[:, k : k + 1], (128, 128))
        rows_ref[k, 1] = jnp.broadcast_to(ys[:, k : k + 1], (128, 128))
    for k in range(8):
        lead_ref[k, 0] = jnp.broadcast_to(xs[:, 24 + k : 25 + k], (128, 128))
        lead_ref[k, 1] = jnp.broadcast_to(ys[:, 24 + k : 25 + k], (128, 128))

    def assemble(k, _):
        for l in range(8):
            work[rows_of(k), SB + 128 * l : SB + 128 * l + 128] = piece(tab, lead_ref, 0, k, l)

            @pl.when(k <= l)
            def _():
                work[rows_of(k), 128 * l : 128 * l + 128] = piece(tab, lead_ref, 1, k, l)

            @pl.when(k > l)
            def _():
                work[rows_of(k), 128 * l : 128 * l + 128] = jnp.zeros((128, 128), jnp.float32)

        return 0

    lax.fori_loop(0, count, assemble, 0)
    work[SB:] = jnp.zeros((128, width + 128), jnp.float32)
    eye = jnp.where(apart() == 0, 1.0, 0.0)
    diag[...] = work[:128, :128]
    wcur[...] = jnp.zeros((128, 384), jnp.bfloat16)

    def build(k, l, token):
        cols = slice(128 * l, 128 * l + 128)
        hi, lo = split(piece(table, rows_ref, 1, k, l, token))
        x_hi[rows_of(k), cols] = hi
        x_lo[rows_of(k), cols] = lo
        base[rows_of(k), cols] = piece(table, rows_ref, 0, k, l, token)

    def scale(p):
        here = rows_of(p)
        spot = rows_of(jnp.where(p == count, 2 * count, p))
        work[:SB, spot] = jnp.zeros((SB, 128), jnp.float32)
        work[here, spot] = eye
        for c in range(width // chunk):
            cols = slice(c * chunk, c * chunk + chunk)
            new = mm(wcur[...], cat_right(work[here, cols]))
            work[here, cols] = new
            right[:, cols] = cat_right(new)
            for j in range(chunk // 128):
                n = c * (chunk // 128) + j
                if n < count:
                    flip = new[:, 128 * j : 128 * j + 128].T
                    there = slice(128 * n, 128 * n + 128)
                    left[there] = cat_left(jnp.where(p < n, flip, 0.0))
                    hi, lo = split(jnp.where(p < n, 0.0, flip))
                    wt[0, there, here] = hi
                    wt[1, there, here] = lo
            if c * chunk >= SB:
                hi, lo = split(new)
                z_hi[here, c * chunk - SB : c * chunk - SB + chunk] = hi
                z_lo[here, c * chunk - SB : c * chunk - SB + chunk] = lo

    def step(i, _):
        p = jnp.where(i == 0, count, i - 1)
        scale(p)
        for c in range(width // chunk):
            cols = slice(c * chunk, c * chunk + chunk)
            work[:SB, cols] -= mm(left[...], right[:, cols])
        w = factor128(diag[...], lambda p, t: build(2 * i + p // 8, p % 8, t))[1]
        wcur[...] = cat_left(w)
        here, after = rows_of(i), rows_of(i + 1)
        u = mm(wcur[...], cat_right(work[here, after]))
        diag[...] = work[after, after] - mm(cat_left(u.T), cat_right(u))
        return 0

    lax.fori_loop(0, count, step, 0)
    scale(count - 1)

    @pl.when(at_ref[1] == 0)
    def _():
        for i in range(count):
            here = slice(128 * i, 128 * i + 128)
            z_hi[here] = jnp.where(col == row + 128 * i, -1.0, 0.0).astype(jnp.bfloat16)
            z_lo[here] = jnp.zeros((128, SB), jnp.bfloat16)

    for c in range(SB // chunk):
        cols = slice(c * chunk, c * chunk + chunk)
        y_hi, y_lo = z_hi[:SB, cols], z_lo[:SB, cols]
        for m in range(4):
            some = slice(m * 256, m * 256 + 256)
            deep = slice(m * 256, SB)
            w_hi, w_lo = wt[0, some, deep], wt[1, some, deep]
            work[some, cols] = (
                mm(w_hi, y_lo[m * 256 :]) + mm(w_lo, y_hi[m * 256 :]) + mm(w_hi, y_hi[m * 256 :])
            )
        for m in range(4):
            some = slice(m * 256, m * 256 + 256)
            hi, lo = split(work[some, cols])
            z_hi[some, cols] = hi
            z_lo[some, cols] = lo

    tall = 512

    def product(r, _):
        here = pl.ds(pl.multiple_of(r * tall, tall), tall)
        for c in range(SB // chunk):
            cols = slice(c * chunk, c * chunk + chunk)
            part = (
                mm(x_hi[here], z_lo[:SB, cols])
                + mm(x_lo[here], z_hi[:SB, cols])
                + mm(x_hi[here], z_hi[:SB, cols])
            )
            value = jnp.where(at_ref[1] == 0, 0.0, base[here, cols]) - part
            down = (at_ref[0] * 4 + r) * tall + lax.broadcasted_iota(jnp.int32, value.shape, 0)
            over = at_ref[1] * SB + c * chunk + lax.broadcasted_iota(jnp.int32, value.shape, 1)
            base[here, cols] = jnp.where((down < SB) & (over > down), 0.0, value)
        pltpu.make_async_copy(base.at[here], out_ref.at[here], sems.at[r]).start()
        return 0

    lax.fori_loop(0, 4, product, 0)
    for r in range(4):
        here = slice(r * tall, r * tall + tall)
        pltpu.make_async_copy(base.at[here], out_ref.at[here], sems.at[r]).wait()


def tail_solve(at, turned):
    vmem = pl.BlockSpec(memory_space=pltpu.VMEM)
    return pl.pallas_call(
        tail_kernel,
        out_shape=jax.ShapeDtypeStruct((2048, SB), jnp.float32),
        in_specs=[pl.BlockSpec(memory_space=pltpu.SMEM), vmem],
        out_specs=pl.BlockSpec(memory_space=pl.ANY),
        scratch_shapes=[
            pltpu.VMEM((8, 2, 128, 128), jnp.float32),
            pltpu.VMEM((16, 2, 128, 128), jnp.float32),
            pltpu.VMEM((SB + 128, 2 * SB + 128), jnp.float32),
            pltpu.VMEM((128, 128), jnp.float32),
            pltpu.VMEM((128, 384), jnp.bfloat16),
            pltpu.VMEM((SB, 384), jnp.bfloat16),
            pltpu.VMEM((384, 2 * SB), jnp.bfloat16),
            pltpu.VMEM((2, SB, SB + 128), jnp.bfloat16),
            pltpu.VMEM((SB + 128, SB), jnp.bfloat16),
            pltpu.VMEM((SB + 128, SB), jnp.bfloat16),
            pltpu.VMEM((2048, SB), jnp.bfloat16),
            pltpu.VMEM((2048, SB), jnp.bfloat16),
            pltpu.VMEM((2048, SB), jnp.float32),
            pltpu.VMEM((2, 8, 9, 8, 128), jnp.float32),
            pltpu.VMEM((2, 8, 9, 16, 128), jnp.float32),
            pltpu.SemaphoreType.DMA((4,)),
        ],
        compiler_params=pltpu.CompilerParams(vmem_limit_bytes=60 * 2**20),
    )(at, turned)


def root_phase(outgoing, row_at, col_at):
    arrived = lax.all_to_all(
        outgoing.reshape(128, 32, 128), ("row", "col"), split_axis=0, concat_axis=0, tiled=True
    )
    turned = jnp.transpose(arrived, (1, 2, 0))

    return tail_solve(jnp.stack([row_at, col_at]), turned)


def on_device(offsets, point_order, nugget, interp):
    outgoing = box_phase(offsets[0, 0], point_order[0], nugget[0], interp[0, 0])
    return root_phase(outgoing, lax.axis_index("row"), lax.axis_index("col"))


def solution(mesh):
    in_specs = (
        P("row", "col", None, None),
        P("row", "col", None),
        P("row", "col", None),
        P("row", "col", None, None),
    )
    out_specs = P("row", "col")
    return jax.shard_map(
        on_device, mesh=mesh, in_specs=in_specs, out_specs=out_specs, check_vma=False
    )
```
